128 devices in a mesh: wa: 16 (over x, z), ha: 8 (over y, core).
Axes of the slice: x: 4, y: 4, z: 4, core: 2. Of those that a mesh axis runs over, the one named last changes fastest.
Arguments:
- tokens: bfloat16 [512, 16384], P('ha', 'wa'), may hold values from -100 to 100, as said below
- norm_gain: float32 [16384], P('wa'), may hold values from 0.5 to 1.5
- gate_weight: bfloat16 [16384, 26624], P('wa', 'ha'), may hold values from -0.046875 to 0.046875
- up_weight: bfloat16 [16384, 26624], P('wa', 'ha'), may hold values from -0.046875 to 0.046875
- down_weight: bfloat16 [26624, 16384], P('ha', 'wa'), may hold values from -0.0390625 to 0.0390625
Outputs:
- mixed: bfloat16 [512, 16384], P('ha', 'wa')
The draws below stay inside these ranges and needn't reach their ends.
Inputs may be any that keep to these rules, and one draw needn't show every extreme that they name: `tokens`: real-valued activations.
All inputs are finite; a program needn't handle non-finite values.
Results may differ from the reference program's by a relative error of at most 0.0064.
Values may be sent and summed in bfloat16 or wider, within the bound.
A program may use at most 128 MiB of HBM per device.

```python
import math
import jax
import jax.numpy as jnp
from jax import lax

D = 16384
FFW = 26624
TOKENS = 512


def draw_tokens(key, part):
    key_base, key_rows, key_columns = jax.random.split(key, 3)
    position = jnp.arange(D, dtype=jnp.float32)[None, :] / D
    row_scale = jnp.exp(jax.random.uniform(key_rows, (TOKENS, 1), jnp.float32, 0.0, math.log(10.0)))
    column_factor = jnp.exp(jax.random.uniform(key_columns, (1, D), jnp.float32, -0.6, 0.6))
    base = jnp.clip(jax.random.normal(key_base, (TOKENS, D), jnp.float32), -4.5, 4.5)
    rising = jnp.exp(position * math.log(3.0))
    return (0.3 * base * row_scale * column_factor * rising).astype(jnp.bfloat16)


def block_scale(rng, shape, cuts, low, largest):
    loudness, own = 1.0, jax.random.fold_in(rng, 6)
    for dim, shards_of in cuts:
        steps = jnp.exp(jax.random.uniform(jax.random.fold_in(own, dim), (shards_of,), jnp.float32, low / len(cuts), largest / len(cuts)))
        loudness = loudness * jnp.repeat(steps, shape[dim] // shards_of).reshape([-1 if axis == dim else 1 for axis in range(len(shape))])
    return loudness


def gaussian(rng, shape, scale, most, shards=(), kind=jnp.bfloat16):
    entries = jax.random.normal(rng, shape, jnp.float32) * scale
    if len(shards) > 0:
        entries = block_scale(rng, shape, shards, -0.22, 0.18) * entries
    return jnp.clip(entries, min=-most, max=most).astype(kind)


def setup_inputs(seed: int = 0) -> dict:
    key_list = jax.random.split(jax.random.key(seed), 6)
    return {
        "tokens": draw_tokens(jax.random.fold_in(key_list[5], 71), 0),
        "norm_gain": jnp.clip(1.0 + 0.1 * jax.random.normal(key_list[1], (D,), jnp.float32), 0.5, 1.5),
        "gate_weight": gaussian(key_list[2], (D, FFW), D ** -0.5, 0.046875, ((0, 16), (1, 8))),
        "up_weight": gaussian(key_list[3], (D, FFW), D ** -0.5, 0.046875, ((0, 16), (1, 8))),
        "down_weight": gaussian(key_list[4], (FFW, D), FFW ** -0.5, 0.0390625, ((0, 8), (1, 16))),
    }


def reference(tokens, norm_gain, gate_weight, up_weight, down_weight):
    values = tokens.astype(jnp.float32)
    squares = lax.optimization_barrier(jnp.mean(values * values, axis=1, keepdims=True))
    normed = (values * lax.rsqrt(squares + 1e-05) * norm_gain[None, :]).astype(jnp.bfloat16)
    gate = jnp.dot(normed, gate_weight, preferred_element_type=jnp.float32)
    up = jnp.dot(normed, up_weight, preferred_element_type=jnp.float32)
    hidden = (jax.nn.silu(gate) * up).astype(jnp.bfloat16)
    return jnp.dot(hidden, down_weight, preferred_element_type=jnp.float32).astype(jnp.bfloat16)
```

```python
import jax
import jax.numpy as jnp
from jax import lax
from jax.sharding import PartitionSpec as P


def activate(summed, hidden_width, model_width):
    gate = summed[:, :hidden_width]
    up = summed[:, hidden_width:2 * hidden_width]
    squares = summed[:, 2 * hidden_width:2 * hidden_width + 1]
    scale = lax.rsqrt(squares / model_width + 1e-05)
    return (jax.nn.silu(gate * scale) * (up * scale)).astype(jnp.bfloat16)


def body(tokens, norm_gain, gate_weight, up_weight, down_weight):
    gathered = lax.all_gather(tokens, "ha", axis=0, tiled=True)
    own_values = gathered.astype(jnp.float32)
    model_width = own_values.shape[1] * lax.axis_size("wa")
    squares = jnp.sum(own_values * own_values, axis=1, keepdims=True)
    scaled = (own_values * norm_gain[None, :]).astype(jnp.bfloat16)
    hidden_width = gate_weight.shape[1]
    gate_part = jnp.dot(scaled, gate_weight, preferred_element_type=jnp.float32)
    up_part = jnp.dot(scaled, up_weight, preferred_element_type=jnp.float32)
    square_block = jnp.broadcast_to(squares, (squares.shape[0], 128))
    summed = lax.psum_scatter(
        jnp.concatenate([gate_part, up_part, square_block], axis=1), "wa", scatter_dimension=0, tiled=True
    )
    hidden = activate(summed, hidden_width, model_width)
    partial_out = jnp.dot(
        lax.all_gather(hidden, "wa", axis=0, tiled=True),
        down_weight,
        preferred_element_type=jnp.float32,
    )
    mixed_out = lax.psum_scatter(partial_out, "ha", scatter_dimension=0, tiled=True)
    return mixed_out.astype(jnp.bfloat16)


def solution(mesh):
    placed = (P("ha", "wa"), P("wa"), P("wa", "ha"), P("wa", "ha"), P("ha", "wa"))
    return jax.shard_map(body, mesh=mesh, in_specs=placed, out_specs=P("ha", "wa"), check_vma=False)
```

```python
import functools

import jax
import jax.numpy as jnp
from jax import lax
from jax.experimental import pallas as pl
from jax.experimental.pallas import tpu as pltpu
from jax.sharding import PartitionSpec as P

MESH = pl.DeviceIdType.MESH


def _greet(axis, n, me):
    barrier = pltpu.get_barrier_semaphore()
    for k in range(1, n):
        pl.semaphore_signal(barrier, inc=1, device_id={axis: lax.rem(me + k, n)}, device_id_type=MESH)
    pl.semaphore_wait(barrier, n - 1)


def _exchange_kernel(mode, axis, n, rows, x_ref, out_ref, slots, send_sem, recv_sem):
    me = lax.axis_index(axis)
    _greet(axis, n, me)
    copies = []
    for k in range(1, n):
        peer = lax.rem(me + k, n)
        if mode == "gather":
            source = x_ref
        elif mode == "scatter":
            source = x_ref.at[pl.ds(pl.multiple_of(peer * rows, rows), rows)]
        else:
            source = x_ref
        copy = pltpu.make_async_remote_copy(
            src_ref=source,
            dst_ref=slots.at[k],
            send_sem=send_sem.at[k],
            recv_sem=recv_sem.at[k],
            device_id={axis: peer},
            device_id_type=MESH,
        )
        copy.start()
        copies.append(copy)
    if mode == "gather":
        out_ref[pl.ds(pl.multiple_of(me * rows, rows), rows), :] = x_ref[...]
        for k, copy in enumerate(copies, 1):
            copy.wait()
            sender = lax.rem(me + n - k, n)
            out_ref[pl.ds(pl.multiple_of(sender * rows, rows), rows), :] = slots[k]
    elif mode == "scatter":
        total = x_ref[pl.ds(pl.multiple_of(me * rows, rows), rows), :].astype(jnp.float32)
        for k, copy in enumerate(copies, 1):
            copy.wait()
            total = total + slots[k].astype(jnp.float32)
        out_ref[...] = total
    else:
        for copy in copies:
            copy.wait()
        slots[0] = x_ref[...]
        total = jnp.zeros(out_ref.shape, jnp.float32)
        for sender in range(n):
            total = total + slots[lax.rem(me + n - sender, n)].astype(jnp.float32)
        out_ref[...] = total


def exchange(x, mode, axis, n, collective_id):
    if mode == "gather":
        rows = x.shape[0]
        out_shape = jax.ShapeDtypeStruct((n * rows, x.shape[1]), x.dtype)
    elif mode == "scatter":
        rows = x.shape[0] // n
        out_shape = jax.ShapeDtypeStruct((rows, x.shape[1]), jnp.float32)
    else:
        rows = x.shape[0]
        out_shape = jax.ShapeDtypeStruct(x.shape, jnp.float32)
    return pl.pallas_call(
        functools.partial(_exchange_kernel, mode, axis, n, rows),
        out_shape=out_shape,
        in_specs=[pl.BlockSpec(memory_space=pltpu.VMEM)],
        out_specs=pl.BlockSpec(memory_space=pltpu.VMEM),
        scratch_shapes=[
            pltpu.VMEM((n, rows, x.shape[1]), x.dtype),
            pltpu.SemaphoreType.DMA((n,)),
            pltpu.SemaphoreType.DMA((n,)),
        ],
        compiler_params=pltpu.CompilerParams(collective_id=collective_id, has_side_effects=True),
    )(x)


def body(tokens, norm_gain, gate_weight, up_weight, down_weight):
    n_wa = lax.axis_size("wa")
    n_ha = lax.axis_size("ha")
    own_values = tokens.astype(jnp.float32)
    model_width = own_values.shape[1] * n_wa
    own_rows = own_values.shape[0]
    partial_squares = jnp.sum(own_values * own_values, axis=1)
    packed = jnp.pad(partial_squares.reshape(8, own_rows // 8), ((0, 0), (0, 128 - own_rows // 8)))
    squares = exchange(packed, "sum", "wa", n_wa, 0)[:, : own_rows // 8].reshape(own_rows, 1)
    mean_square = squares / model_width
    normed = (own_values * lax.rsqrt(mean_square + 1e-05) * norm_gain[None, :]).astype(jnp.bfloat16)
    gathered = exchange(normed, "gather", "ha", n_ha, 1)
    hidden_width = gate_weight.shape[1]
    gate_part = jnp.dot(gathered, gate_weight, preferred_element_type=jnp.float32)
    up_part = jnp.dot(gathered, up_weight, preferred_element_type=jnp.float32)
    both = jnp.concatenate([gate_part, up_part], axis=1).astype(jnp.bfloat16)
    summed = exchange(both, "scatter", "wa", n_wa, 2)
    gate = summed[:, :hidden_width]
    up = summed[:, hidden_width:]
    hidden = (jax.nn.silu(gate) * up).astype(jnp.bfloat16)
    all_hidden = exchange(hidden, "gather", "wa", n_wa, 3)
    partial_out = jnp.dot(all_hidden, down_weight, preferred_element_type=jnp.float32)
    mixed_out = exchange(partial_out, "scatter", "ha", n_ha, 4)
    return mixed_out.astype(jnp.bfloat16)


def solution(mesh):
    placed = (P("ha", "wa"), P("wa"), P("wa", "ha"), P("wa", "ha"), P("ha", "wa"))
    return jax.shard_map(body, mesh=mesh, in_specs=placed, out_specs=P("ha", "wa"), check_vma=False)
```

```python
import functools

import jax
import jax.numpy as jnp
from jax import lax
from jax.experimental import pallas as pl
from jax.experimental.pallas import tpu as pltpu
from jax.sharding import PartitionSpec as P

MESH = pl.DeviceIdType.MESH


def _greet(axis, n, me):
    barrier = pltpu.get_barrier_semaphore()
    for k in range(1, n):
        pl.semaphore_signal(barrier, inc=1, device_id={axis: lax.rem(me + k, n)}, device_id_type=MESH)
    pl.semaphore_wait(barrier, n - 1)


def _exchange_kernel(mode, axis, n, rows, x_ref, out_ref, slots, send_sem, recv_sem):
    me = lax.axis_index(axis)
    _greet(axis, n, me)
    copies = []
    for k in range(1, n):
        peer = lax.rem(me + k, n)
        if mode == "gather":
            source = x_ref
        elif mode == "scatter":
            source = x_ref.at[pl.ds(pl.multiple_of(peer * rows, rows), rows)]
        else:
            source = x_ref
        copy = pltpu.make_async_remote_copy(
            src_ref=source,
            dst_ref=slots.at[k],
            send_sem=send_sem.at[k],
            recv_sem=recv_sem.at[k],
            device_id={axis: peer},
            device_id_type=MESH,
        )
        copy.start()
        copies.append(copy)
    if mode == "gather":
        out_ref[pl.ds(pl.multiple_of(me * rows, rows), rows), :] = x_ref[...]
        for k, copy in enumerate(copies, 1):
            copy.wait()
            sender = lax.rem(me + n - k, n)
            out_ref[pl.ds(pl.multiple_of(sender * rows, rows), rows), :] = slots[k]
    elif mode == "scatter":
        total = x_ref[pl.ds(pl.multiple_of(me * rows, rows), rows), :].astype(jnp.float32)
        for k, copy in enumerate(copies, 1):
            copy.wait()
            total = total + slots[k].astype(jnp.float32)
        out_ref[...] = total
    else:
        for copy in copies:
            copy.wait()
        slots[0] = x_ref[...]
        total = jnp.zeros(out_ref.shape, jnp.float32)
        for sender in range(n):
            total = total + slots[lax.rem(me + n - sender, n)].astype(jnp.float32)
        out_ref[...] = total


def exchange(x, mode, axis, n, collective_id):
    if mode == "gather":
        rows = x.shape[0]
        out_shape = jax.ShapeDtypeStruct((n * rows, x.shape[1]), x.dtype)
    elif mode == "scatter":
        rows = x.shape[0] // n
        out_shape = jax.ShapeDtypeStruct((rows, x.shape[1]), jnp.float32)
    else:
        rows = x.shape[0]
        out_shape = jax.ShapeDtypeStruct(x.shape, jnp.float32)
    return pl.pallas_call(
        functools.partial(_exchange_kernel, mode, axis, n, rows),
        out_shape=out_shape,
        in_specs=[pl.BlockSpec(memory_space=pltpu.VMEM)],
        out_specs=pl.BlockSpec(memory_space=pltpu.VMEM),
        scratch_shapes=[
            pltpu.VMEM((n, rows, x.shape[1]), x.dtype),
            pltpu.SemaphoreType.DMA((n,)),
            pltpu.SemaphoreType.DMA((n,)),
        ],
        compiler_params=pltpu.CompilerParams(collective_id=collective_id, has_side_effects=True),
    )(x)


def body(tokens, norm_gain, gate_weight, up_weight, down_weight):
    n_wa = lax.axis_size("wa")
    n_ha = lax.axis_size("ha")
    own_values = tokens.astype(jnp.float32)
    model_width = own_values.shape[1] * n_wa
    own_rows = own_values.shape[0]
    partial_squares = jnp.sum(own_values * own_values, axis=1)
    packed = jnp.pad(partial_squares.reshape(8, own_rows // 8), ((0, 0), (0, 128 - own_rows // 8)))
    squares = exchange(packed, "sum", "wa", n_wa, 0)[:, : own_rows // 8].reshape(own_rows, 1)
    mean_square = squares / model_width
    normed = (own_values * lax.rsqrt(mean_square + 1e-05) * norm_gain[None, :]).astype(jnp.bfloat16)
    gathered = exchange(normed, "gather", "ha", n_ha, 1)
    hidden_width = gate_weight.shape[1]
    gate_part = jnp.dot(gathered, gate_weight, preferred_element_type=jnp.float32)
    up_part = jnp.dot(gathered, up_weight, preferred_element_type=jnp.float32)
    summed = lax.psum_scatter(
        jnp.concatenate([gate_part, up_part], axis=1), "wa", scatter_dimension=0, tiled=True
    )
    gate = summed[:, :hidden_width]
    up = summed[:, hidden_width:]
    hidden = (jax.nn.silu(gate) * up).astype(jnp.bfloat16)
    all_hidden = lax.all_gather(hidden, "wa", axis=0, tiled=True)
    partial_out = jnp.dot(all_hidden, down_weight, preferred_element_type=jnp.float32)
    mixed_out = exchange(partial_out.astype(jnp.bfloat16), "scatter", "ha", n_ha, 4)
    return mixed_out.astype(jnp.bfloat16)


def solution(mesh):
    placed = (P("ha", "wa"), P("wa"), P("wa", "ha"), P("wa", "ha"), P("ha", "wa"))
    return jax.shard_map(body, mesh=mesh, in_specs=placed, out_specs=P("ha", "wa"), check_vma=False)
```

```python
import functools

import jax
import jax.numpy as jnp
from jax import lax
from jax.experimental import pallas as pl
from jax.experimental.pallas import tpu as pltpu
from jax.sharding import PartitionSpec as P

MESH = pl.DeviceIdType.MESH


def _greet(axis, n, me):
    barrier = pltpu.get_barrier_semaphore()
    for k in range(1, n):
        pl.semaphore_signal(barrier, inc=1, device_id={axis: lax.rem(me + k, n)}, device_id_type=MESH)
    pl.semaphore_wait(barrier, n - 1)


def _exchange_kernel(mode, axis, n, rows, x_ref, out_ref, slots, send_sem, recv_sem):
    me = lax.axis_index(axis)
    _greet(axis, n, me)
    copies = []
    for k in range(1, n):
        peer = lax.rem(me + k, n)
        if mode == "gather":
            source = x_ref
        elif mode == "scatter":
            source = x_ref.at[pl.ds(pl.multiple_of(peer * rows, rows), rows)]
        else:
            source = x_ref
        copy = pltpu.make_async_remote_copy(
            src_ref=source,
            dst_ref=slots.at[k],
            send_sem=send_sem.at[k],
            recv_sem=recv_sem.at[k],
            device_id={axis: peer},
            device_id_type=MESH,
        )
        copy.start()
        copies.append(copy)
    if mode == "gather":
        out_ref[pl.ds(pl.multiple_of(me * rows, rows), rows), :] = x_ref[...]
        for k, copy in enumerate(copies, 1):
            copy.wait()
            sender = lax.rem(me + n - k, n)
            out_ref[pl.ds(pl.multiple_of(sender * rows, rows), rows), :] = slots[k]
    elif mode == "scatter":
        total = x_ref[pl.ds(pl.multiple_of(me * rows, rows), rows), :].astype(jnp.float32)
        for k, copy in enumerate(copies, 1):
            copy.wait()
            total = total + slots[k].astype(jnp.float32)
        out_ref[...] = total
    else:
        for copy in copies:
            copy.wait()
        slots[0] = x_ref[...]
        total = jnp.zeros(out_ref.shape, jnp.float32)
        for sender in range(n):
            total = total + slots[lax.rem(me + n - sender, n)].astype(jnp.float32)
        out_ref[...] = total


def exchange(x, mode, axis, n, collective_id):
    if n == 1:
        return x.astype(jnp.float32) if mode != "gather" else x
    if mode == "gather":
        rows = x.shape[0]
        out_shape = jax.ShapeDtypeStruct((n * rows, x.shape[1]), x.dtype)
    elif mode == "scatter":
        rows = x.shape[0] // n
        out_shape = jax.ShapeDtypeStruct((rows, x.shape[1]), jnp.float32)
    else:
        rows = x.shape[0]
        out_shape = jax.ShapeDtypeStruct(x.shape, jnp.float32)
    return pl.pallas_call(
        functools.partial(_exchange_kernel, mode, axis, n, rows),
        out_shape=out_shape,
        in_specs=[pl.BlockSpec(memory_space=pltpu.VMEM)],
        out_specs=pl.BlockSpec(memory_space=pltpu.VMEM),
        scratch_shapes=[
            pltpu.VMEM((n, rows, x.shape[1]), x.dtype),
            pltpu.SemaphoreType.DMA((n,)),
            pltpu.SemaphoreType.DMA((n,)),
        ],
        compiler_params=pltpu.CompilerParams(collective_id=collective_id, has_side_effects=True),
    )(x)


def _ring_rs_kernel(side, cols, p_ref, out_ref, recv1, acc1, s1, recv2, acc2, send_sem, recv_sem):
    w = lax.axis_index("wa")
    x, z = w // side, lax.rem(w, side)

    def peer(axis, delta):
        if axis == 0:
            return lax.rem(x + delta + side, side) * side + z
        return x * side + lax.rem(z + delta + side, side)

    barrier = pltpu.get_barrier_semaphore()
    for axis in (0, 1):
        for delta in (1, -1):
            pl.semaphore_signal(barrier, inc=1, device_id={"wa": peer(axis, delta)}, device_id_type=MESH)
    pl.semaphore_wait(barrier, 4)

    flows = []
    for f in range(4):
        first = 0 if f < 2 else 1
        delta = 1 if f % 2 == 0 else -1
        flows.append((first, delta, pl.ds(f * cols, cols)))

    def own1(f, chunk):
        first, _, c = flows[f]
        if first == 0:
            return p_ref.at[chunk, :, :, c]
        return p_ref.at[:, chunk, :, c]

    def sem(stage, step, f):
        return (stage * 3 + step) * 4 + f

    sends = []
    pos1 = [x if flows[f][0] == 0 else z for f in range(4)]
    pos2 = [z if flows[f][0] == 0 else x for f in range(4)]
    last = [None] * 4
    for step in range(side - 1):
        for f in range(4):
            first, delta, _ = flows[f]
            chunk = lax.rem(pos1[f] - delta * (step + 1) + 2 * side, side)
            if step == 0:
                source = own1(f, chunk)
            else:
                last[f].wait_recv()
                acc1[f, step - 1] = recv1[f, step - 1] + own1(f, chunk)[...]
                source = acc1.at[f, step - 1]
            copy = pltpu.make_async_remote_copy(
                src_ref=source, dst_ref=recv1.at[f, step],
                send_sem=send_sem.at[sem(0, step, f)], recv_sem=recv_sem.at[sem(0, step, f)],
                device_id={"wa": peer(first, delta)}, device_id_type=MESH)
            copy.start()
            sends.append(copy)
            last[f] = copy
    for f in range(4):
        last[f].wait_recv()
        s1[f] = recv1[f, side - 2] + own1(f, pos1[f])[...]
    for step in range(side - 1):
        for f in range(4):
            first, delta, _ = flows[f]
            chunk = lax.rem(pos2[f] - delta * (step + 1) + 2 * side, side)
            if step == 0:
                source = s1.at[f, chunk]
            else:
                last[f].wait_recv()
                acc2[f, step - 1] = recv2[f, step - 1] + s1[f, chunk]
                source = acc2.at[f, step - 1]
            copy = pltpu.make_async_remote_copy(
                src_ref=source, dst_ref=recv2.at[f, step],
                send_sem=send_sem.at[sem(1, step, f)], recv_sem=recv_sem.at[sem(1, step, f)],
                device_id={"wa": peer(1 - first, delta)}, device_id_type=MESH)
            copy.start()
            sends.append(copy)
            last[f] = copy
    for f in range(4):
        last[f].wait_recv()
        out_ref[:, flows[f][2]] = recv2[f, side - 2] + s1[f, pos2[f]]
    for copy in sends:
        copy.wait_send()


def ring_reduce_scatter(partial, n, collective_id):
    side = 4
    rows = partial.shape[0] // n
    width = partial.shape[1]
    cols = width // 4
    p4 = partial.reshape(side, side, rows, width)
    f32 = jnp.float32
    return pl.pallas_call(
        functools.partial(_ring_rs_kernel, side, cols),
        out_shape=jax.ShapeDtypeStruct((rows, width), f32),
        in_specs=[pl.BlockSpec(memory_space=pltpu.VMEM)],
        out_specs=pl.BlockSpec(memory_space=pltpu.VMEM),
        scratch_shapes=[
            pltpu.VMEM((4, side - 1, side, rows, cols), f32),
            pltpu.VMEM((4, side - 2, side, rows, cols), f32),
            pltpu.VMEM((4, side, rows, cols), f32),
            pltpu.VMEM((4, side - 1, rows, cols), f32),
            pltpu.VMEM((4, side - 2, rows, cols), f32),
            pltpu.SemaphoreType.DMA((24,)),
            pltpu.SemaphoreType.DMA((24,)),
        ],
        compiler_params=pltpu.CompilerParams(
            collective_id=collective_id, has_side_effects=True, vmem_limit_bytes=60 * 1024 * 1024),
    )(p4)


def body(tokens, norm_gain, gate_weight, up_weight, down_weight):
    n_wa = lax.axis_size("wa")
    n_ha = lax.axis_size("ha")
    own_values = tokens.astype(jnp.float32)
    model_width = own_values.shape[1] * n_wa
    own_rows = own_values.shape[0]
    partial_squares = jnp.sum(own_values * own_values, axis=1)
    packed = jnp.pad(partial_squares.reshape(8, own_rows // 8), ((0, 0), (0, 128 - own_rows // 8)))
    squares = exchange(packed, "sum", "wa", n_wa, 0)[:, : own_rows // 8].reshape(own_rows, 1)
    mean_square = squares / model_width
    normed = (own_values * lax.rsqrt(mean_square + 1e-05) * norm_gain[None, :]).astype(jnp.bfloat16)
    gathered = exchange(normed, "gather", "ha", n_ha, 1)
    hidden_width = gate_weight.shape[1]
    gate_part = jnp.dot(gathered, gate_weight, preferred_element_type=jnp.float32)
    up_part = jnp.dot(gathered, up_weight, preferred_element_type=jnp.float32)
    summed = ring_reduce_scatter(jnp.concatenate([gate_part, up_part], axis=1), n_wa, 2)
    gate = summed[:, :hidden_width]
    up = summed[:, hidden_width:]
    hidden = (jax.nn.silu(gate) * up).astype(jnp.bfloat16)
    all_hidden = lax.all_gather(hidden, "wa", axis=0, tiled=True)
    partial_out = jnp.dot(all_hidden, down_weight, preferred_element_type=jnp.float32)
    mixed_out = exchange(partial_out.astype(jnp.bfloat16), "scatter", "ha", n_ha, 4)
    return mixed_out.astype(jnp.bfloat16)


def solution(mesh):
    placed = (P("ha", "wa"), P("wa"), P("wa", "ha"), P("wa", "ha"), P("ha", "wa"))
    return jax.shard_map(body, mesh=mesh, in_specs=placed, out_specs=P("ha", "wa"), check_vma=False)
```

```python
import functools

import jax
import jax.numpy as jnp
from jax import lax
from jax.experimental import pallas as pl
from jax.experimental.pallas import tpu as pltpu
from jax.sharding import PartitionSpec as P

MESH = pl.DeviceIdType.MESH


def _greet(axis, n, me):
    barrier = pltpu.get_barrier_semaphore()
    for k in range(1, n):
        pl.semaphore_signal(barrier, inc=1, device_id={axis: lax.rem(me + k, n)}, device_id_type=MESH)
    pl.semaphore_wait(barrier, n - 1)


def _exchange_kernel(mode, axis, n, rows, x_ref, out_ref, slots, send_sem, recv_sem):
    me = lax.axis_index(axis)
    _greet(axis, n, me)
    copies = []
    for k in range(1, n):
        peer = lax.rem(me + k, n)
        if mode == "gather":
            source = x_ref
        elif mode == "scatter":
            source = x_ref.at[pl.ds(pl.multiple_of(peer * rows, rows), rows)]
        else:
            source = x_ref
        copy = pltpu.make_async_remote_copy(
            src_ref=source,
            dst_ref=slots.at[k],
            send_sem=send_sem.at[k],
            recv_sem=recv_sem.at[k],
            device_id={axis: peer},
            device_id_type=MESH,
        )
        copy.start()
        copies.append(copy)
    if mode == "gather":
        out_ref[pl.ds(pl.multiple_of(me * rows, rows), rows), :] = x_ref[...]
        for k, copy in enumerate(copies, 1):
            copy.wait()
            sender = lax.rem(me + n - k, n)
            out_ref[pl.ds(pl.multiple_of(sender * rows, rows), rows), :] = slots[k]
    elif mode == "scatter":
        total = x_ref[pl.ds(pl.multiple_of(me * rows, rows), rows), :].astype(jnp.float32)
        for k, copy in enumerate(copies, 1):
            copy.wait()
            total = total + slots[k].astype(jnp.float32)
        out_ref[...] = total
    else:
        for copy in copies:
            copy.wait()
        slots[0] = x_ref[...]
        total = jnp.zeros(out_ref.shape, jnp.float32)
        for sender in range(n):
            total = total + slots[lax.rem(me + n - sender, n)].astype(jnp.float32)
        out_ref[...] = total


def exchange(x, mode, axis, n, collective_id):
    if n == 1:
        return x.astype(jnp.float32) if mode != "gather" else x
    if mode == "gather":
        rows = x.shape[0]
        out_shape = jax.ShapeDtypeStruct((n * rows, x.shape[1]), x.dtype)
    elif mode == "scatter":
        rows = x.shape[0] // n
        out_shape = jax.ShapeDtypeStruct((rows, x.shape[1]), jnp.float32)
    else:
        rows = x.shape[0]
        out_shape = jax.ShapeDtypeStruct(x.shape, jnp.float32)
    return pl.pallas_call(
        functools.partial(_exchange_kernel, mode, axis, n, rows),
        out_shape=out_shape,
        in_specs=[pl.BlockSpec(memory_space=pltpu.VMEM)],
        out_specs=pl.BlockSpec(memory_space=pltpu.VMEM),
        scratch_shapes=[
            pltpu.VMEM((n, rows, x.shape[1]), x.dtype),
            pltpu.SemaphoreType.DMA((n,)),
            pltpu.SemaphoreType.DMA((n,)),
        ],
        compiler_params=pltpu.CompilerParams(collective_id=collective_id, has_side_effects=True),
    )(x)


def _ring_rs_kernel(side, cols, p_ref, out_ref, recv1, acc1, s1, recv2, acc2, send_sem, recv_sem):
    w = lax.axis_index("wa")
    x, z = w // side, lax.rem(w, side)

    def peer(axis, delta):
        if axis == 0:
            return lax.rem(x + delta + side, side) * side + z
        return x * side + lax.rem(z + delta + side, side)

    barrier = pltpu.get_barrier_semaphore()
    for axis in (0, 1):
        for delta in (1, -1):
            pl.semaphore_signal(barrier, inc=1, device_id={"wa": peer(axis, delta)}, device_id_type=MESH)
    pl.semaphore_wait(barrier, 4)

    flows = []
    for f in range(4):
        first = 0 if f < 2 else 1
        delta = 1 if f % 2 == 0 else -1
        flows.append((first, delta, pl.ds(f * cols, cols)))

    def own1(f, chunk):
        first, _, c = flows[f]
        if first == 0:
            return p_ref.at[chunk, :, :, c]
        return p_ref.at[:, chunk, :, c]

    def sem(stage, step, f):
        return (stage * 3 + step) * 4 + f

    sends = []
    pos1 = [x if flows[f][0] == 0 else z for f in range(4)]
    pos2 = [z if flows[f][0] == 0 else x for f in range(4)]
    last = [None] * 4
    for step in range(side - 1):
        for f in range(4):
            first, delta, _ = flows[f]
            chunk = lax.rem(pos1[f] - delta * (step + 1) + 2 * side, side)
            if step == 0:
                source = own1(f, chunk)
            else:
                last[f].wait_recv()
                acc1[f, step - 1] = recv1[f, step - 1] + own1(f, chunk)[...]
                source = acc1.at[f, step - 1]
            copy = pltpu.make_async_remote_copy(
                src_ref=source, dst_ref=recv1.at[f, step],
                send_sem=send_sem.at[sem(0, step, f)], recv_sem=recv_sem.at[sem(0, step, f)],
                device_id={"wa": peer(first, delta)}, device_id_type=MESH)
            copy.start()
            sends.append(copy)
            last[f] = copy
    for f in range(4):
        last[f].wait_recv()
        s1[f] = recv1[f, side - 2] + own1(f, pos1[f])[...]
    for step in range(side - 1):
        for f in range(4):
            first, delta, _ = flows[f]
            chunk = lax.rem(pos2[f] - delta * (step + 1) + 2 * side, side)
            if step == 0:
                source = s1.at[f, chunk]
            else:
                last[f].wait_recv()
                acc2[f, step - 1] = recv2[f, step - 1] + s1[f, chunk]
                source = acc2.at[f, step - 1]
            copy = pltpu.make_async_remote_copy(
                src_ref=source, dst_ref=recv2.at[f, step],
                send_sem=send_sem.at[sem(1, step, f)], recv_sem=recv_sem.at[sem(1, step, f)],
                device_id={"wa": peer(1 - first, delta)}, device_id_type=MESH)
            copy.start()
            sends.append(copy)
            last[f] = copy
    for f in range(4):
        last[f].wait_recv()
        out_ref[:, flows[f][2]] = recv2[f, side - 2] + s1[f, pos2[f]]
    for copy in sends:
        copy.wait_send()


def ring_reduce_scatter(partial, n, collective_id):
    side = 4
    rows = partial.shape[0] // n
    width = partial.shape[1]
    cols = width // 4
    p4 = partial.reshape(side, side, rows, width)
    f32 = jnp.float32
    return pl.pallas_call(
        functools.partial(_ring_rs_kernel, side, cols),
        out_shape=jax.ShapeDtypeStruct((rows, width), f32),
        in_specs=[pl.BlockSpec(memory_space=pltpu.VMEM)],
        out_specs=pl.BlockSpec(memory_space=pltpu.VMEM),
        scratch_shapes=[
            pltpu.VMEM((4, side - 1, side, rows, cols), f32),
            pltpu.VMEM((4, side - 2, side, rows, cols), f32),
            pltpu.VMEM((4, side, rows, cols), f32),
            pltpu.VMEM((4, side - 1, rows, cols), f32),
            pltpu.VMEM((4, side - 2, rows, cols), f32),
            pltpu.SemaphoreType.DMA((24,)),
            pltpu.SemaphoreType.DMA((24,)),
        ],
        compiler_params=pltpu.CompilerParams(
            collective_id=collective_id, has_side_effects=True, vmem_limit_bytes=60 * 1024 * 1024),
    )(p4)


def _grid_ag_kernel(side, cols, h_ref, out_ref, gath, send_sem, recv_sem, local_sem):
    w = lax.axis_index("wa")
    x, z = w // side, lax.rem(w, side)

    def peer(axis, k):
        if axis == 0:
            return lax.rem(x + k, side) * side + z
        return x * side + lax.rem(z + k, side)

    barrier = pltpu.get_barrier_semaphore()
    for axis in (0, 1):
        for k in range(1, side):
            pl.semaphore_signal(barrier, inc=1, device_id={"wa": peer(axis, k)}, device_id_type=MESH)
    pl.semaphore_wait(barrier, 2 * (side - 1))

    halves = [pl.ds(0, cols), pl.ds(cols, cols)]
    locals_ = []
    for f in range(2):
        c = halves[f]
        copy = pltpu.make_async_copy(h_ref.at[:, c], gath.at[x, z, :, c], local_sem.at[f])
        copy.start()
        locals_.append(copy)
    sends = []
    stage2 = []
    stage1 = [[], []]
    for f in range(2):
        c = halves[f]
        for k in range(1, side):
            index = (f * 2 + 0) * side + k
            copy = pltpu.make_async_remote_copy(
                src_ref=h_ref.at[:, c], dst_ref=gath.at[x, z, :, c],
                send_sem=send_sem.at[index], recv_sem=recv_sem.at[index],
                device_id={"wa": peer(f, k)}, device_id_type=MESH)
            copy.start()
            sends.append(copy)
            stage1[f].append(copy)
    for f in range(2):
        c = halves[f]
        locals_[f].wait()
        for copy in stage1[f]:
            copy.wait_recv()
        if f == 0:
            view = gath.at[:, z, :, c]
        else:
            view = gath.at[x, :, :, c]
        for k in range(1, side):
            index = (f * 2 + 1) * side + k
            copy = pltpu.make_async_remote_copy(
                src_ref=view, dst_ref=view,
                send_sem=send_sem.at[index], recv_sem=recv_sem.at[index],
                device_id={"wa": peer(1 - f, k)}, device_id_type=MESH)
            copy.start()
            stage2.append(copy)
    for copy in sends:
        copy.wait_send()
    for copy in stage2:
        copy.wait()
    final = pltpu.make_async_copy(gath, out_ref, local_sem.at[2])
    final.start()
    final.wait()


def grid_all_gather(h, n, collective_id):
    side = 4
    rows, width = h.shape
    cols = width // 2
    out = pl.pallas_call(
        functools.partial(_grid_ag_kernel, side, cols),
        out_shape=jax.ShapeDtypeStruct((side, side, rows, width), h.dtype),
        in_specs=[pl.BlockSpec(memory_space=pltpu.VMEM)],
        out_specs=pl.BlockSpec(memory_space=pltpu.VMEM),
        scratch_shapes=[
            pltpu.VMEM((side, side, rows, width), h.dtype),
            pltpu.SemaphoreType.DMA((4 * side,)),
            pltpu.SemaphoreType.DMA((4 * side,)),
            pltpu.SemaphoreType.DMA((3,)),
        ],
        compiler_params=pltpu.CompilerParams(collective_id=collective_id, has_side_effects=True),
    )(h)
    return out.reshape(n * rows, width)


def body(tokens, norm_gain, gate_weight, up_weight, down_weight):
    n_wa = lax.axis_size("wa")
    n_ha = lax.axis_size("ha")
    own_values = tokens.astype(jnp.float32)
    model_width = own_values.shape[1] * n_wa
    own_rows = own_values.shape[0]
    partial_squares = jnp.sum(own_values * own_values, axis=1)
    packed = jnp.pad(partial_squares.reshape(8, own_rows // 8), ((0, 0), (0, 128 - own_rows // 8)))
    squares = exchange(packed, "sum", "wa", n_wa, 0)[:, : own_rows // 8].reshape(own_rows, 1)
    mean_square = squares / model_width
    normed = (own_values * lax.rsqrt(mean_square + 1e-05) * norm_gain[None, :]).astype(jnp.bfloat16)
    gathered = exchange(normed, "gather", "ha", n_ha, 1)
    hidden_width = gate_weight.shape[1]
    gate_part = jnp.dot(gathered, gate_weight, preferred_element_type=jnp.float32)
    up_part = jnp.dot(gathered, up_weight, preferred_element_type=jnp.float32)
    summed = ring_reduce_scatter(jnp.concatenate([gate_part, up_part], axis=1), n_wa, 2)
    gate = summed[:, :hidden_width]
    up = summed[:, hidden_width:]
    hidden = (jax.nn.silu(gate) * up).astype(jnp.bfloat16)
    all_hidden = grid_all_gather(hidden, n_wa, 3)
    partial_out = jnp.dot(all_hidden, down_weight, preferred_element_type=jnp.float32)
    mixed_out = exchange(partial_out.astype(jnp.bfloat16), "scatter", "ha", n_ha, 4)
    return mixed_out.astype(jnp.bfloat16)


def solution(mesh):
    placed = (P("ha", "wa"), P("wa"), P("wa", "ha"), P("wa", "ha"), P("ha", "wa"))
    return jax.shard_map(body, mesh=mesh, in_specs=placed, out_specs=P("ha", "wa"), check_vma=False)
```

```python
import functools

import jax
import jax.numpy as jnp
from jax import lax
from jax.experimental import pallas as pl
from jax.experimental.pallas import tpu as pltpu
from jax.sharding import PartitionSpec as P

MESH = pl.DeviceIdType.MESH


def _greet(axis, n, me):
    barrier = pltpu.get_barrier_semaphore()
    for k in range(1, n):
        pl.semaphore_signal(barrier, inc=1, device_id={axis: lax.rem(me + k, n)}, device_id_type=MESH)
    pl.semaphore_wait(barrier, n - 1)


def _exchange_kernel(mode, axis, n, rows, x_ref, out_ref, slots, send_sem, recv_sem):
    me = lax.axis_index(axis)
    _greet(axis, n, me)
    copies = []
    for k in range(1, n):
        peer = lax.rem(me + k, n)
        if mode == "gather":
            source = x_ref
        elif mode == "scatter":
            source = x_ref.at[pl.ds(pl.multiple_of(peer * rows, rows), rows)]
        else:
            source = x_ref
        copy = pltpu.make_async_remote_copy(
            src_ref=source,
            dst_ref=slots.at[k],
            send_sem=send_sem.at[k],
            recv_sem=recv_sem.at[k],
            device_id={axis: peer},
            device_id_type=MESH,
        )
        copy.start()
        copies.append(copy)
    if mode == "gather":
        out_ref[pl.ds(pl.multiple_of(me * rows, rows), rows), :] = x_ref[...]
        for k, copy in enumerate(copies, 1):
            copy.wait()
            sender = lax.rem(me + n - k, n)
            out_ref[pl.ds(pl.multiple_of(sender * rows, rows), rows), :] = slots[k]
    elif mode == "scatter":
        total = x_ref[pl.ds(pl.multiple_of(me * rows, rows), rows), :].astype(jnp.float32)
        for k, copy in enumerate(copies, 1):
            copy.wait()
            total = total + slots[k].astype(jnp.float32)
        out_ref[...] = total
    else:
        for copy in copies:
            copy.wait()
        slots[0] = x_ref[...]
        total = jnp.zeros(out_ref.shape, jnp.float32)
        for sender in range(n):
            total = total + slots[lax.rem(me + n - sender, n)].astype(jnp.float32)
        out_ref[...] = total


def exchange(x, mode, axis, n, collective_id):
    if n == 1:
        return x.astype(jnp.float32) if mode != "gather" else x
    if mode == "gather":
        rows = x.shape[0]
        out_shape = jax.ShapeDtypeStruct((n * rows, x.shape[1]), x.dtype)
    elif mode == "scatter":
        rows = x.shape[0] // n
        out_shape = jax.ShapeDtypeStruct((rows, x.shape[1]), jnp.float32)
    else:
        rows = x.shape[0]
        out_shape = jax.ShapeDtypeStruct(x.shape, jnp.float32)
    return pl.pallas_call(
        functools.partial(_exchange_kernel, mode, axis, n, rows),
        out_shape=out_shape,
        in_specs=[pl.BlockSpec(memory_space=pltpu.VMEM)],
        out_specs=pl.BlockSpec(memory_space=pltpu.VMEM),
        scratch_shapes=[
            pltpu.VMEM((n, rows, x.shape[1]), x.dtype),
            pltpu.SemaphoreType.DMA((n,)),
            pltpu.SemaphoreType.DMA((n,)),
        ],
        compiler_params=pltpu.CompilerParams(collective_id=collective_id, has_side_effects=True),
    )(x)


def _ring_rs_kernel(side, cols, g_ref, u_ref, out_ref, recv1, acc1, s1, recv2, acc2, send_sem, recv_sem):
    w = lax.axis_index("wa")
    x, z = w // side, lax.rem(w, side)

    def peer(axis, delta):
        if axis == 0:
            return lax.rem(x + delta + side, side) * side + z
        return x * side + lax.rem(z + delta + side, side)

    barrier = pltpu.get_barrier_semaphore()
    for axis in (0, 1):
        for delta in (1, -1):
            pl.semaphore_signal(barrier, inc=1, device_id={"wa": peer(axis, delta)}, device_id_type=MESH)
    pl.semaphore_wait(barrier, 4)

    flows = []
    for f in range(4):
        first = 0 if f < 2 else 1
        delta = 1 if f % 2 == 0 else -1
        flows.append((first, delta, pl.ds(f * cols, cols)))

    def own1(f, chunk):
        first = flows[f][0]
        p_ref = g_ref if f < 2 else u_ref
        c = pl.ds((f % 2) * cols, cols)
        if first == 0:
            return p_ref.at[chunk, :, :, c]
        return p_ref.at[:, chunk, :, c]

    def sem(stage, step, f):
        return (stage * 3 + step) * 4 + f

    sends = []
    pos1 = [x if flows[f][0] == 0 else z for f in range(4)]
    pos2 = [z if flows[f][0] == 0 else x for f in range(4)]
    last = [None] * 4
    for step in range(side - 1):
        for f in range(4):
            first, delta, _ = flows[f]
            chunk = lax.rem(pos1[f] - delta * (step + 1) + 2 * side, side)
            if step == 0:
                source = own1(f, chunk)
            else:
                last[f].wait_recv()
                acc1[f, step - 1] = recv1[f, step - 1] + own1(f, chunk)[...]
                source = acc1.at[f, step - 1]
            copy = pltpu.make_async_remote_copy(
                src_ref=source, dst_ref=recv1.at[f, step],
                send_sem=send_sem.at[sem(0, step, f)], recv_sem=recv_sem.at[sem(0, step, f)],
                device_id={"wa": peer(first, delta)}, device_id_type=MESH)
            copy.start()
            sends.append(copy)
            last[f] = copy
    for f in range(4):
        last[f].wait_recv()
        s1[f] = recv1[f, side - 2] + own1(f, pos1[f])[...]
    for step in range(side - 1):
        for f in range(4):
            first, delta, _ = flows[f]
            chunk = lax.rem(pos2[f] - delta * (step + 1) + 2 * side, side)
            if step == 0:
                source = s1.at[f, chunk]
            else:
                last[f].wait_recv()
                acc2[f, step - 1] = recv2[f, step - 1] + s1[f, chunk]
                source = acc2.at[f, step - 1]
            copy = pltpu.make_async_remote_copy(
                src_ref=source, dst_ref=recv2.at[f, step],
                send_sem=send_sem.at[sem(1, step, f)], recv_sem=recv_sem.at[sem(1, step, f)],
                device_id={"wa": peer(1 - first, delta)}, device_id_type=MESH)
            copy.start()
            sends.append(copy)
            last[f] = copy
    for f in range(4):
        last[f].wait_recv()
        out_ref[:, flows[f][2]] = recv2[f, side - 2] + s1[f, pos2[f]]
    for copy in sends:
        copy.wait_send()


def ring_reduce_scatter(gate_part, up_part, n, collective_id):
    side = 4
    rows = gate_part.shape[0] // n
    width = 2 * gate_part.shape[1]
    cols = width // 4
    g4 = gate_part.reshape(side, side, rows, width // 2)
    u4 = up_part.reshape(side, side, rows, width // 2)
    f32 = jnp.float32
    return pl.pallas_call(
        functools.partial(_ring_rs_kernel, side, cols),
        out_shape=jax.ShapeDtypeStruct((rows, width), f32),
        in_specs=[pl.BlockSpec(memory_space=pltpu.VMEM)] * 2,
        out_specs=pl.BlockSpec(memory_space=pltpu.VMEM),
        scratch_shapes=[
            pltpu.VMEM((4, side - 1, side, rows, cols), f32),
            pltpu.VMEM((4, side - 2, side, rows, cols), f32),
            pltpu.VMEM((4, side, rows, cols), f32),
            pltpu.VMEM((4, side - 1, rows, cols), f32),
            pltpu.VMEM((4, side - 2, rows, cols), f32),
            pltpu.SemaphoreType.DMA((24,)),
            pltpu.SemaphoreType.DMA((24,)),
        ],
        compiler_params=pltpu.CompilerParams(
            collective_id=collective_id, has_side_effects=True, vmem_limit_bytes=60 * 1024 * 1024),
    )(g4, u4)


def _grid_ag_kernel(side, cols, h_ref, out_ref, gath, send_sem, recv_sem, local_sem):
    w = lax.axis_index("wa")
    x, z = w // side, lax.rem(w, side)

    def peer(axis, k):
        if axis == 0:
            return lax.rem(x + k, side) * side + z
        return x * side + lax.rem(z + k, side)

    barrier = pltpu.get_barrier_semaphore()
    for axis in (0, 1):
        for k in range(1, side):
            pl.semaphore_signal(barrier, inc=1, device_id={"wa": peer(axis, k)}, device_id_type=MESH)
    pl.semaphore_wait(barrier, 2 * (side - 1))

    halves = [pl.ds(0, cols), pl.ds(cols, cols)]
    locals_ = []
    for f in range(2):
        c = halves[f]
        copy = pltpu.make_async_copy(h_ref.at[:, c], gath.at[x, z, :, c], local_sem.at[f])
        copy.start()
        locals_.append(copy)
    sends = []
    stage2 = []
    stage1 = [[], []]
    for f in range(2):
        c = halves[f]
        for k in range(1, side):
            index = (f * 2 + 0) * side + k
            copy = pltpu.make_async_remote_copy(
                src_ref=h_ref.at[:, c], dst_ref=gath.at[x, z, :, c],
                send_sem=send_sem.at[index], recv_sem=recv_sem.at[index],
                device_id={"wa": peer(f, k)}, device_id_type=MESH)
            copy.start()
            sends.append(copy)
            stage1[f].append(copy)
    for f in range(2):
        c = halves[f]
        locals_[f].wait()
        for copy in stage1[f]:
            copy.wait_recv()
        if f == 0:
            view = gath.at[:, z, :, c]
        else:
            view = gath.at[x, :, :, c]
        for k in range(1, side):
            index = (f * 2 + 1) * side + k
            copy = pltpu.make_async_remote_copy(
                src_ref=view, dst_ref=view,
                send_sem=send_sem.at[index], recv_sem=recv_sem.at[index],
                device_id={"wa": peer(1 - f, k)}, device_id_type=MESH)
            copy.start()
            stage2.append(copy)
    for copy in sends:
        copy.wait_send()
    for copy in stage2:
        copy.wait()
    final = pltpu.make_async_copy(gath, out_ref, local_sem.at[2])
    final.start()
    final.wait()


def grid_all_gather(h, n, collective_id):
    side = 4
    rows, width = h.shape
    cols = width // 2
    out = pl.pallas_call(
        functools.partial(_grid_ag_kernel, side, cols),
        out_shape=jax.ShapeDtypeStruct((side, side, rows, width), h.dtype),
        in_specs=[pl.BlockSpec(memory_space=pltpu.VMEM)],
        out_specs=pl.BlockSpec(memory_space=pltpu.VMEM),
        scratch_shapes=[
            pltpu.VMEM((side, side, rows, width), h.dtype),
            pltpu.SemaphoreType.DMA((4 * side,)),
            pltpu.SemaphoreType.DMA((4 * side,)),
            pltpu.SemaphoreType.DMA((3,)),
        ],
        compiler_params=pltpu.CompilerParams(collective_id=collective_id, has_side_effects=True),
    )(h)
    return out.reshape(n * rows, width)


def body(tokens, norm_gain, gate_weight, up_weight, down_weight):
    n_wa = lax.axis_size("wa")
    n_ha = lax.axis_size("ha")
    own_values = tokens.astype(jnp.float32)
    model_width = own_values.shape[1] * n_wa
    own_rows = own_values.shape[0]
    partial_squares = jnp.sum(own_values * own_values, axis=1)
    packed = jnp.pad(partial_squares.reshape(8, own_rows // 8), ((0, 0), (0, 128 - own_rows // 8)))
    squares = exchange(packed, "sum", "wa", n_wa, 0)[:, : own_rows // 8].reshape(own_rows, 1)
    mean_square = squares / model_width
    normed = (own_values * lax.rsqrt(mean_square + 1e-05) * norm_gain[None, :]).astype(jnp.bfloat16)
    gathered = exchange(normed, "gather", "ha", n_ha, 1)
    hidden_width = gate_weight.shape[1]
    gate_part = jnp.dot(gathered, gate_weight, preferred_element_type=jnp.float32)
    up_part = jnp.dot(gathered, up_weight, preferred_element_type=jnp.float32)
    summed = ring_reduce_scatter(gate_part, up_part, n_wa, 2)
    gate = summed[:, :hidden_width]
    up = summed[:, hidden_width:]
    hidden = (jax.nn.silu(gate) * up).astype(jnp.bfloat16)
    all_hidden = grid_all_gather(hidden, n_wa, 3)
    partial_out = jnp.dot(all_hidden, down_weight, preferred_element_type=jnp.float32)
    mixed_out = exchange(partial_out.astype(jnp.bfloat16), "scatter", "ha", n_ha, 4)
    return mixed_out.astype(jnp.bfloat16)


def solution(mesh):
    placed = (P("ha", "wa"), P("wa"), P("wa", "ha"), P("wa", "ha"), P("ha", "wa"))
    return jax.shard_map(body, mesh=mesh, in_specs=placed, out_specs=P("ha", "wa"), check_vma=False)
```

```python
import functools

import jax
import jax.numpy as jnp
from jax import lax
from jax.experimental import pallas as pl
from jax.experimental.pallas import tpu as pltpu
from jax.sharding import PartitionSpec as P

MESH = pl.DeviceIdType.MESH


def _greet(axis, n, me):
    barrier = pltpu.get_barrier_semaphore()
    for k in range(1, n):
        pl.semaphore_signal(barrier, inc=1, device_id={axis: lax.rem(me + k, n)}, device_id_type=MESH)
    pl.semaphore_wait(barrier, n - 1)


def _exchange_kernel(mode, axis, n, rows, x_ref, out_ref, slots, send_sem, recv_sem):
    me = lax.axis_index(axis)
    _greet(axis, n, me)
    copies = []
    for k in range(1, n):
        peer = lax.rem(me + k, n)
        if mode == "gather":
            source = x_ref
        elif mode == "scatter":
            source = x_ref.at[pl.ds(pl.multiple_of(peer * rows, rows), rows)]
        else:
            source = x_ref
        copy = pltpu.make_async_remote_copy(
            src_ref=source,
            dst_ref=slots.at[k],
            send_sem=send_sem.at[k],
            recv_sem=recv_sem.at[k],
            device_id={axis: peer},
            device_id_type=MESH,
        )
        copy.start()
        copies.append(copy)
    if mode == "gather":
        out_ref[pl.ds(pl.multiple_of(me * rows, rows), rows), :] = x_ref[...]
        for k, copy in enumerate(copies, 1):
            copy.wait()
            sender = lax.rem(me + n - k, n)
            out_ref[pl.ds(pl.multiple_of(sender * rows, rows), rows), :] = slots[k]
    elif mode == "scatter":
        total = x_ref[pl.ds(pl.multiple_of(me * rows, rows), rows), :].astype(jnp.float32)
        for k, copy in enumerate(copies, 1):
            copy.wait()
            total = total + slots[k].astype(jnp.float32)
        out_ref[...] = total
    else:
        for copy in copies:
            copy.wait()
        slots[0] = x_ref[...]
        total = jnp.zeros(out_ref.shape, jnp.float32)
        for sender in range(n):
            total = total + slots[lax.rem(me + n - sender, n)].astype(jnp.float32)
        out_ref[...] = total


def exchange(x, mode, axis, n, collective_id):
    if n == 1:
        return x.astype(jnp.float32) if mode != "gather" else x
    if mode == "gather":
        rows = x.shape[0]
        out_shape = jax.ShapeDtypeStruct((n * rows, x.shape[1]), x.dtype)
    elif mode == "scatter":
        rows = x.shape[0] // n
        out_shape = jax.ShapeDtypeStruct((rows, x.shape[1]), jnp.float32)
    else:
        rows = x.shape[0]
        out_shape = jax.ShapeDtypeStruct(x.shape, jnp.float32)
    return pl.pallas_call(
        functools.partial(_exchange_kernel, mode, axis, n, rows),
        out_shape=out_shape,
        in_specs=[pl.BlockSpec(memory_space=pltpu.VMEM)],
        out_specs=pl.BlockSpec(memory_space=pltpu.VMEM),
        scratch_shapes=[
            pltpu.VMEM((n, rows, x.shape[1]), x.dtype),
            pltpu.SemaphoreType.DMA((n,)),
            pltpu.SemaphoreType.DMA((n,)),
        ],
        compiler_params=pltpu.CompilerParams(collective_id=collective_id, has_side_effects=True),
    )(x)


def _ring_rs_kernel(side, cols, t_ref, g_hbm, u_hbm, out_ref, wbuf, first_buf, tmp, recv1, acc1, s1,
                    recv2, acc2, send_sem, recv_sem, w_sem):
    w = lax.axis_index("wa")
    x, z = w // side, lax.rem(w, side)
    loads = []
    for f in range(4):
        source = g_hbm if f < 2 else u_hbm
        load = pltpu.make_async_copy(source.at[:, pl.ds((f % 2) * cols, cols)], wbuf.at[f], w_sem.at[f])
        load.start()
        loads.append(load)

    def peer(axis, delta):
        if axis == 0:
            return lax.rem(x + delta + side, side) * side + z
        return x * side + lax.rem(z + delta + side, side)

    barrier = pltpu.get_barrier_semaphore()
    for axis in (0, 1):
        for delta in (1, -1):
            pl.semaphore_signal(barrier, inc=1, device_id={"wa": peer(axis, delta)}, device_id_type=MESH)
    pl.semaphore_wait(barrier, 4)

    flows = []
    for f in range(4):
        first = 0 if f < 2 else 1
        delta = 1 if f % 2 == 0 else -1
        flows.append((first, delta, pl.ds(f * cols, cols)))

    def own1(f, chunk):
        if flows[f][0] == 0:
            rows = t_ref[chunk]
        else:
            rows = t_ref[:, chunk]
        block = rows.reshape(side * rows.shape[1], rows.shape[2])
        product = jnp.dot(block, wbuf[f], preferred_element_type=jnp.float32)
        return product.reshape(side, rows.shape[1], cols)

    def sem(stage, step, f):
        return (stage * 3 + step) * 4 + f

    sends = []
    pos1 = [x if flows[f][0] == 0 else z for f in range(4)]
    pos2 = [z if flows[f][0] == 0 else x for f in range(4)]
    last = [None] * 4
    for step in range(side - 1):
        for f in range(4):
            first, delta, _ = flows[f]
            chunk = lax.rem(pos1[f] - delta * (step + 1) + 2 * side, side)
            if step == 0:
                loads[f].wait()
                first_buf[f] = own1(f, chunk)
                source = first_buf.at[f]
            else:
                tmp[f] = own1(f, chunk)
                last[f].wait_recv()
                acc1[f, step - 1] = recv1[f, step - 1] + tmp[f]
                source = acc1.at[f, step - 1]
            copy = pltpu.make_async_remote_copy(
                src_ref=source, dst_ref=recv1.at[f, step],
                send_sem=send_sem.at[sem(0, step, f)], recv_sem=recv_sem.at[sem(0, step, f)],
                device_id={"wa": peer(first, delta)}, device_id_type=MESH)
            copy.start()
            sends.append(copy)
            last[f] = copy
    for f in range(4):
        tmp[f] = own1(f, pos1[f])
        last[f].wait_recv()
        s1[f] = recv1[f, side - 2] + tmp[f]
    for step in range(side - 1):
        for f in range(4):
            first, delta, _ = flows[f]
            chunk = lax.rem(pos2[f] - delta * (step + 1) + 2 * side, side)
            if step == 0:
                source = s1.at[f, chunk]
            else:
                last[f].wait_recv()
                acc2[f, step - 1] = recv2[f, step - 1] + s1[f, chunk]
                source = acc2.at[f, step - 1]
            copy = pltpu.make_async_remote_copy(
                src_ref=source, dst_ref=recv2.at[f, step],
                send_sem=send_sem.at[sem(1, step, f)], recv_sem=recv_sem.at[sem(1, step, f)],
                device_id={"wa": peer(1 - first, delta)}, device_id_type=MESH)
            copy.start()
            sends.append(copy)
            last[f] = copy
    for f in range(4):
        last[f].wait_recv()
        out_ref[:, flows[f][2]] = recv2[f, side - 2] + s1[f, pos2[f]]
    for copy in sends:
        copy.wait_send()


def ring_reduce_scatter(tokens, gate_weight, up_weight, n, collective_id):
    side = 4
    rows = tokens.shape[0] // n
    depth = tokens.shape[1]
    width = 2 * gate_weight.shape[1]
    cols = width // 4
    t4 = tokens.reshape(side, side, rows, depth)
    f32 = jnp.float32
    return pl.pallas_call(
        functools.partial(_ring_rs_kernel, side, cols),
        out_shape=jax.ShapeDtypeStruct((rows, width), f32),
        in_specs=[pl.BlockSpec(memory_space=pltpu.VMEM), pl.BlockSpec(memory_space=pl.ANY),
                  pl.BlockSpec(memory_space=pl.ANY)],
        out_specs=pl.BlockSpec(memory_space=pltpu.VMEM),
        scratch_shapes=[
            pltpu.VMEM((4, depth, cols), gate_weight.dtype),
            pltpu.VMEM((4, side, rows, cols), f32),
            pltpu.VMEM((4, side, rows, cols), f32),
            pltpu.VMEM((4, side - 1, side, rows, cols), f32),
            pltpu.VMEM((4, side - 2, side, rows, cols), f32),
            pltpu.VMEM((4, side, rows, cols), f32),
            pltpu.VMEM((4, side - 1, rows, cols), f32),
            pltpu.VMEM((4, side - 2, rows, cols), f32),
            pltpu.SemaphoreType.DMA((24,)),
            pltpu.SemaphoreType.DMA((24,)),
            pltpu.SemaphoreType.DMA((4,)),
        ],
        compiler_params=pltpu.CompilerParams(
            collective_id=collective_id, has_side_effects=True, vmem_limit_bytes=63 * 1024 * 1024),
    )(t4, gate_weight, up_weight)


def _grid_ag_kernel(side, cols, h_ref, out_ref, gath, send_sem, recv_sem, local_sem):
    w = lax.axis_index("wa")
    x, z = w // side, lax.rem(w, side)

    def peer(axis, k):
        if axis == 0:
            return lax.rem(x + k, side) * side + z
        return x * side + lax.rem(z + k, side)

    barrier = pltpu.get_barrier_semaphore()
    for axis in (0, 1):
        for k in range(1, side):
            pl.semaphore_signal(barrier, inc=1, device_id={"wa": peer(axis, k)}, device_id_type=MESH)
    pl.semaphore_wait(barrier, 2 * (side - 1))

    halves = [pl.ds(0, cols), pl.ds(cols, cols)]
    locals_ = []
    for f in range(2):
        c = halves[f]
        copy = pltpu.make_async_copy(h_ref.at[:, c], gath.at[x, z, :, c], local_sem.at[f])
        copy.start()
        locals_.append(copy)
    sends = []
    stage2 = []
    stage1 = [[], []]
    for f in range(2):
        c = halves[f]
        for k in range(1, side):
            index = (f * 2 + 0) * side + k
            copy = pltpu.make_async_remote_copy(
                src_ref=h_ref.at[:, c], dst_ref=gath.at[x, z, :, c],
                send_sem=send_sem.at[index], recv_sem=recv_sem.at[index],
                device_id={"wa": peer(f, k)}, device_id_type=MESH)
            copy.start()
            sends.append(copy)
            stage1[f].append(copy)
    for f in range(2):
        c = halves[f]
        locals_[f].wait()
        for copy in stage1[f]:
            copy.wait_recv()
        if f == 0:
            view = gath.at[:, z, :, c]
        else:
            view = gath.at[x, :, :, c]
        for k in range(1, side):
            index = (f * 2 + 1) * side + k
            copy = pltpu.make_async_remote_copy(
                src_ref=view, dst_ref=view,
                send_sem=send_sem.at[index], recv_sem=recv_sem.at[index],
                device_id={"wa": peer(1 - f, k)}, device_id_type=MESH)
            copy.start()
            stage2.append(copy)
    for copy in sends:
        copy.wait_send()
    for copy in stage2:
        copy.wait()
    final = pltpu.make_async_copy(gath, out_ref, local_sem.at[2])
    final.start()
    final.wait()


def grid_all_gather(h, n, collective_id):
    side = 4
    rows, width = h.shape
    cols = width // 2
    out = pl.pallas_call(
        functools.partial(_grid_ag_kernel, side, cols),
        out_shape=jax.ShapeDtypeStruct((side, side, rows, width), h.dtype),
        in_specs=[pl.BlockSpec(memory_space=pltpu.VMEM)],
        out_specs=pl.BlockSpec(memory_space=pltpu.VMEM),
        scratch_shapes=[
            pltpu.VMEM((side, side, rows, width), h.dtype),
            pltpu.SemaphoreType.DMA((4 * side,)),
            pltpu.SemaphoreType.DMA((4 * side,)),
            pltpu.SemaphoreType.DMA((3,)),
        ],
        compiler_params=pltpu.CompilerParams(collective_id=collective_id, has_side_effects=True),
    )(h)
    return out.reshape(n * rows, width)


def body(tokens, norm_gain, gate_weight, up_weight, down_weight):
    n_wa = lax.axis_size("wa")
    n_ha = lax.axis_size("ha")
    own_values = tokens.astype(jnp.float32)
    model_width = own_values.shape[1] * n_wa
    own_rows = own_values.shape[0]
    partial_squares = jnp.sum(own_values * own_values, axis=1)
    packed = jnp.pad(partial_squares.reshape(8, own_rows // 8), ((0, 0), (0, 128 - own_rows // 8)))
    squares = exchange(packed, "sum", "wa", n_wa, 0)[:, : own_rows // 8].reshape(own_rows, 1)
    mean_square = squares / model_width
    normed = (own_values * lax.rsqrt(mean_square + 1e-05) * norm_gain[None, :]).astype(jnp.bfloat16)
    gathered = exchange(normed, "gather", "ha", n_ha, 1)
    hidden_width = gate_weight.shape[1]
    summed = ring_reduce_scatter(gathered, gate_weight, up_weight, n_wa, 2)
    gate = summed[:, :hidden_width]
    up = summed[:, hidden_width:]
    hidden = (jax.nn.silu(gate) * up).astype(jnp.bfloat16)
    all_hidden = grid_all_gather(hidden, n_wa, 3)
    partial_out = jnp.dot(all_hidden, down_weight, preferred_element_type=jnp.float32)
    mixed_out = exchange(partial_out.astype(jnp.bfloat16), "scatter", "ha", n_ha, 4)
    return mixed_out.astype(jnp.bfloat16)


def solution(mesh):
    placed = (P("ha", "wa"), P("wa"), P("wa", "ha"), P("wa", "ha"), P("ha", "wa"))
    return jax.shard_map(body, mesh=mesh, in_specs=placed, out_specs=P("ha", "wa"), check_vma=False)
```

```python
import functools

import jax
import jax.numpy as jnp
from jax import lax
from jax.experimental import pallas as pl
from jax.experimental.pallas import tpu as pltpu
from jax.sharding import PartitionSpec as P

MESH = pl.DeviceIdType.MESH


def _greet(axis, n, me):
    barrier = pltpu.get_barrier_semaphore()
    for k in range(1, n):
        pl.semaphore_signal(barrier, inc=1, device_id={axis: lax.rem(me + k, n)}, device_id_type=MESH)
    pl.semaphore_wait(barrier, n - 1)


def _exchange_kernel(mode, axis, n, rows, x_ref, out_ref, slots, send_sem, recv_sem):
    me = lax.axis_index(axis)
    _greet(axis, n, me)
    copies = []
    for k in range(1, n):
        peer = lax.rem(me + k, n)
        if mode == "gather":
            source = x_ref
        elif mode == "scatter":
            source = x_ref.at[pl.ds(pl.multiple_of(peer * rows, rows), rows)]
        else:
            source = x_ref
        copy = pltpu.make_async_remote_copy(
            src_ref=source,
            dst_ref=slots.at[k],
            send_sem=send_sem.at[k],
            recv_sem=recv_sem.at[k],
            device_id={axis: peer},
            device_id_type=MESH,
        )
        copy.start()
        copies.append(copy)
    if mode == "gather":
        out_ref[pl.ds(pl.multiple_of(me * rows, rows), rows), :] = x_ref[...]
        for k, copy in enumerate(copies, 1):
            copy.wait()
            sender = lax.rem(me + n - k, n)
            out_ref[pl.ds(pl.multiple_of(sender * rows, rows), rows), :] = slots[k]
    elif mode == "scatter":
        total = x_ref[pl.ds(pl.multiple_of(me * rows, rows), rows), :].astype(jnp.float32)
        for k, copy in enumerate(copies, 1):
            copy.wait()
            total = total + slots[k].astype(jnp.float32)
        out_ref[...] = total
    else:
        for copy in copies:
            copy.wait()
        slots[0] = x_ref[...]
        total = jnp.zeros(out_ref.shape, jnp.float32)
        for sender in range(n):
            total = total + slots[lax.rem(me + n - sender, n)].astype(jnp.float32)
        out_ref[...] = total


def exchange(x, mode, axis, n, collective_id):
    if n == 1:
        return x.astype(jnp.float32) if mode != "gather" else x
    if mode == "gather":
        rows = x.shape[0]
        out_shape = jax.ShapeDtypeStruct((n * rows, x.shape[1]), x.dtype)
    elif mode == "scatter":
        rows = x.shape[0] // n
        out_shape = jax.ShapeDtypeStruct((rows, x.shape[1]), jnp.float32)
    else:
        rows = x.shape[0]
        out_shape = jax.ShapeDtypeStruct(x.shape, jnp.float32)
    return pl.pallas_call(
        functools.partial(_exchange_kernel, mode, axis, n, rows),
        out_shape=out_shape,
        in_specs=[pl.BlockSpec(memory_space=pltpu.VMEM)],
        out_specs=pl.BlockSpec(memory_space=pltpu.VMEM),
        scratch_shapes=[
            pltpu.VMEM((n, rows, x.shape[1]), x.dtype),
            pltpu.SemaphoreType.DMA((n,)),
            pltpu.SemaphoreType.DMA((n,)),
        ],
        compiler_params=pltpu.CompilerParams(collective_id=collective_id, has_side_effects=True),
    )(x)


def _ring_rs_kernel(side, cols, t_ref, g_hbm, u_hbm, out_ref, wbuf, first_buf, tmp, recv1, acc1, s1,
                    recv2, acc2, send_sem, recv_sem, w_sem):
    w = lax.axis_index("wa")
    x, z = w // side, lax.rem(w, side)
    loads = []
    for f in range(4):
        source = g_hbm if f < 2 else u_hbm
        load = pltpu.make_async_copy(source.at[:, pl.ds((f % 2) * cols, cols)], wbuf.at[f], w_sem.at[f])
        load.start()
        loads.append(load)

    def peer(axis, delta):
        if axis == 0:
            return lax.rem(x + delta + side, side) * side + z
        return x * side + lax.rem(z + delta + side, side)

    barrier = pltpu.get_barrier_semaphore()
    for axis in (0, 1):
        for delta in (1, -1):
            pl.semaphore_signal(barrier, inc=1, device_id={"wa": peer(axis, delta)}, device_id_type=MESH)
    pl.semaphore_wait(barrier, 4)

    flows = []
    for f in range(4):
        first = 0 if f < 2 else 1
        delta = 1 if f % 2 == 0 else -1
        flows.append((first, delta, pl.ds(f * cols, cols)))

    def own1(f, chunk):
        if flows[f][0] == 0:
            rows = t_ref[chunk]
        else:
            rows = t_ref[:, chunk]
        block = rows.reshape(side * rows.shape[1], rows.shape[2])
        product = jnp.dot(block, wbuf[f], preferred_element_type=jnp.float32)
        return product.reshape(side, rows.shape[1], cols)

    def sem(stage, step, f):
        return (stage * 3 + step) * 4 + f

    sends = []
    pos1 = [x if flows[f][0] == 0 else z for f in range(4)]
    pos2 = [z if flows[f][0] == 0 else x for f in range(4)]
    last = [None] * 4
    for step in range(side - 1):
        for f in range(4):
            first, delta, _ = flows[f]
            chunk = lax.rem(pos1[f] - delta * (step + 1) + 2 * side, side)
            if step == 0:
                loads[f].wait()
                first_buf[f] = own1(f, chunk)
                source = first_buf.at[f]
            else:
                tmp[f] = own1(f, chunk)
                last[f].wait_recv()
                acc1[f, step - 1] = recv1[f, step - 1] + tmp[f]
                source = acc1.at[f, step - 1]
            copy = pltpu.make_async_remote_copy(
                src_ref=source, dst_ref=recv1.at[f, step],
                send_sem=send_sem.at[sem(0, step, f)], recv_sem=recv_sem.at[sem(0, step, f)],
                device_id={"wa": peer(first, delta)}, device_id_type=MESH)
            copy.start()
            sends.append(copy)
            last[f] = copy
    for f in range(4):
        tmp[f] = own1(f, pos1[f])
        last[f].wait_recv()
        s1[f] = recv1[f, side - 2] + tmp[f]
    for step in range(side - 1):
        for f in range(4):
            first, delta, _ = flows[f]
            chunk = lax.rem(pos2[f] - delta * (step + 1) + 2 * side, side)
            if step == 0:
                source = s1.at[f, chunk]
            else:
                last[f].wait_recv()
                acc2[f, step - 1] = recv2[f, step - 1] + s1[f, chunk]
                source = acc2.at[f, step - 1]
            copy = pltpu.make_async_remote_copy(
                src_ref=source, dst_ref=recv2.at[f, step],
                send_sem=send_sem.at[sem(1, step, f)], recv_sem=recv_sem.at[sem(1, step, f)],
                device_id={"wa": peer(1 - first, delta)}, device_id_type=MESH)
            copy.start()
            sends.append(copy)
            last[f] = copy
    for f in range(4):
        last[f].wait_recv()
        out_ref[:, flows[f][2]] = recv2[f, side - 2] + s1[f, pos2[f]]
    for copy in sends:
        copy.wait_send()


def ring_reduce_scatter(tokens, gate_weight, up_weight, n, collective_id):
    side = 4
    rows = tokens.shape[0] // n
    depth = tokens.shape[1]
    width = 2 * gate_weight.shape[1]
    cols = width // 4
    t4 = tokens.reshape(side, side, rows, depth)
    f32 = jnp.float32
    return pl.pallas_call(
        functools.partial(_ring_rs_kernel, side, cols),
        out_shape=jax.ShapeDtypeStruct((rows, width), f32),
        in_specs=[pl.BlockSpec(memory_space=pltpu.VMEM), pl.BlockSpec(memory_space=pl.ANY),
                  pl.BlockSpec(memory_space=pl.ANY)],
        out_specs=pl.BlockSpec(memory_space=pltpu.VMEM),
        scratch_shapes=[
            pltpu.VMEM((4, depth, cols), gate_weight.dtype),
            pltpu.VMEM((4, side, rows, cols), f32),
            pltpu.VMEM((4, side, rows, cols), f32),
            pltpu.VMEM((4, side - 1, side, rows, cols), f32),
            pltpu.VMEM((4, side - 2, side, rows, cols), f32),
            pltpu.VMEM((4, side, rows, cols), f32),
            pltpu.VMEM((4, side - 1, rows, cols), f32),
            pltpu.VMEM((4, side - 2, rows, cols), f32),
            pltpu.SemaphoreType.DMA((24,)),
            pltpu.SemaphoreType.DMA((24,)),
            pltpu.SemaphoreType.DMA((4,)),
        ],
        compiler_params=pltpu.CompilerParams(
            collective_id=collective_id, has_side_effects=True, vmem_limit_bytes=63 * 1024 * 1024),
    )(t4, gate_weight, up_weight)


def _grid_ag_kernel(side, cols, h_ref, out_ref, gath, send_sem, recv_sem, local_sem):
    w = lax.axis_index("wa")
    x, z = w // side, lax.rem(w, side)

    def peer(axis, k):
        if axis == 0:
            return lax.rem(x + k, side) * side + z
        return x * side + lax.rem(z + k, side)

    barrier = pltpu.get_barrier_semaphore()
    for axis in (0, 1):
        for k in range(1, side):
            pl.semaphore_signal(barrier, inc=1, device_id={"wa": peer(axis, k)}, device_id_type=MESH)
    pl.semaphore_wait(barrier, 2 * (side - 1))

    halves = [pl.ds(0, cols), pl.ds(cols, cols)]
    locals_ = []
    for f in range(2):
        c = halves[f]
        copy = pltpu.make_async_copy(h_ref.at[:, c], gath.at[x, z, :, c], local_sem.at[f])
        copy.start()
        locals_.append(copy)
    sends = []
    stage2 = []
    stage1 = [[], []]
    for f in range(2):
        c = halves[f]
        for k in range(1, side):
            index = (f * 2 + 0) * side + k
            copy = pltpu.make_async_remote_copy(
                src_ref=h_ref.at[:, c], dst_ref=gath.at[x, z, :, c],
                send_sem=send_sem.at[index], recv_sem=recv_sem.at[index],
                device_id={"wa": peer(f, k)}, device_id_type=MESH)
            copy.start()
            sends.append(copy)
            stage1[f].append(copy)
    for f in range(2):
        c = halves[f]
        locals_[f].wait()
        for copy in stage1[f]:
            copy.wait_recv()
        if f == 0:
            view = gath.at[:, z, :, c]
        else:
            view = gath.at[x, :, :, c]
        for k in range(1, side):
            index = (f * 2 + 1) * side + k
            copy = pltpu.make_async_remote_copy(
                src_ref=view, dst_ref=view,
                send_sem=send_sem.at[index], recv_sem=recv_sem.at[index],
                device_id={"wa": peer(1 - f, k)}, device_id_type=MESH)
            copy.start()
            stage2.append(copy)
    for copy in sends:
        copy.wait_send()
    for copy in stage2:
        copy.wait()
    final = pltpu.make_async_copy(gath, out_ref, local_sem.at[2])
    final.start()
    final.wait()


def grid_all_gather(h, n, collective_id):
    side = 4
    rows, width = h.shape
    cols = width // 2
    out = pl.pallas_call(
        functools.partial(_grid_ag_kernel, side, cols),
        out_shape=jax.ShapeDtypeStruct((side, side, rows, width), h.dtype),
        in_specs=[pl.BlockSpec(memory_space=pltpu.VMEM)],
        out_specs=pl.BlockSpec(memory_space=pltpu.VMEM),
        scratch_shapes=[
            pltpu.VMEM((side, side, rows, width), h.dtype),
            pltpu.SemaphoreType.DMA((4 * side,)),
            pltpu.SemaphoreType.DMA((4 * side,)),
            pltpu.SemaphoreType.DMA((3,)),
        ],
        compiler_params=pltpu.CompilerParams(collective_id=collective_id, has_side_effects=True),
    )(h)
    return out.reshape(n * rows, width)


def _down_rs_kernel(n, rows, h_ref, w_hbm, out_ref, wbuf, sendbuf, slots, send_sem, recv_sem, w_sem):
    me = lax.axis_index("ha")
    load = pltpu.make_async_copy(w_hbm, wbuf, w_sem.at[0])
    load.start()
    _greet("ha", n, me)
    load.wait()
    copies = []
    for k in range(1, n):
        peer = lax.rem(me + k, n)
        block = h_ref[pl.ds(pl.multiple_of(peer * rows, rows), rows), :]
        sendbuf[k] = jnp.dot(block, wbuf[...], preferred_element_type=jnp.float32).astype(sendbuf.dtype)
        copy = pltpu.make_async_remote_copy(
            src_ref=sendbuf.at[k], dst_ref=slots.at[k],
            send_sem=send_sem.at[k], recv_sem=recv_sem.at[k],
            device_id={"ha": peer}, device_id_type=MESH)
        copy.start()
        copies.append(copy)
    block = h_ref[pl.ds(pl.multiple_of(me * rows, rows), rows), :]
    total = jnp.dot(block, wbuf[...], preferred_element_type=jnp.float32)
    for k, copy in enumerate(copies, 1):
        copy.wait()
        total = total + slots[k].astype(jnp.float32)
    out_ref[...] = total


def down_reduce_scatter(hidden, down_weight, n, collective_id):
    rows = hidden.shape[0] // n
    depth, width = down_weight.shape
    return pl.pallas_call(
        functools.partial(_down_rs_kernel, n, rows),
        out_shape=jax.ShapeDtypeStruct((rows, width), jnp.float32),
        in_specs=[pl.BlockSpec(memory_space=pltpu.VMEM), pl.BlockSpec(memory_space=pl.ANY)],
        out_specs=pl.BlockSpec(memory_space=pltpu.VMEM),
        scratch_shapes=[
            pltpu.VMEM((depth, width), down_weight.dtype),
            pltpu.VMEM((n, rows, width), jnp.bfloat16),
            pltpu.VMEM((n, rows, width), jnp.bfloat16),
            pltpu.SemaphoreType.DMA((n,)),
            pltpu.SemaphoreType.DMA((n,)),
            pltpu.SemaphoreType.DMA((1,)),
        ],
        compiler_params=pltpu.CompilerParams(
            collective_id=collective_id, has_side_effects=True, vmem_limit_bytes=48 * 1024 * 1024),
    )(hidden, down_weight)


def body(tokens, norm_gain, gate_weight, up_weight, down_weight):
    n_wa = lax.axis_size("wa")
    n_ha = lax.axis_size("ha")
    own_values = tokens.astype(jnp.float32)
    model_width = own_values.shape[1] * n_wa
    own_rows = own_values.shape[0]
    partial_squares = jnp.sum(own_values * own_values, axis=1)
    packed = jnp.pad(partial_squares.reshape(8, own_rows // 8), ((0, 0), (0, 128 - own_rows // 8)))
    squares = exchange(packed, "sum", "wa", n_wa, 0)[:, : own_rows // 8].reshape(own_rows, 1)
    mean_square = squares / model_width
    normed = (own_values * lax.rsqrt(mean_square + 1e-05) * norm_gain[None, :]).astype(jnp.bfloat16)
    gathered = exchange(normed, "gather", "ha", n_ha, 1)
    hidden_width = gate_weight.shape[1]
    summed = ring_reduce_scatter(gathered, gate_weight, up_weight, n_wa, 2)
    gate = summed[:, :hidden_width]
    up = summed[:, hidden_width:]
    hidden = (jax.nn.silu(gate) * up).astype(jnp.bfloat16)
    all_hidden = grid_all_gather(hidden, n_wa, 3)
    mixed_out = down_reduce_scatter(all_hidden, down_weight, n_ha, 4)
    return mixed_out.astype(jnp.bfloat16)


def solution(mesh):
    placed = (P("ha", "wa"), P("wa"), P("wa", "ha"), P("wa", "ha"), P("ha", "wa"))
    return jax.shard_map(body, mesh=mesh, in_specs=placed, out_specs=P("ha", "wa"), check_vma=False)
```

```python
import functools

import jax
import jax.numpy as jnp
from jax import lax
from jax.experimental import pallas as pl
from jax.experimental.pallas import tpu as pltpu
from jax.sharding import PartitionSpec as P

MESH = pl.DeviceIdType.MESH


def _greet(axis, n, me):
    barrier = pltpu.get_barrier_semaphore()
    for k in range(1, n):
        pl.semaphore_signal(barrier, inc=1, device_id={axis: lax.rem(me + k, n)}, device_id_type=MESH)
    pl.semaphore_wait(barrier, n - 1)


def _exchange_kernel(mode, axis, n, rows, x_ref, out_ref, slots, send_sem, recv_sem):
    me = lax.axis_index(axis)
    _greet(axis, n, me)
    copies = []
    for k in range(1, n):
        peer = lax.rem(me + k, n)
        if mode == "gather":
            source = x_ref
        elif mode == "scatter":
            source = x_ref.at[pl.ds(pl.multiple_of(peer * rows, rows), rows)]
        else:
            source = x_ref
        copy = pltpu.make_async_remote_copy(
            src_ref=source,
            dst_ref=slots.at[k],
            send_sem=send_sem.at[k],
            recv_sem=recv_sem.at[k],
            device_id={axis: peer},
            device_id_type=MESH,
        )
        copy.start()
        copies.append(copy)
    if mode == "gather":
        out_ref[pl.ds(pl.multiple_of(me * rows, rows), rows), :] = x_ref[...]
        for k, copy in enumerate(copies, 1):
            copy.wait()
            sender = lax.rem(me + n - k, n)
            out_ref[pl.ds(pl.multiple_of(sender * rows, rows), rows), :] = slots[k]
    elif mode == "scatter":
        total = x_ref[pl.ds(pl.multiple_of(me * rows, rows), rows), :].astype(jnp.float32)
        for k, copy in enumerate(copies, 1):
            copy.wait()
            total = total + slots[k].astype(jnp.float32)
        out_ref[...] = total
    else:
        for copy in copies:
            copy.wait()
        slots[0] = x_ref[...]
        total = jnp.zeros(out_ref.shape, jnp.float32)
        for sender in range(n):
            total = total + slots[lax.rem(me + n - sender, n)].astype(jnp.float32)
        out_ref[...] = total


def exchange(x, mode, axis, n, collective_id):
    if n == 1:
        return x.astype(jnp.float32) if mode != "gather" else x
    if mode == "gather":
        rows = x.shape[0]
        out_shape = jax.ShapeDtypeStruct((n * rows, x.shape[1]), x.dtype)
    elif mode == "scatter":
        rows = x.shape[0] // n
        out_shape = jax.ShapeDtypeStruct((rows, x.shape[1]), jnp.float32)
    else:
        rows = x.shape[0]
        out_shape = jax.ShapeDtypeStruct(x.shape, jnp.float32)
    return pl.pallas_call(
        functools.partial(_exchange_kernel, mode, axis, n, rows),
        out_shape=out_shape,
        in_specs=[pl.BlockSpec(memory_space=pltpu.VMEM)],
        out_specs=pl.BlockSpec(memory_space=pltpu.VMEM),
        scratch_shapes=[
            pltpu.VMEM((n, rows, x.shape[1]), x.dtype),
            pltpu.SemaphoreType.DMA((n,)),
            pltpu.SemaphoreType.DMA((n,)),
        ],
        compiler_params=pltpu.CompilerParams(collective_id=collective_id, has_side_effects=True),
    )(x)


def _ring_rs_kernel(side, cols, parts, t_ref, g_hbm, u_hbm, out_ref, wbuf, first_buf, tmp, recv1, acc1, s1,
                    recv2, acc2, send_sem, recv_sem, w_sem):
    w = lax.axis_index("wa")
    x, z = w // side, lax.rem(w, side)
    loads = []
    for f in range(4):
        source = g_hbm if f < 2 else u_hbm
        load = pltpu.make_async_copy(source.at[:, pl.ds((f % 2) * cols, cols)], wbuf.at[f], w_sem.at[f])
        load.start()
        loads.append(load)

    def peer(axis, delta):
        if axis == 0:
            return lax.rem(x + delta + side, side) * side + z
        return x * side + lax.rem(z + delta + side, side)

    barrier = pltpu.get_barrier_semaphore()
    for axis in (0, 1):
        for delta in (1, -1):
            pl.semaphore_signal(barrier, inc=1, device_id={"wa": peer(axis, delta)}, device_id_type=MESH)
    pl.semaphore_wait(barrier, 4)

    flows = []
    for f in range(4):
        first = 0 if f < 2 else 1
        delta = 1 if f % 2 == 0 else -1
        flows.append((first, delta, pl.ds(f * cols, cols)))

    def own1(f, chunk):
        if flows[f][0] == 0:
            rows = t_ref[chunk]
        else:
            rows = t_ref[:, chunk]
        block = rows.reshape(side * rows.shape[1], rows.shape[2])
        product = jnp.dot(block, wbuf[f], preferred_element_type=jnp.float32)
        return product.reshape(side, rows.shape[1], cols)

    def sem(stage, step, f, h):
        return ((stage * 3 + step) * 4 + f) * parts + h

    sub = t_ref.shape[2] // parts
    halves = [pl.ds(h * sub, sub) for h in range(parts)]
    sends = []
    pos1 = [x if flows[f][0] == 0 else z for f in range(4)]
    pos2 = [z if flows[f][0] == 0 else x for f in range(4)]
    last = [[None] * parts for _ in range(4)]

    def send(stage, step, f, h, source, target, axis):
        copy = pltpu.make_async_remote_copy(
            src_ref=source, dst_ref=target,
            send_sem=send_sem.at[sem(stage, step, f, h)], recv_sem=recv_sem.at[sem(stage, step, f, h)],
            device_id={"wa": peer(axis, flows[f][1])}, device_id_type=MESH)
        copy.start()
        sends.append(copy)
        last[f][h] = copy

    for step in range(side - 1):
        for f in range(4):
            first, delta, _ = flows[f]
            chunk = lax.rem(pos1[f] - delta * (step + 1) + 2 * side, side)
            if step == 0:
                loads[f].wait()
                first_buf[f] = own1(f, chunk)
                for h, r in enumerate(halves):
                    send(0, step, f, h, first_buf.at[f, :, r], recv1.at[f, step, :, r], first)
            else:
                tmp[f] = own1(f, chunk)
                for h, r in enumerate(halves):
                    last[f][h].wait_recv()
                    acc1[f, step - 1, :, r] = recv1[f, step - 1, :, r] + tmp[f, :, r]
                    send(0, step, f, h, acc1.at[f, step - 1, :, r], recv1.at[f, step, :, r], first)
    for f in range(4):
        first, delta, _ = flows[f]
        tmp[f] = own1(f, pos1[f])
        chunk = lax.rem(pos2[f] - delta + 2 * side, side)
        for h, r in enumerate(halves):
            last[f][h].wait_recv()
            s1[f, :, r] = recv1[f, side - 2, :, r] + tmp[f, :, r]
            send(1, 0, f, h, s1.at[f, chunk, r], recv2.at[f, 0, r], 1 - first)
    for step in range(1, side - 1):
        for f in range(4):
            first, delta, _ = flows[f]
            chunk = lax.rem(pos2[f] - delta * (step + 1) + 2 * side, side)
            for h, r in enumerate(halves):
                last[f][h].wait_recv()
                acc2[f, step - 1, r] = recv2[f, step - 1, r] + s1[f, chunk, r]
                send(1, step, f, h, acc2.at[f, step - 1, r], recv2.at[f, step, r], 1 - first)
    for f in range(4):
        for h, r in enumerate(halves):
            last[f][h].wait_recv()
            out_ref[r, flows[f][2]] = recv2[f, side - 2, r] + s1[f, pos2[f], r]
    for copy in sends:
        copy.wait_send()


def ring_reduce_scatter(tokens, gate_weight, up_weight, n, collective_id):
    side = 4
    rows = tokens.shape[0] // n
    depth = tokens.shape[1]
    width = 2 * gate_weight.shape[1]
    cols = width // 4
    t4 = tokens.reshape(side, side, rows, depth)
    f32 = jnp.float32
    return pl.pallas_call(
        functools.partial(_ring_rs_kernel, side, cols, 2),
        out_shape=jax.ShapeDtypeStruct((rows, width), f32),
        in_specs=[pl.BlockSpec(memory_space=pltpu.VMEM), pl.BlockSpec(memory_space=pl.ANY),
                  pl.BlockSpec(memory_space=pl.ANY)],
        out_specs=pl.BlockSpec(memory_space=pltpu.VMEM),
        scratch_shapes=[
            pltpu.VMEM((4, depth, cols), gate_weight.dtype),
            pltpu.VMEM((4, side, rows, cols), f32),
            pltpu.VMEM((4, side, rows, cols), f32),
            pltpu.VMEM((4, side - 1, side, rows, cols), f32),
            pltpu.VMEM((4, side - 2, side, rows, cols), f32),
            pltpu.VMEM((4, side, rows, cols), f32),
            pltpu.VMEM((4, side - 1, rows, cols), f32),
            pltpu.VMEM((4, side - 2, rows, cols), f32),
            pltpu.SemaphoreType.DMA((48,)),
            pltpu.SemaphoreType.DMA((48,)),
            pltpu.SemaphoreType.DMA((4,)),
        ],
        compiler_params=pltpu.CompilerParams(
            collective_id=collective_id, has_side_effects=True, vmem_limit_bytes=63 * 1024 * 1024),
    )(t4, gate_weight, up_weight)


def _grid_ag_kernel(side, cols, h_ref, out_ref, gath, send_sem, recv_sem, local_sem):
    w = lax.axis_index("wa")
    x, z = w // side, lax.rem(w, side)

    def peer(axis, k):
        if axis == 0:
            return lax.rem(x + k, side) * side + z
        return x * side + lax.rem(z + k, side)

    barrier = pltpu.get_barrier_semaphore()
    for axis in (0, 1):
        for k in range(1, side):
            pl.semaphore_signal(barrier, inc=1, device_id={"wa": peer(axis, k)}, device_id_type=MESH)
    pl.semaphore_wait(barrier, 2 * (side - 1))

    halves = [pl.ds(0, cols), pl.ds(cols, cols)]
    locals_ = []
    for f in range(2):
        c = halves[f]
        copy = pltpu.make_async_copy(h_ref.at[:, c], gath.at[x, z, :, c], local_sem.at[f])
        copy.start()
        locals_.append(copy)
    sends = []
    stage2 = []
    stage1 = [[], []]
    for f in range(2):
        c = halves[f]
        for k in range(1, side):
            index = (f * 2 + 0) * side + k
            copy = pltpu.make_async_remote_copy(
                src_ref=h_ref.at[:, c], dst_ref=gath.at[x, z, :, c],
                send_sem=send_sem.at[index], recv_sem=recv_sem.at[index],
                device_id={"wa": peer(f, k)}, device_id_type=MESH)
            copy.start()
            sends.append(copy)
            stage1[f].append(copy)
    for f in range(2):
        c = halves[f]
        locals_[f].wait()
        for copy in stage1[f]:
            copy.wait_recv()
        if f == 0:
            view = gath.at[:, z, :, c]
        else:
            view = gath.at[x, :, :, c]
        for k in range(1, side):
            index = (f * 2 + 1) * side + k
            copy = pltpu.make_async_remote_copy(
                src_ref=view, dst_ref=view,
                send_sem=send_sem.at[index], recv_sem=recv_sem.at[index],
                device_id={"wa": peer(1 - f, k)}, device_id_type=MESH)
            copy.start()
            stage2.append(copy)
    for copy in sends:
        copy.wait_send()
    for copy in stage2:
        copy.wait()
    final = pltpu.make_async_copy(gath, out_ref, local_sem.at[2])
    final.start()
    final.wait()


def grid_all_gather(h, n, collective_id):
    side = 4
    rows, width = h.shape
    cols = width // 2
    out = pl.pallas_call(
        functools.partial(_grid_ag_kernel, side, cols),
        out_shape=jax.ShapeDtypeStruct((side, side, rows, width), h.dtype),
        in_specs=[pl.BlockSpec(memory_space=pltpu.VMEM)],
        out_specs=pl.BlockSpec(memory_space=pltpu.VMEM),
        scratch_shapes=[
            pltpu.VMEM((side, side, rows, width), h.dtype),
            pltpu.SemaphoreType.DMA((4 * side,)),
            pltpu.SemaphoreType.DMA((4 * side,)),
            pltpu.SemaphoreType.DMA((3,)),
        ],
        compiler_params=pltpu.CompilerParams(collective_id=collective_id, has_side_effects=True),
    )(h)
    return out.reshape(n * rows, width)


def _down_rs_kernel(n, rows, h_ref, w_hbm, out_ref, wbuf, sendbuf, slots, send_sem, recv_sem, w_sem):
    me = lax.axis_index("ha")
    load = pltpu.make_async_copy(w_hbm, wbuf, w_sem.at[0])
    load.start()
    _greet("ha", n, me)
    load.wait()
    copies = []
    for k in range(1, n):
        peer = lax.rem(me + k, n)
        block = h_ref[pl.ds(pl.multiple_of(peer * rows, rows), rows), :]
        sendbuf[k] = jnp.dot(block, wbuf[...], preferred_element_type=jnp.float32).astype(sendbuf.dtype)
        copy = pltpu.make_async_remote_copy(
            src_ref=sendbuf.at[k], dst_ref=slots.at[k],
            send_sem=send_sem.at[k], recv_sem=recv_sem.at[k],
            device_id={"ha": peer}, device_id_type=MESH)
        copy.start()
        copies.append(copy)
    block = h_ref[pl.ds(pl.multiple_of(me * rows, rows), rows), :]
    total = jnp.dot(block, wbuf[...], preferred_element_type=jnp.float32)
    for k, copy in enumerate(copies, 1):
        copy.wait()
        total = total + slots[k].astype(jnp.float32)
    out_ref[...] = total


def down_reduce_scatter(hidden, down_weight, n, collective_id):
    rows = hidden.shape[0] // n
    depth, width = down_weight.shape
    return pl.pallas_call(
        functools.partial(_down_rs_kernel, n, rows),
        out_shape=jax.ShapeDtypeStruct((rows, width), jnp.float32),
        in_specs=[pl.BlockSpec(memory_space=pltpu.VMEM), pl.BlockSpec(memory_space=pl.ANY)],
        out_specs=pl.BlockSpec(memory_space=pltpu.VMEM),
        scratch_shapes=[
            pltpu.VMEM((depth, width), down_weight.dtype),
            pltpu.VMEM((n, rows, width), jnp.bfloat16),
            pltpu.VMEM((n, rows, width), jnp.bfloat16),
            pltpu.SemaphoreType.DMA((n,)),
            pltpu.SemaphoreType.DMA((n,)),
            pltpu.SemaphoreType.DMA((1,)),
        ],
        compiler_params=pltpu.CompilerParams(
            collective_id=collective_id, has_side_effects=True, vmem_limit_bytes=48 * 1024 * 1024),
    )(hidden, down_weight)


def body(tokens, norm_gain, gate_weight, up_weight, down_weight):
    n_wa = lax.axis_size("wa")
    n_ha = lax.axis_size("ha")
    own_values = tokens.astype(jnp.float32)
    model_width = own_values.shape[1] * n_wa
    own_rows = own_values.shape[0]
    partial_squares = jnp.sum(own_values * own_values, axis=1)
    packed = jnp.pad(partial_squares.reshape(8, own_rows // 8), ((0, 0), (0, 128 - own_rows // 8)))
    squares = exchange(packed, "sum", "wa", n_wa, 0)[:, : own_rows // 8].reshape(own_rows, 1)
    mean_square = squares / model_width
    normed = (own_values * lax.rsqrt(mean_square + 1e-05) * norm_gain[None, :]).astype(jnp.bfloat16)
    gathered = exchange(normed, "gather", "ha", n_ha, 1)
    hidden_width = gate_weight.shape[1]
    summed = ring_reduce_scatter(gathered, gate_weight, up_weight, n_wa, 2)
    gate = summed[:, :hidden_width]
    up = summed[:, hidden_width:]
    hidden = (jax.nn.silu(gate) * up).astype(jnp.bfloat16)
    all_hidden = grid_all_gather(hidden, n_wa, 3)
    mixed_out = down_reduce_scatter(all_hidden, down_weight, n_ha, 4)
    return mixed_out.astype(jnp.bfloat16)


def solution(mesh):
    placed = (P("ha", "wa"), P("wa"), P("wa", "ha"), P("wa", "ha"), P("ha", "wa"))
    return jax.shard_map(body, mesh=mesh, in_specs=placed, out_specs=P("ha", "wa"), check_vma=False)
```

```python
import functools

import jax
import jax.numpy as jnp
from jax import lax
from jax.experimental import pallas as pl
from jax.experimental.pallas import tpu as pltpu
from jax.sharding import PartitionSpec as P

MESH = pl.DeviceIdType.MESH


def _greet(axis, n, me):
    barrier = pltpu.get_barrier_semaphore()
    for k in range(1, n):
        pl.semaphore_signal(barrier, inc=1, device_id={axis: lax.rem(me + k, n)}, device_id_type=MESH)
    pl.semaphore_wait(barrier, n - 1)


def _exchange_kernel(mode, axis, n, rows, x_ref, out_ref, slots, send_sem, recv_sem):
    me = lax.axis_index(axis)
    _greet(axis, n, me)
    copies = []
    for k in range(1, n):
        peer = lax.rem(me + k, n)
        if mode == "gather":
            source = x_ref
        elif mode == "scatter":
            source = x_ref.at[pl.ds(pl.multiple_of(peer * rows, rows), rows)]
        else:
            source = x_ref
        copy = pltpu.make_async_remote_copy(
            src_ref=source,
            dst_ref=slots.at[k],
            send_sem=send_sem.at[k],
            recv_sem=recv_sem.at[k],
            device_id={axis: peer},
            device_id_type=MESH,
        )
        copy.start()
        copies.append(copy)
    if mode == "gather":
        out_ref[pl.ds(pl.multiple_of(me * rows, rows), rows), :] = x_ref[...]
        for k, copy in enumerate(copies, 1):
            copy.wait()
            sender = lax.rem(me + n - k, n)
            out_ref[pl.ds(pl.multiple_of(sender * rows, rows), rows), :] = slots[k]
    elif mode == "scatter":
        total = x_ref[pl.ds(pl.multiple_of(me * rows, rows), rows), :].astype(jnp.float32)
        for k, copy in enumerate(copies, 1):
            copy.wait()
            total = total + slots[k].astype(jnp.float32)
        out_ref[...] = total
    else:
        for copy in copies:
            copy.wait()
        slots[0] = x_ref[...]
        total = jnp.zeros(out_ref.shape, jnp.float32)
        for sender in range(n):
            total = total + slots[lax.rem(me + n - sender, n)].astype(jnp.float32)
        out_ref[...] = total


def exchange(x, mode, axis, n, collective_id):
    if n == 1:
        return x.astype(jnp.float32) if mode != "gather" else x
    if mode == "gather":
        rows = x.shape[0]
        out_shape = jax.ShapeDtypeStruct((n * rows, x.shape[1]), x.dtype)
    elif mode == "scatter":
        rows = x.shape[0] // n
        out_shape = jax.ShapeDtypeStruct((rows, x.shape[1]), jnp.float32)
    else:
        rows = x.shape[0]
        out_shape = jax.ShapeDtypeStruct(x.shape, jnp.float32)
    return pl.pallas_call(
        functools.partial(_exchange_kernel, mode, axis, n, rows),
        out_shape=out_shape,
        in_specs=[pl.BlockSpec(memory_space=pltpu.VMEM)],
        out_specs=pl.BlockSpec(memory_space=pltpu.VMEM),
        scratch_shapes=[
            pltpu.VMEM((n, rows, x.shape[1]), x.dtype),
            pltpu.SemaphoreType.DMA((n,)),
            pltpu.SemaphoreType.DMA((n,)),
        ],
        compiler_params=pltpu.CompilerParams(collective_id=collective_id, has_side_effects=True),
    )(x)


def _ring_rs_kernel(side, cols, parts, t_ref, g_hbm, u_hbm, out_ref, wbuf, first_buf, tmp, recv1, acc1, s1,
                    recv2, acc2, send_sem, recv_sem, w_sem):
    w = lax.axis_index("wa")
    x, z = w // side, lax.rem(w, side)
    loads = []
    for f in range(4):
        source = g_hbm if f < 2 else u_hbm
        load = pltpu.make_async_copy(source.at[:, pl.ds((f % 2) * cols, cols)], wbuf.at[f], w_sem.at[f])
        load.start()
        loads.append(load)

    def peer(axis, delta):
        if axis == 0:
            return lax.rem(x + delta + side, side) * side + z
        return x * side + lax.rem(z + delta + side, side)

    barrier = pltpu.get_barrier_semaphore()
    for axis in (0, 1):
        for delta in (1, -1):
            pl.semaphore_signal(barrier, inc=1, device_id={"wa": peer(axis, delta)}, device_id_type=MESH)
    pl.semaphore_wait(barrier, 4)

    flows = []
    for f in range(4):
        first = 0 if f < 2 else 1
        delta = 1 if f % 2 == 0 else -1
        flows.append((first, delta, pl.ds(f * cols, cols)))

    def own1(f, chunk):
        if flows[f][0] == 0:
            rows = t_ref[chunk]
        else:
            rows = t_ref[:, chunk]
        block = rows.reshape(side * rows.shape[1], rows.shape[2])
        product = jnp.dot(block, wbuf[f], preferred_element_type=jnp.float32)
        return product.reshape(side, rows.shape[1], cols)

    def sem(stage, step, f, h):
        return ((stage * 3 + step) * 4 + f) * parts + h

    sub = t_ref.shape[2] // parts
    halves = [pl.ds(h * sub, sub) for h in range(parts)]
    sends = []
    pos1 = [x if flows[f][0] == 0 else z for f in range(4)]
    pos2 = [z if flows[f][0] == 0 else x for f in range(4)]
    last = [[None] * parts for _ in range(4)]

    def send(stage, step, f, h, source, target, axis):
        copy = pltpu.make_async_remote_copy(
            src_ref=source, dst_ref=target,
            send_sem=send_sem.at[sem(stage, step, f, h)], recv_sem=recv_sem.at[sem(stage, step, f, h)],
            device_id={"wa": peer(axis, flows[f][1])}, device_id_type=MESH)
        copy.start()
        sends.append(copy)
        last[f][h] = copy

    for step in range(side - 1):
        for f in range(4):
            first, delta, _ = flows[f]
            chunk = lax.rem(pos1[f] - delta * (step + 1) + 2 * side, side)
            if step == 0:
                loads[f].wait()
                first_buf[f] = own1(f, chunk)
                for h, r in enumerate(halves):
                    send(0, step, f, h, first_buf.at[f, :, r], recv1.at[f, step, :, r], first)
            else:
                tmp[f] = own1(f, chunk)
                for h, r in enumerate(halves):
                    last[f][h].wait_recv()
                    acc1[f, step - 1, :, r] = recv1[f, step - 1, :, r] + tmp[f, :, r]
                    send(0, step, f, h, acc1.at[f, step - 1, :, r], recv1.at[f, step, :, r], first)
    for f in range(4):
        first, delta, _ = flows[f]
        tmp[f] = own1(f, pos1[f])
        chunk = lax.rem(pos2[f] - delta + 2 * side, side)
        for h, r in enumerate(halves):
            last[f][h].wait_recv()
            s1[f, :, r] = recv1[f, side - 2, :, r] + tmp[f, :, r]
            send(1, 0, f, h, s1.at[f, chunk, r], recv2.at[f, 0, r], 1 - first)
    for step in range(1, side - 1):
        for f in range(4):
            first, delta, _ = flows[f]
            chunk = lax.rem(pos2[f] - delta * (step + 1) + 2 * side, side)
            for h, r in enumerate(halves):
                last[f][h].wait_recv()
                acc2[f, step - 1, r] = recv2[f, step - 1, r] + s1[f, chunk, r]
                send(1, step, f, h, acc2.at[f, step - 1, r], recv2.at[f, step, r], 1 - first)
    for f in range(4):
        for h, r in enumerate(halves):
            last[f][h].wait_recv()
            out_ref[r, flows[f][2]] = recv2[f, side - 2, r] + s1[f, pos2[f], r]
    for copy in sends:
        copy.wait_send()


def ring_reduce_scatter(tokens, gate_weight, up_weight, n, collective_id):
    side = 4
    rows = tokens.shape[0] // n
    depth = tokens.shape[1]
    width = 2 * gate_weight.shape[1]
    cols = width // 4
    t4 = tokens.reshape(side, side, rows, depth)
    f32 = jnp.float32
    return pl.pallas_call(
        functools.partial(_ring_rs_kernel, side, cols, 2),
        out_shape=jax.ShapeDtypeStruct((rows, width), f32),
        in_specs=[pl.BlockSpec(memory_space=pltpu.VMEM), pl.BlockSpec(memory_space=pl.ANY),
                  pl.BlockSpec(memory_space=pl.ANY)],
        out_specs=pl.BlockSpec(memory_space=pltpu.VMEM),
        scratch_shapes=[
            pltpu.VMEM((4, depth, cols), gate_weight.dtype),
            pltpu.VMEM((4, side, rows, cols), f32),
            pltpu.VMEM((4, side, rows, cols), f32),
            pltpu.VMEM((4, side - 1, side, rows, cols), f32),
            pltpu.VMEM((4, side - 2, side, rows, cols), f32),
            pltpu.VMEM((4, side, rows, cols), f32),
            pltpu.VMEM((4, side - 1, rows, cols), f32),
            pltpu.VMEM((4, side - 2, rows, cols), f32),
            pltpu.SemaphoreType.DMA((48,)),
            pltpu.SemaphoreType.DMA((48,)),
            pltpu.SemaphoreType.DMA((4,)),
        ],
        compiler_params=pltpu.CompilerParams(
            collective_id=collective_id, has_side_effects=True, vmem_limit_bytes=63 * 1024 * 1024),
    )(t4, gate_weight, up_weight)


def _grid_ag_kernel(side, cols, h_ref, out_ref, gath, send_sem, recv_sem, local_sem):
    w = lax.axis_index("wa")
    x, z = w // side, lax.rem(w, side)

    def peer(axis, delta):
        if axis == 0:
            return lax.rem(x + delta + side, side) * side + z
        return x * side + lax.rem(z + delta + side, side)

    barrier = pltpu.get_barrier_semaphore()
    for axis in (0, 1):
        for delta in (1, -1):
            pl.semaphore_signal(barrier, inc=1, device_id={"wa": peer(axis, delta)}, device_id_type=MESH)
    pl.semaphore_wait(barrier, 4)

    halves = [pl.ds(0, cols), pl.ds(cols, cols)]
    rows = h_ref.shape[0]
    locals_ = []
    for f in range(2):
        c = halves[f]
        copy = pltpu.make_async_copy(h_ref.at[:, c], gath.at[x, z, :, c], local_sem.at[f])
        copy.start()
        locals_.append(copy)

    def piece(f, stage, at, part=None):
        c = halves[f]
        along_x = (f == 0) == (stage == 0)
        if stage == 0:
            span = slice(None) if part is None else pl.ds(part * (rows // 2), rows // 2)
            if along_x:
                return gath.at[at, z, span, c]
            return gath.at[x, at, span, c]
        span = slice(None) if part is None else pl.ds(part * (side // 2), side // 2)
        if along_x:
            return gath.at[at, span, :, c]
        return gath.at[span, at, :, c]

    sends = []
    for stage in range(2):
        first, geometry = {}, {}
        for f in range(2):
            along_x = (f == 0) == (stage == 0)
            axis = 0 if along_x else 1
            pos = x if along_x else z
            base = (f * 2 + stage) * 4
            geometry[f] = (axis, pos, base)
            if stage == 0:
                locals_[f].wait()
            own = piece(f, stage, pos)
            first[f] = []
            for j, delta in enumerate((1, -1)):
                copy = pltpu.make_async_remote_copy(
                    src_ref=own, dst_ref=own,
                    send_sem=send_sem.at[base + j], recv_sem=recv_sem.at[base + j],
                    device_id={"wa": peer(axis, delta)}, device_id_type=MESH)
                copy.start()
                first[f].append(copy)
                sends.append(copy)
        second = []
        for f in range(2):
            axis, pos, base = geometry[f]
            for j, delta in enumerate((1, -1)):
                first[f][j].wait_recv()
                origin = lax.rem(pos - delta + side, side)
                part = piece(f, stage, origin, j)
                copy = pltpu.make_async_remote_copy(
                    src_ref=part, dst_ref=part,
                    send_sem=send_sem.at[base + 2 + j], recv_sem=recv_sem.at[base + 2 + j],
                    device_id={"wa": peer(axis, delta)}, device_id_type=MESH)
                copy.start()
                second.append(copy)
                sends.append(copy)
        for copy in second:
            copy.wait_recv()
    for copy in sends:
        copy.wait_send()
    final = pltpu.make_async_copy(gath, out_ref, local_sem.at[2])
    final.start()
    final.wait()


def grid_all_gather(h, n, collective_id):
    side = 4
    rows, width = h.shape
    cols = width // 2
    out = pl.pallas_call(
        functools.partial(_grid_ag_kernel, side, cols),
        out_shape=jax.ShapeDtypeStruct((side, side, rows, width), h.dtype),
        in_specs=[pl.BlockSpec(memory_space=pltpu.VMEM)],
        out_specs=pl.BlockSpec(memory_space=pltpu.VMEM),
        scratch_shapes=[
            pltpu.VMEM((side, side, rows, width), h.dtype),
            pltpu.SemaphoreType.DMA((4 * side,)),
            pltpu.SemaphoreType.DMA((4 * side,)),
            pltpu.SemaphoreType.DMA((3,)),
        ],
        compiler_params=pltpu.CompilerParams(collective_id=collective_id, has_side_effects=True),
    )(h)
    return out.reshape(n * rows, width)


def _down_rs_kernel(n, rows, h_ref, w_hbm, out_ref, wbuf, sendbuf, slots, send_sem, recv_sem, w_sem):
    me = lax.axis_index("ha")
    load = pltpu.make_async_copy(w_hbm, wbuf, w_sem.at[0])
    load.start()
    _greet("ha", n, me)
    load.wait()
    copies = []
    for k in range(1, n):
        peer = lax.rem(me + k, n)
        block = h_ref[pl.ds(pl.multiple_of(peer * rows, rows), rows), :]
        sendbuf[k] = jnp.dot(block, wbuf[...], preferred_element_type=jnp.float32).astype(sendbuf.dtype)
        copy = pltpu.make_async_remote_copy(
            src_ref=sendbuf.at[k], dst_ref=slots.at[k],
            send_sem=send_sem.at[k], recv_sem=recv_sem.at[k],
            device_id={"ha": peer}, device_id_type=MESH)
        copy.start()
        copies.append(copy)
    block = h_ref[pl.ds(pl.multiple_of(me * rows, rows), rows), :]
    total = jnp.dot(block, wbuf[...], preferred_element_type=jnp.float32)
    for k, copy in enumerate(copies, 1):
        copy.wait()
        total = total + slots[k].astype(jnp.float32)
    out_ref[...] = total


def down_reduce_scatter(hidden, down_weight, n, collective_id):
    rows = hidden.shape[0] // n
    depth, width = down_weight.shape
    return pl.pallas_call(
        functools.partial(_down_rs_kernel, n, rows),
        out_shape=jax.ShapeDtypeStruct((rows, width), jnp.float32),
        in_specs=[pl.BlockSpec(memory_space=pltpu.VMEM), pl.BlockSpec(memory_space=pl.ANY)],
        out_specs=pl.BlockSpec(memory_space=pltpu.VMEM),
        scratch_shapes=[
            pltpu.VMEM((depth, width), down_weight.dtype),
            pltpu.VMEM((n, rows, width), jnp.bfloat16),
            pltpu.VMEM((n, rows, width), jnp.bfloat16),
            pltpu.SemaphoreType.DMA((n,)),
            pltpu.SemaphoreType.DMA((n,)),
            pltpu.SemaphoreType.DMA((1,)),
        ],
        compiler_params=pltpu.CompilerParams(
            collective_id=collective_id, has_side_effects=True, vmem_limit_bytes=48 * 1024 * 1024),
    )(hidden, down_weight)


def body(tokens, norm_gain, gate_weight, up_weight, down_weight):
    n_wa = lax.axis_size("wa")
    n_ha = lax.axis_size("ha")
    own_values = tokens.astype(jnp.float32)
    model_width = own_values.shape[1] * n_wa
    own_rows = own_values.shape[0]
    partial_squares = jnp.sum(own_values * own_values, axis=1)
    packed = jnp.pad(partial_squares.reshape(8, own_rows // 8), ((0, 0), (0, 128 - own_rows // 8)))
    squares = exchange(packed, "sum", "wa", n_wa, 0)[:, : own_rows // 8].reshape(own_rows, 1)
    mean_square = squares / model_width
    normed = (own_values * lax.rsqrt(mean_square + 1e-05) * norm_gain[None, :]).astype(jnp.bfloat16)
    gathered = exchange(normed, "gather", "ha", n_ha, 1)
    hidden_width = gate_weight.shape[1]
    summed = ring_reduce_scatter(gathered, gate_weight, up_weight, n_wa, 2)
    gate = summed[:, :hidden_width]
    up = summed[:, hidden_width:]
    hidden = (jax.nn.silu(gate) * up).astype(jnp.bfloat16)
    all_hidden = grid_all_gather(hidden, n_wa, 3)
    mixed_out = down_reduce_scatter(all_hidden, down_weight, n_ha, 4)
    return mixed_out.astype(jnp.bfloat16)


def solution(mesh):
    placed = (P("ha", "wa"), P("wa"), P("wa", "ha"), P("wa", "ha"), P("ha", "wa"))
    return jax.shard_map(body, mesh=mesh, in_specs=placed, out_specs=P("ha", "wa"), check_vma=False)
```

```python
import functools

import jax
import jax.numpy as jnp
from jax import lax
from jax.experimental import pallas as pl
from jax.experimental.pallas import tpu as pltpu
from jax.sharding import PartitionSpec as P

MESH = pl.DeviceIdType.MESH


def _greet(axis, n, me):
    barrier = pltpu.get_barrier_semaphore()
    for k in range(1, n):
        pl.semaphore_signal(barrier, inc=1, device_id={axis: lax.rem(me + k, n)}, device_id_type=MESH)
    pl.semaphore_wait(barrier, n - 1)


def _exchange_kernel(mode, axis, n, rows, x_ref, out_ref, slots, send_sem, recv_sem):
    me = lax.axis_index(axis)
    _greet(axis, n, me)
    copies = []
    for k in range(1, n):
        peer = lax.rem(me + k, n)
        if mode == "gather":
            source = x_ref
        elif mode == "scatter":
            source = x_ref.at[pl.ds(pl.multiple_of(peer * rows, rows), rows)]
        else:
            source = x_ref
        copy = pltpu.make_async_remote_copy(
            src_ref=source,
            dst_ref=slots.at[k],
            send_sem=send_sem.at[k],
            recv_sem=recv_sem.at[k],
            device_id={axis: peer},
            device_id_type=MESH,
        )
        copy.start()
        copies.append(copy)
    if mode == "gather":
        out_ref[pl.ds(pl.multiple_of(me * rows, rows), rows), :] = x_ref[...]
        for k, copy in enumerate(copies, 1):
            copy.wait()
            sender = lax.rem(me + n - k, n)
            out_ref[pl.ds(pl.multiple_of(sender * rows, rows), rows), :] = slots[k]
    elif mode == "scatter":
        total = x_ref[pl.ds(pl.multiple_of(me * rows, rows), rows), :].astype(jnp.float32)
        for k, copy in enumerate(copies, 1):
            copy.wait()
            total = total + slots[k].astype(jnp.float32)
        out_ref[...] = total
    else:
        for copy in copies:
            copy.wait()
        slots[0] = x_ref[...]
        total = jnp.zeros(out_ref.shape, jnp.float32)
        for sender in range(n):
            total = total + slots[lax.rem(me + n - sender, n)].astype(jnp.float32)
        out_ref[...] = total


def exchange(x, mode, axis, n, collective_id):
    if n == 1:
        return x.astype(jnp.float32) if mode != "gather" else x
    if mode == "gather":
        rows = x.shape[0]
        out_shape = jax.ShapeDtypeStruct((n * rows, x.shape[1]), x.dtype)
    elif mode == "scatter":
        rows = x.shape[0] // n
        out_shape = jax.ShapeDtypeStruct((rows, x.shape[1]), jnp.float32)
    else:
        rows = x.shape[0]
        out_shape = jax.ShapeDtypeStruct(x.shape, jnp.float32)
    return pl.pallas_call(
        functools.partial(_exchange_kernel, mode, axis, n, rows),
        out_shape=out_shape,
        in_specs=[pl.BlockSpec(memory_space=pltpu.VMEM)],
        out_specs=pl.BlockSpec(memory_space=pltpu.VMEM),
        scratch_shapes=[
            pltpu.VMEM((n, rows, x.shape[1]), x.dtype),
            pltpu.SemaphoreType.DMA((n,)),
            pltpu.SemaphoreType.DMA((n,)),
        ],
        compiler_params=pltpu.CompilerParams(collective_id=collective_id, has_side_effects=True),
    )(x)


def _ring_rs_kernel(side, cols, parts, t_ref, g_hbm, u_hbm, out_ref, wbuf, first_buf, recv_b, tmp, recv1,
                    acc1, s1, recv2, acc2, send_sem, recv_sem, w_sem):
    w = lax.axis_index("wa")
    x, z = w // side, lax.rem(w, side)
    loads = []
    for f in range(4):
        source = g_hbm if f < 2 else u_hbm
        load = pltpu.make_async_copy(source.at[:, pl.ds((f % 2) * cols, cols)], wbuf.at[f], w_sem.at[f])
        load.start()
        loads.append(load)

    def peer(axis, delta):
        if axis == 0:
            return lax.rem(x + delta + side, side) * side + z
        return x * side + lax.rem(z + delta + side, side)

    barrier = pltpu.get_barrier_semaphore()
    for axis in (0, 1):
        for delta in (1, -1):
            pl.semaphore_signal(barrier, inc=1, device_id={"wa": peer(axis, delta)}, device_id_type=MESH)
    pl.semaphore_wait(barrier, 4)

    flows = []
    for f in range(4):
        first = 0 if f < 2 else 1
        delta = 1 if f % 2 == 0 else -1
        flows.append((first, delta, pl.ds(f * cols, cols)))

    def own1(f, chunk):
        if flows[f][0] == 0:
            rows = t_ref[chunk]
        else:
            rows = t_ref[:, chunk]
        block = rows.reshape(side * rows.shape[1], rows.shape[2])
        product = jnp.dot(block, wbuf[f], preferred_element_type=jnp.float32)
        return product.reshape(side, rows.shape[1], cols)

    def sem(stage, step, f, h):
        return ((stage * 3 + step) * 4 + f) * parts + h

    sub = t_ref.shape[2] // parts
    halves = [pl.ds(h * sub, sub) for h in range(parts)]
    sends = []
    pos1 = [x if flows[f][0] == 0 else z for f in range(4)]
    pos2 = [z if flows[f][0] == 0 else x for f in range(4)]
    last = [[None] * parts for _ in range(4)]

    def send(stage, step, f, h, source, target, axis):
        copy = pltpu.make_async_remote_copy(
            src_ref=source, dst_ref=target,
            send_sem=send_sem.at[sem(stage, step, f, h)], recv_sem=recv_sem.at[sem(stage, step, f, h)],
            device_id={"wa": peer(axis, flows[f][1])}, device_id_type=MESH)
        copy.start()
        sends.append(copy)
        last[f][h] = copy

    for step in range(side - 1):
        for f in range(4):
            first, delta, _ = flows[f]
            chunk = lax.rem(pos1[f] - delta * (step + 1) + 2 * side, side)
            if step == 0:
                loads[f].wait()
                first_buf[f] = own1(f, chunk).astype(first_buf.dtype)
                for h, r in enumerate(halves):
                    send(0, step, f, h, first_buf.at[f, :, r], recv_b.at[f, :, r], first)
            else:
                tmp[f] = own1(f, chunk)
                for h, r in enumerate(halves):
                    last[f][h].wait_recv()
                    if step == 1:
                        arrived = recv_b[f, :, r].astype(jnp.float32)
                    else:
                        arrived = recv1[f, step - 1, :, r]
                    acc1[f, step - 1, :, r] = arrived + tmp[f, :, r]
                    send(0, step, f, h, acc1.at[f, step - 1, :, r], recv1.at[f, step, :, r], first)
    for f in range(4):
        first, delta, _ = flows[f]
        tmp[f] = own1(f, pos1[f])
        chunk = lax.rem(pos2[f] - delta + 2 * side, side)
        for h, r in enumerate(halves):
            last[f][h].wait_recv()
            s1[f, :, r] = recv1[f, side - 2, :, r] + tmp[f, :, r]
            send(1, 0, f, h, s1.at[f, chunk, r], recv2.at[f, 0, r], 1 - first)
    for step in range(1, side - 1):
        for f in range(4):
            first, delta, _ = flows[f]
            chunk = lax.rem(pos2[f] - delta * (step + 1) + 2 * side, side)
            for h, r in enumerate(halves):
                last[f][h].wait_recv()
                acc2[f, step - 1, r] = recv2[f, step - 1, r] + s1[f, chunk, r]
                send(1, step, f, h, acc2.at[f, step - 1, r], recv2.at[f, step, r], 1 - first)
    for f in range(4):
        for h, r in enumerate(halves):
            last[f][h].wait_recv()
            out_ref[r, flows[f][2]] = recv2[f, side - 2, r] + s1[f, pos2[f], r]
    for copy in sends:
        copy.wait_send()


def ring_reduce_scatter(tokens, gate_weight, up_weight, n, collective_id):
    side = 4
    rows = tokens.shape[0] // n
    depth = tokens.shape[1]
    width = 2 * gate_weight.shape[1]
    cols = width // 4
    t4 = tokens.reshape(side, side, rows, depth)
    f32 = jnp.float32
    return pl.pallas_call(
        functools.partial(_ring_rs_kernel, side, cols, 2),
        out_shape=jax.ShapeDtypeStruct((rows, width), f32),
        in_specs=[pl.BlockSpec(memory_space=pltpu.VMEM), pl.BlockSpec(memory_space=pl.ANY),
                  pl.BlockSpec(memory_space=pl.ANY)],
        out_specs=pl.BlockSpec(memory_space=pltpu.VMEM),
        scratch_shapes=[
            pltpu.VMEM((4, depth, cols), gate_weight.dtype),
            pltpu.VMEM((4, side, rows, cols), jnp.bfloat16),
            pltpu.VMEM((4, side, rows, cols), jnp.bfloat16),
            pltpu.VMEM((4, side, rows, cols), f32),
            pltpu.VMEM((4, side - 1, side, rows, cols), f32),
            pltpu.VMEM((4, side - 2, side, rows, cols), f32),
            pltpu.VMEM((4, side, rows, cols), f32),
            pltpu.VMEM((4, side - 1, rows, cols), f32),
            pltpu.VMEM((4, side - 2, rows, cols), f32),
            pltpu.SemaphoreType.DMA((48,)),
            pltpu.SemaphoreType.DMA((48,)),
            pltpu.SemaphoreType.DMA((4,)),
        ],
        compiler_params=pltpu.CompilerParams(
            collective_id=collective_id, has_side_effects=True, vmem_limit_bytes=63 * 1024 * 1024),
    )(t4, gate_weight, up_weight)


def _grid_ag_kernel(side, cols, h_ref, out_ref, gath, send_sem, recv_sem, local_sem):
    w = lax.axis_index("wa")
    x, z = w // side, lax.rem(w, side)

    def peer(axis, delta):
        if axis == 0:
            return lax.rem(x + delta + side, side) * side + z
        return x * side + lax.rem(z + delta + side, side)

    barrier = pltpu.get_barrier_semaphore()
    for axis in (0, 1):
        for delta in (1, -1):
            pl.semaphore_signal(barrier, inc=1, device_id={"wa": peer(axis, delta)}, device_id_type=MESH)
    pl.semaphore_wait(barrier, 4)

    halves = [pl.ds(0, cols), pl.ds(cols, cols)]
    rows = h_ref.shape[0]
    locals_ = []
    for f in range(2):
        c = halves[f]
        copy = pltpu.make_async_copy(h_ref.at[:, c], gath.at[x, z, :, c], local_sem.at[f])
        copy.start()
        locals_.append(copy)

    def piece(f, stage, at, part=None):
        c = halves[f]
        along_x = (f == 0) == (stage == 0)
        if stage == 0:
            span = slice(None) if part is None else pl.ds(part * (rows // 2), rows // 2)
            if along_x:
                return gath.at[at, z, span, c]
            return gath.at[x, at, span, c]
        span = slice(None) if part is None else pl.ds(part * (side // 2), side // 2)
        if along_x:
            return gath.at[at, span, :, c]
        return gath.at[span, at, :, c]

    sends = []
    for stage in range(2):
        first, geometry = {}, {}
        for f in range(2):
            along_x = (f == 0) == (stage == 0)
            axis = 0 if along_x else 1
            pos = x if along_x else z
            base = (f * 2 + stage) * 4
            geometry[f] = (axis, pos, base)
            if stage == 0:
                locals_[f].wait()
            own = piece(f, stage, pos)
            first[f] = []
            for j, delta in enumerate((1, -1)):
                copy = pltpu.make_async_remote_copy(
                    src_ref=own, dst_ref=own,
                    send_sem=send_sem.at[base + j], recv_sem=recv_sem.at[base + j],
                    device_id={"wa": peer(axis, delta)}, device_id_type=MESH)
                copy.start()
                first[f].append(copy)
                sends.append(copy)
        second = []
        for f in range(2):
            axis, pos, base = geometry[f]
            for j, delta in enumerate((1, -1)):
                first[f][j].wait_recv()
                origin = lax.rem(pos - delta + side, side)
                part = piece(f, stage, origin, j)
                copy = pltpu.make_async_remote_copy(
                    src_ref=part, dst_ref=part,
                    send_sem=send_sem.at[base + 2 + j], recv_sem=recv_sem.at[base + 2 + j],
                    device_id={"wa": peer(axis, delta)}, device_id_type=MESH)
                copy.start()
                second.append(copy)
                sends.append(copy)
        for copy in second:
            copy.wait_recv()
    for copy in sends:
        copy.wait_send()
    final = pltpu.make_async_copy(gath, out_ref, local_sem.at[2])
    final.start()
    final.wait()


def grid_all_gather(h, n, collective_id):
    side = 4
    rows, width = h.shape
    cols = width // 2
    out = pl.pallas_call(
        functools.partial(_grid_ag_kernel, side, cols),
        out_shape=jax.ShapeDtypeStruct((side, side, rows, width), h.dtype),
        in_specs=[pl.BlockSpec(memory_space=pltpu.VMEM)],
        out_specs=pl.BlockSpec(memory_space=pltpu.VMEM),
        scratch_shapes=[
            pltpu.VMEM((side, side, rows, width), h.dtype),
            pltpu.SemaphoreType.DMA((4 * side,)),
            pltpu.SemaphoreType.DMA((4 * side,)),
            pltpu.SemaphoreType.DMA((3,)),
        ],
        compiler_params=pltpu.CompilerParams(collective_id=collective_id, has_side_effects=True),
    )(h)
    return out.reshape(n * rows, width)


def _down_rs_kernel(n, rows, h_ref, w_hbm, out_ref, wbuf, sendbuf, slots, send_sem, recv_sem, w_sem):
    me = lax.axis_index("ha")
    load = pltpu.make_async_copy(w_hbm, wbuf, w_sem.at[0])
    load.start()
    _greet("ha", n, me)
    load.wait()
    copies = []
    for k in range(1, n):
        peer = lax.rem(me + k, n)
        block = h_ref[pl.ds(pl.multiple_of(peer * rows, rows), rows), :]
        sendbuf[k] = jnp.dot(block, wbuf[...], preferred_element_type=jnp.float32).astype(sendbuf.dtype)
        copy = pltpu.make_async_remote_copy(
            src_ref=sendbuf.at[k], dst_ref=slots.at[k],
            send_sem=send_sem.at[k], recv_sem=recv_sem.at[k],
            device_id={"ha": peer}, device_id_type=MESH)
        copy.start()
        copies.append(copy)
    block = h_ref[pl.ds(pl.multiple_of(me * rows, rows), rows), :]
    total = jnp.dot(block, wbuf[...], preferred_element_type=jnp.float32)
    for k, copy in enumerate(copies, 1):
        copy.wait()
        total = total + slots[k].astype(jnp.float32)
    out_ref[...] = total


def down_reduce_scatter(hidden, down_weight, n, collective_id):
    rows = hidden.shape[0] // n
    depth, width = down_weight.shape
    return pl.pallas_call(
        functools.partial(_down_rs_kernel, n, rows),
        out_shape=jax.ShapeDtypeStruct((rows, width), jnp.float32),
        in_specs=[pl.BlockSpec(memory_space=pltpu.VMEM), pl.BlockSpec(memory_space=pl.ANY)],
        out_specs=pl.BlockSpec(memory_space=pltpu.VMEM),
        scratch_shapes=[
            pltpu.VMEM((depth, width), down_weight.dtype),
            pltpu.VMEM((n, rows, width), jnp.bfloat16),
            pltpu.VMEM((n, rows, width), jnp.bfloat16),
            pltpu.SemaphoreType.DMA((n,)),
            pltpu.SemaphoreType.DMA((n,)),
            pltpu.SemaphoreType.DMA((1,)),
        ],
        compiler_params=pltpu.CompilerParams(
            collective_id=collective_id, has_side_effects=True, vmem_limit_bytes=48 * 1024 * 1024),
    )(hidden, down_weight)


def body(tokens, norm_gain, gate_weight, up_weight, down_weight):
    n_wa = lax.axis_size("wa")
    n_ha = lax.axis_size("ha")
    own_values = tokens.astype(jnp.float32)
    model_width = own_values.shape[1] * n_wa
    own_rows = own_values.shape[0]
    partial_squares = jnp.sum(own_values * own_values, axis=1)
    packed = jnp.pad(partial_squares.reshape(8, own_rows // 8), ((0, 0), (0, 128 - own_rows // 8)))
    squares = exchange(packed, "sum", "wa", n_wa, 0)[:, : own_rows // 8].reshape(own_rows, 1)
    mean_square = squares / model_width
    normed = (own_values * lax.rsqrt(mean_square + 1e-05) * norm_gain[None, :]).astype(jnp.bfloat16)
    gathered = exchange(normed, "gather", "ha", n_ha, 1)
    hidden_width = gate_weight.shape[1]
    summed = ring_reduce_scatter(gathered, gate_weight, up_weight, n_wa, 2)
    gate = summed[:, :hidden_width]
    up = summed[:, hidden_width:]
    hidden = (jax.nn.silu(gate) * up).astype(jnp.bfloat16)
    all_hidden = grid_all_gather(hidden, n_wa, 3)
    mixed_out = down_reduce_scatter(all_hidden, down_weight, n_ha, 4)
    return mixed_out.astype(jnp.bfloat16)


def solution(mesh):
    placed = (P("ha", "wa"), P("wa"), P("wa", "ha"), P("wa", "ha"), P("ha", "wa"))
    return jax.shard_map(body, mesh=mesh, in_specs=placed, out_specs=P("ha", "wa"), check_vma=False)
```

```python
import functools

import jax
import jax.numpy as jnp
from jax import lax
from jax.experimental import pallas as pl
from jax.experimental.pallas import tpu as pltpu
from jax.sharding import PartitionSpec as P

MESH = pl.DeviceIdType.MESH


def _greet(axis, n, me):
    barrier = pltpu.get_barrier_semaphore()
    for k in range(1, n):
        pl.semaphore_signal(barrier, inc=1, device_id={axis: lax.rem(me + k, n)}, device_id_type=MESH)
    pl.semaphore_wait(barrier, n - 1)


def _exchange_kernel(mode, axis, n, rows, x_ref, out_ref, slots, send_sem, recv_sem):
    me = lax.axis_index(axis)
    _greet(axis, n, me)
    copies = []
    for k in range(1, n):
        peer = lax.rem(me + k, n)
        if mode == "gather":
            source = x_ref
        elif mode == "scatter":
            source = x_ref.at[pl.ds(pl.multiple_of(peer * rows, rows), rows)]
        else:
            source = x_ref
        copy = pltpu.make_async_remote_copy(
            src_ref=source,
            dst_ref=slots.at[k],
            send_sem=send_sem.at[k],
            recv_sem=recv_sem.at[k],
            device_id={axis: peer},
            device_id_type=MESH,
        )
        copy.start()
        copies.append(copy)
    if mode == "gather":
        out_ref[pl.ds(pl.multiple_of(me * rows, rows), rows), :] = x_ref[...]
        for k, copy in enumerate(copies, 1):
            copy.wait()
            sender = lax.rem(me + n - k, n)
            out_ref[pl.ds(pl.multiple_of(sender * rows, rows), rows), :] = slots[k]
    elif mode == "scatter":
        total = x_ref[pl.ds(pl.multiple_of(me * rows, rows), rows), :].astype(jnp.float32)
        for k, copy in enumerate(copies, 1):
            copy.wait()
            total = total + slots[k].astype(jnp.float32)
        out_ref[...] = total
    else:
        for copy in copies:
            copy.wait()
        slots[0] = x_ref[...]
        total = jnp.zeros(out_ref.shape, jnp.float32)
        for sender in range(n):
            total = total + slots[lax.rem(me + n - sender, n)].astype(jnp.float32)
        out_ref[...] = total


def exchange(x, mode, axis, n, collective_id):
    if n == 1:
        return x.astype(jnp.float32) if mode != "gather" else x
    if mode == "gather":
        rows = x.shape[0]
        out_shape = jax.ShapeDtypeStruct((n * rows, x.shape[1]), x.dtype)
    elif mode == "scatter":
        rows = x.shape[0] // n
        out_shape = jax.ShapeDtypeStruct((rows, x.shape[1]), jnp.float32)
    else:
        rows = x.shape[0]
        out_shape = jax.ShapeDtypeStruct(x.shape, jnp.float32)
    return pl.pallas_call(
        functools.partial(_exchange_kernel, mode, axis, n, rows),
        out_shape=out_shape,
        in_specs=[pl.BlockSpec(memory_space=pltpu.VMEM)],
        out_specs=pl.BlockSpec(memory_space=pltpu.VMEM),
        scratch_shapes=[
            pltpu.VMEM((n, rows, x.shape[1]), x.dtype),
            pltpu.SemaphoreType.DMA((n,)),
            pltpu.SemaphoreType.DMA((n,)),
        ],
        compiler_params=pltpu.CompilerParams(collective_id=collective_id, has_side_effects=True),
    )(x)


def _ring_rs_kernel(side, cols, parts, t_ref, g_hbm, u_hbm, out_ref, summed, wbuf, first_buf, recv_b, tmp, recv1,
                    acc1, s1, recv2, acc2, send_sem, recv_sem, w_sem):
    w = lax.axis_index("wa")
    x, z = w // side, lax.rem(w, side)
    loads = []
    for f in range(4):
        source = g_hbm if f < 2 else u_hbm
        load = pltpu.make_async_copy(source.at[:, pl.ds((f % 2) * cols, cols)], wbuf.at[f], w_sem.at[f])
        load.start()
        loads.append(load)

    def peer(axis, delta):
        if axis == 0:
            return lax.rem(x + delta + side, side) * side + z
        return x * side + lax.rem(z + delta + side, side)

    barrier = pltpu.get_barrier_semaphore()
    for axis in (0, 1):
        for delta in (1, -1):
            pl.semaphore_signal(barrier, inc=1, device_id={"wa": peer(axis, delta)}, device_id_type=MESH)
    pl.semaphore_wait(barrier, 4)

    flows = []
    for f in range(4):
        first = 0 if f < 2 else 1
        delta = 1 if f % 2 == 0 else -1
        flows.append((first, delta, pl.ds(f * cols, cols)))

    def own1(f, chunk):
        if flows[f][0] == 0:
            rows = t_ref[chunk]
        else:
            rows = t_ref[:, chunk]
        block = rows.reshape(side * rows.shape[1], rows.shape[2])
        product = jnp.dot(block, wbuf[f], preferred_element_type=jnp.float32)
        return product.reshape(side, rows.shape[1], cols)

    def sem(stage, step, f, h):
        return ((stage * 3 + step) * 4 + f) * parts + h

    sub = t_ref.shape[2] // parts
    halves = [pl.ds(h * sub, sub) for h in range(parts)]
    sends = []
    pos1 = [x if flows[f][0] == 0 else z for f in range(4)]
    pos2 = [z if flows[f][0] == 0 else x for f in range(4)]
    last = [[None] * parts for _ in range(4)]

    def send(stage, step, f, h, source, target, axis):
        copy = pltpu.make_async_remote_copy(
            src_ref=source, dst_ref=target,
            send_sem=send_sem.at[sem(stage, step, f, h)], recv_sem=recv_sem.at[sem(stage, step, f, h)],
            device_id={"wa": peer(axis, flows[f][1])}, device_id_type=MESH)
        copy.start()
        sends.append(copy)
        last[f][h] = copy

    for step in range(side - 1):
        for f in range(4):
            first, delta, _ = flows[f]
            chunk = lax.rem(pos1[f] - delta * (step + 1) + 2 * side, side)
            if step == 0:
                loads[f].wait()
                first_buf[f] = own1(f, chunk).astype(first_buf.dtype)
                for h, r in enumerate(halves):
                    send(0, step, f, h, first_buf.at[f, :, r], recv_b.at[f, :, r], first)
            else:
                tmp[f] = own1(f, chunk)
                for h, r in enumerate(halves):
                    last[f][h].wait_recv()
                    if step == 1:
                        arrived = recv_b[f, :, r].astype(jnp.float32)
                    else:
                        arrived = recv1[f, step - 1, :, r]
                    acc1[f, step - 1, :, r] = arrived + tmp[f, :, r]
                    send(0, step, f, h, acc1.at[f, step - 1, :, r], recv1.at[f, step, :, r], first)
    for f in range(4):
        first, delta, _ = flows[f]
        tmp[f] = own1(f, pos1[f])
        chunk = lax.rem(pos2[f] - delta + 2 * side, side)
        for h, r in enumerate(halves):
            last[f][h].wait_recv()
            s1[f, :, r] = recv1[f, side - 2, :, r] + tmp[f, :, r]
            send(1, 0, f, h, s1.at[f, chunk, r], recv2.at[f, 0, r], 1 - first)
    for step in range(1, side - 1):
        for f in range(4):
            first, delta, _ = flows[f]
            chunk = lax.rem(pos2[f] - delta * (step + 1) + 2 * side, side)
            for h, r in enumerate(halves):
                last[f][h].wait_recv()
                acc2[f, step - 1, r] = recv2[f, step - 1, r] + s1[f, chunk, r]
                send(1, step, f, h, acc2.at[f, step - 1, r], recv2.at[f, step, r], 1 - first)
    for f in range(4):
        for h, r in enumerate(halves):
            last[f][h].wait_recv()
            summed[r, flows[f][2]] = recv2[f, side - 2, r] + s1[f, pos2[f], r]
    gate = summed[:, pl.ds(0, 2 * cols)]
    up = summed[:, pl.ds(2 * cols, 2 * cols)]
    out_ref[...] = (gate / (1.0 + jnp.exp(-gate)) * up).astype(out_ref.dtype)
    for copy in sends:
        copy.wait_send()


def ring_reduce_scatter(tokens, gate_weight, up_weight, n, collective_id):
    side = 4
    rows = tokens.shape[0] // n
    depth = tokens.shape[1]
    width = 2 * gate_weight.shape[1]
    cols = width // 4
    t4 = tokens.reshape(side, side, rows, depth)
    f32 = jnp.float32
    return pl.pallas_call(
        functools.partial(_ring_rs_kernel, side, cols, 2),
        out_shape=jax.ShapeDtypeStruct((rows, width // 2), jnp.bfloat16),
        in_specs=[pl.BlockSpec(memory_space=pltpu.VMEM), pl.BlockSpec(memory_space=pl.ANY),
                  pl.BlockSpec(memory_space=pl.ANY)],
        out_specs=pl.BlockSpec(memory_space=pltpu.VMEM),
        scratch_shapes=[
            pltpu.VMEM((rows, width), f32),
            pltpu.VMEM((4, depth, cols), gate_weight.dtype),
            pltpu.VMEM((4, side, rows, cols), jnp.bfloat16),
            pltpu.VMEM((4, side, rows, cols), jnp.bfloat16),
            pltpu.VMEM((4, side, rows, cols), f32),
            pltpu.VMEM((4, side - 1, side, rows, cols), f32),
            pltpu.VMEM((4, side - 2, side, rows, cols), f32),
            pltpu.VMEM((4, side, rows, cols), f32),
            pltpu.VMEM((4, side - 1, rows, cols), f32),
            pltpu.VMEM((4, side - 2, rows, cols), f32),
            pltpu.SemaphoreType.DMA((48,)),
            pltpu.SemaphoreType.DMA((48,)),
            pltpu.SemaphoreType.DMA((4,)),
        ],
        compiler_params=pltpu.CompilerParams(
            collective_id=collective_id, has_side_effects=True, vmem_limit_bytes=63 * 1024 * 1024),
    )(t4, gate_weight, up_weight)


def _grid_ag_kernel(side, cols, h_ref, out_ref, gath, send_sem, recv_sem, local_sem):
    w = lax.axis_index("wa")
    x, z = w // side, lax.rem(w, side)

    def peer(axis, delta):
        if axis == 0:
            return lax.rem(x + delta + side, side) * side + z
        return x * side + lax.rem(z + delta + side, side)

    barrier = pltpu.get_barrier_semaphore()
    for axis in (0, 1):
        for delta in (1, -1):
            pl.semaphore_signal(barrier, inc=1, device_id={"wa": peer(axis, delta)}, device_id_type=MESH)
    pl.semaphore_wait(barrier, 4)

    halves = [pl.ds(0, cols), pl.ds(cols, cols)]
    rows = h_ref.shape[0]
    locals_ = []
    for f in range(2):
        c = halves[f]
        copy = pltpu.make_async_copy(h_ref.at[:, c], gath.at[x, z, :, c], local_sem.at[f])
        copy.start()
        locals_.append(copy)

    def piece(f, stage, at, part=None):
        c = halves[f]
        along_x = (f == 0) == (stage == 0)
        if stage == 0:
            span = slice(None) if part is None else pl.ds(part * (rows // 2), rows // 2)
            if along_x:
                return gath.at[at, z, span, c]
            return gath.at[x, at, span, c]
        span = slice(None) if part is None else pl.ds(part * (side // 2), side // 2)
        if along_x:
            return gath.at[at, span, :, c]
        return gath.at[span, at, :, c]

    sends = []
    for stage in range(2):
        first, geometry = {}, {}
        for f in range(2):
            along_x = (f == 0) == (stage == 0)
            axis = 0 if along_x else 1
            pos = x if along_x else z
            base = (f * 2 + stage) * 4
            geometry[f] = (axis, pos, base)
            if stage == 0:
                locals_[f].wait()
            own = piece(f, stage, pos)
            first[f] = []
            for j, delta in enumerate((1, -1)):
                copy = pltpu.make_async_remote_copy(
                    src_ref=own, dst_ref=own,
                    send_sem=send_sem.at[base + j], recv_sem=recv_sem.at[base + j],
                    device_id={"wa": peer(axis, delta)}, device_id_type=MESH)
                copy.start()
                first[f].append(copy)
                sends.append(copy)
        second = []
        for f in range(2):
            axis, pos, base = geometry[f]
            for j, delta in enumerate((1, -1)):
                first[f][j].wait_recv()
                origin = lax.rem(pos - delta + side, side)
                part = piece(f, stage, origin, j)
                copy = pltpu.make_async_remote_copy(
                    src_ref=part, dst_ref=part,
                    send_sem=send_sem.at[base + 2 + j], recv_sem=recv_sem.at[base + 2 + j],
                    device_id={"wa": peer(axis, delta)}, device_id_type=MESH)
                copy.start()
                second.append(copy)
                sends.append(copy)
        for copy in second:
            copy.wait_recv()
    for copy in sends:
        copy.wait_send()
    final = pltpu.make_async_copy(gath, out_ref, local_sem.at[2])
    final.start()
    final.wait()


def grid_all_gather(h, n, collective_id):
    side = 4
    rows, width = h.shape
    cols = width // 2
    out = pl.pallas_call(
        functools.partial(_grid_ag_kernel, side, cols),
        out_shape=jax.ShapeDtypeStruct((side, side, rows, width), h.dtype),
        in_specs=[pl.BlockSpec(memory_space=pltpu.VMEM)],
        out_specs=pl.BlockSpec(memory_space=pltpu.VMEM),
        scratch_shapes=[
            pltpu.VMEM((side, side, rows, width), h.dtype),
            pltpu.SemaphoreType.DMA((4 * side,)),
            pltpu.SemaphoreType.DMA((4 * side,)),
            pltpu.SemaphoreType.DMA((3,)),
        ],
        compiler_params=pltpu.CompilerParams(collective_id=collective_id, has_side_effects=True),
    )(h)
    return out.reshape(n * rows, width)


def _down_rs_kernel(n, rows, h_ref, w_hbm, out_ref, wbuf, sendbuf, slots, send_sem, recv_sem, w_sem):
    me = lax.axis_index("ha")
    load = pltpu.make_async_copy(w_hbm, wbuf, w_sem.at[0])
    load.start()
    _greet("ha", n, me)
    load.wait()
    copies = []
    for k in range(1, n):
        peer = lax.rem(me + k, n)
        block = h_ref[pl.ds(pl.multiple_of(peer * rows, rows), rows), :]
        sendbuf[k] = jnp.dot(block, wbuf[...], preferred_element_type=jnp.float32).astype(sendbuf.dtype)
        copy = pltpu.make_async_remote_copy(
            src_ref=sendbuf.at[k], dst_ref=slots.at[k],
            send_sem=send_sem.at[k], recv_sem=recv_sem.at[k],
            device_id={"ha": peer}, device_id_type=MESH)
        copy.start()
        copies.append(copy)
    block = h_ref[pl.ds(pl.multiple_of(me * rows, rows), rows), :]
    total = jnp.dot(block, wbuf[...], preferred_element_type=jnp.float32)
    for k, copy in enumerate(copies, 1):
        copy.wait()
        total = total + slots[k].astype(jnp.float32)
    out_ref[...] = total


def down_reduce_scatter(hidden, down_weight, n, collective_id):
    rows = hidden.shape[0] // n
    depth, width = down_weight.shape
    return pl.pallas_call(
        functools.partial(_down_rs_kernel, n, rows),
        out_shape=jax.ShapeDtypeStruct((rows, width), jnp.float32),
        in_specs=[pl.BlockSpec(memory_space=pltpu.VMEM), pl.BlockSpec(memory_space=pl.ANY)],
        out_specs=pl.BlockSpec(memory_space=pltpu.VMEM),
        scratch_shapes=[
            pltpu.VMEM((depth, width), down_weight.dtype),
            pltpu.VMEM((n, rows, width), jnp.bfloat16),
            pltpu.VMEM((n, rows, width), jnp.bfloat16),
            pltpu.SemaphoreType.DMA((n,)),
            pltpu.SemaphoreType.DMA((n,)),
            pltpu.SemaphoreType.DMA((1,)),
        ],
        compiler_params=pltpu.CompilerParams(
            collective_id=collective_id, has_side_effects=True, vmem_limit_bytes=48 * 1024 * 1024),
    )(hidden, down_weight)


def body(tokens, norm_gain, gate_weight, up_weight, down_weight):
    n_wa = lax.axis_size("wa")
    n_ha = lax.axis_size("ha")
    own_values = tokens.astype(jnp.float32)
    model_width = own_values.shape[1] * n_wa
    own_rows = own_values.shape[0]
    partial_squares = jnp.sum(own_values * own_values, axis=1)
    packed = jnp.pad(partial_squares.reshape(8, own_rows // 8), ((0, 0), (0, 128 - own_rows // 8)))
    squares = exchange(packed, "sum", "wa", n_wa, 0)[:, : own_rows // 8].reshape(own_rows, 1)
    mean_square = squares / model_width
    normed = (own_values * lax.rsqrt(mean_square + 1e-05) * norm_gain[None, :]).astype(jnp.bfloat16)
    gathered = exchange(normed, "gather", "ha", n_ha, 1)
    hidden_width = gate_weight.shape[1]
    hidden = ring_reduce_scatter(gathered, gate_weight, up_weight, n_wa, 2)
    all_hidden = grid_all_gather(hidden, n_wa, 3)
    mixed_out = down_reduce_scatter(all_hidden, down_weight, n_ha, 4)
    return mixed_out.astype(jnp.bfloat16)


def solution(mesh):
    placed = (P("ha", "wa"), P("wa"), P("wa", "ha"), P("wa", "ha"), P("ha", "wa"))
    return jax.shard_map(body, mesh=mesh, in_specs=placed, out_specs=P("ha", "wa"), check_vma=False)
```

```python
import functools

import jax
import jax.numpy as jnp
from jax import lax
from jax.experimental import pallas as pl
from jax.experimental.pallas import tpu as pltpu
from jax.sharding import PartitionSpec as P

MESH = pl.DeviceIdType.MESH


def _greet(axis, n, me):
    barrier = pltpu.get_barrier_semaphore()
    for k in range(1, n):
        pl.semaphore_signal(barrier, inc=1, device_id={axis: lax.rem(me + k, n)}, device_id_type=MESH)
    pl.semaphore_wait(barrier, n - 1)


def _exchange_kernel(mode, axis, n, rows, x_ref, out_ref, slots, send_sem, recv_sem):
    me = lax.axis_index(axis)
    _greet(axis, n, me)
    copies = []
    for k in range(1, n):
        peer = lax.rem(me + k, n)
        if mode == "gather":
            source = x_ref
        elif mode == "scatter":
            source = x_ref.at[pl.ds(pl.multiple_of(peer * rows, rows), rows)]
        else:
            source = x_ref
        copy = pltpu.make_async_remote_copy(
            src_ref=source,
            dst_ref=slots.at[k],
            send_sem=send_sem.at[k],
            recv_sem=recv_sem.at[k],
            device_id={axis: peer},
            device_id_type=MESH,
        )
        copy.start()
        copies.append(copy)
    if mode == "gather":
        out_ref[pl.ds(pl.multiple_of(me * rows, rows), rows), :] = x_ref[...]
        for k, copy in enumerate(copies, 1):
            copy.wait()
            sender = lax.rem(me + n - k, n)
            out_ref[pl.ds(pl.multiple_of(sender * rows, rows), rows), :] = slots[k]
    elif mode == "scatter":
        total = x_ref[pl.ds(pl.multiple_of(me * rows, rows), rows), :].astype(jnp.float32)
        for k, copy in enumerate(copies, 1):
            copy.wait()
            total = total + slots[k].astype(jnp.float32)
        out_ref[...] = total
    else:
        for copy in copies:
            copy.wait()
        slots[0] = x_ref[...]
        total = jnp.zeros(out_ref.shape, jnp.float32)
        for sender in range(n):
            total = total + slots[lax.rem(me + n - sender, n)].astype(jnp.float32)
        out_ref[...] = total


def exchange(x, mode, axis, n, collective_id):
    if n == 1:
        return x.astype(jnp.float32) if mode != "gather" else x
    if mode == "gather":
        rows = x.shape[0]
        out_shape = jax.ShapeDtypeStruct((n * rows, x.shape[1]), x.dtype)
    elif mode == "scatter":
        rows = x.shape[0] // n
        out_shape = jax.ShapeDtypeStruct((rows, x.shape[1]), jnp.float32)
    else:
        rows = x.shape[0]
        out_shape = jax.ShapeDtypeStruct(x.shape, jnp.float32)
    return pl.pallas_call(
        functools.partial(_exchange_kernel, mode, axis, n, rows),
        out_shape=out_shape,
        in_specs=[pl.BlockSpec(memory_space=pltpu.VMEM)],
        out_specs=pl.BlockSpec(memory_space=pltpu.VMEM),
        scratch_shapes=[
            pltpu.VMEM((n, rows, x.shape[1]), x.dtype),
            pltpu.SemaphoreType.DMA((n,)),
            pltpu.SemaphoreType.DMA((n,)),
        ],
        compiler_params=pltpu.CompilerParams(collective_id=collective_id, has_side_effects=True),
    )(x)


def _ring_rs_kernel(side, cols, parts, t_ref, g_hbm, u_hbm, out_ref, summed, wbuf, first_buf, recv_b, tmp, recv1,
                    acc1, s1, recv2, acc2, send_sem, recv_sem, w_sem):
    w = lax.axis_index("wa")
    x, z = w // side, lax.rem(w, side)
    loads = []
    for f in range(4):
        source = g_hbm if f < 2 else u_hbm
        load = pltpu.make_async_copy(source.at[:, pl.ds((f % 2) * cols, cols)], wbuf.at[f], w_sem.at[f])
        load.start()
        loads.append(load)

    def peer(axis, delta):
        if axis == 0:
            return lax.rem(x + delta + side, side) * side + z
        return x * side + lax.rem(z + delta + side, side)

    barrier = pltpu.get_barrier_semaphore()
    for axis in (0, 1):
        for delta in (1, -1):
            pl.semaphore_signal(barrier, inc=1, device_id={"wa": peer(axis, delta)}, device_id_type=MESH)
    pl.semaphore_wait(barrier, 4)

    flows = []
    for f in range(4):
        first = 0 if f < 2 else 1
        delta = 1 if f % 2 == 0 else -1
        flows.append((first, delta, pl.ds(f * cols, cols)))

    def own1(f, chunk):
        if flows[f][0] == 0:
            rows = t_ref[chunk]
        else:
            rows = t_ref[:, chunk]
        block = rows.reshape(side * rows.shape[1], rows.shape[2])
        product = jnp.dot(block, wbuf[f], preferred_element_type=jnp.float32)
        return product.reshape(side, rows.shape[1], cols)

    def sem(stage, step, f, h):
        return ((stage * 3 + step) * 4 + f) * parts + h

    sub = t_ref.shape[2] // parts
    halves = [pl.ds(h * sub, sub) for h in range(parts)]
    sends = []
    pos1 = [x if flows[f][0] == 0 else z for f in range(4)]
    pos2 = [z if flows[f][0] == 0 else x for f in range(4)]
    last = [[None] * parts for _ in range(4)]

    def send(stage, step, f, h, source, target, axis):
        copy = pltpu.make_async_remote_copy(
            src_ref=source, dst_ref=target,
            send_sem=send_sem.at[sem(stage, step, f, h)], recv_sem=recv_sem.at[sem(stage, step, f, h)],
            device_id={"wa": peer(axis, flows[f][1])}, device_id_type=MESH)
        copy.start()
        sends.append(copy)
        last[f][h] = copy

    for step in range(side - 1):
        for f in range(4):
            first, delta, _ = flows[f]
            chunk = lax.rem(pos1[f] - delta * (step + 1) + 2 * side, side)
            if step == 0:
                loads[f].wait()
                first_buf[f] = own1(f, chunk).astype(first_buf.dtype)
                for h, r in enumerate(halves):
                    send(0, step, f, h, first_buf.at[f, :, r], recv_b.at[f, :, r], first)
            else:
                tmp[f] = own1(f, chunk)
                for h, r in enumerate(halves):
                    last[f][h].wait_recv()
                    if step == 1:
                        arrived = recv_b[f, :, r].astype(jnp.float32)
                    else:
                        arrived = recv1[f, step - 1, :, r]
                    acc1[f, step - 1, :, r] = arrived + tmp[f, :, r]
                    send(0, step, f, h, acc1.at[f, step - 1, :, r], recv1.at[f, step, :, r], first)
    for f in range(4):
        first, delta, _ = flows[f]
        tmp[f] = own1(f, pos1[f])
        chunk = lax.rem(pos2[f] - delta + 2 * side, side)
        for h, r in enumerate(halves):
            last[f][h].wait_recv()
            s1[f, :, r] = recv1[f, side - 2, :, r] + tmp[f, :, r]
            send(1, 0, f, h, s1.at[f, chunk, r], recv2.at[f, 0, r], 1 - first)
    for step in range(1, side - 1):
        for f in range(4):
            first, delta, _ = flows[f]
            chunk = lax.rem(pos2[f] - delta * (step + 1) + 2 * side, side)
            for h, r in enumerate(halves):
                last[f][h].wait_recv()
                acc2[f, step - 1, r] = recv2[f, step - 1, r] + s1[f, chunk, r]
                send(1, step, f, h, acc2.at[f, step - 1, r], recv2.at[f, step, r], 1 - first)
    for f in range(4):
        for h, r in enumerate(halves):
            last[f][h].wait_recv()
            summed[r, flows[f][2]] = recv2[f, side - 2, r] + s1[f, pos2[f], r]
    gate = summed[:, pl.ds(0, 2 * cols)]
    up = summed[:, pl.ds(2 * cols, 2 * cols)]
    out_ref[...] = (gate / (1.0 + jnp.exp(-gate)) * up).astype(out_ref.dtype)
    for copy in sends:
        copy.wait_send()


def ring_reduce_scatter(tokens, gate_weight, up_weight, n, collective_id):
    side = 4
    rows = tokens.shape[0] // n
    depth = tokens.shape[1]
    width = 2 * gate_weight.shape[1]
    cols = width // 4
    t4 = tokens.reshape(side, side, rows, depth)
    f32 = jnp.float32
    return pl.pallas_call(
        functools.partial(_ring_rs_kernel, side, cols, 2),
        out_shape=jax.ShapeDtypeStruct((rows, width // 2), jnp.bfloat16),
        in_specs=[pl.BlockSpec(memory_space=pltpu.VMEM), pl.BlockSpec(memory_space=pl.ANY),
                  pl.BlockSpec(memory_space=pl.ANY)],
        out_specs=pl.BlockSpec(memory_space=pltpu.VMEM),
        scratch_shapes=[
            pltpu.VMEM((rows, width), f32),
            pltpu.VMEM((4, depth, cols), gate_weight.dtype),
            pltpu.VMEM((4, side, rows, cols), jnp.bfloat16),
            pltpu.VMEM((4, side, rows, cols), jnp.bfloat16),
            pltpu.VMEM((4, side, rows, cols), f32),
            pltpu.VMEM((4, side - 1, side, rows, cols), f32),
            pltpu.VMEM((4, side - 2, side, rows, cols), f32),
            pltpu.VMEM((4, side, rows, cols), f32),
            pltpu.VMEM((4, side - 1, rows, cols), f32),
            pltpu.VMEM((4, side - 2, rows, cols), f32),
            pltpu.SemaphoreType.DMA((48,)),
            pltpu.SemaphoreType.DMA((48,)),
            pltpu.SemaphoreType.DMA((4,)),
        ],
        compiler_params=pltpu.CompilerParams(
            collective_id=collective_id, has_side_effects=True, vmem_limit_bytes=63 * 1024 * 1024),
    )(t4, gate_weight, up_weight)


def _grid_ag_kernel(side, cols, h_ref, out_ref, gath, send_sem, recv_sem, local_sem):
    w = lax.axis_index("wa")
    x, z = w // side, lax.rem(w, side)

    def peer(axis, delta):
        if axis == 0:
            return lax.rem(x + delta + side, side) * side + z
        return x * side + lax.rem(z + delta + side, side)

    barrier = pltpu.get_barrier_semaphore()
    for axis in (0, 1):
        for delta in (1, -1):
            pl.semaphore_signal(barrier, inc=1, device_id={"wa": peer(axis, delta)}, device_id_type=MESH)
    pl.semaphore_wait(barrier, 4)

    halves = [pl.ds(0, cols), pl.ds(cols, cols)]
    rows = h_ref.shape[0]
    locals_ = []
    for f in range(2):
        c = halves[f]
        copy = pltpu.make_async_copy(h_ref.at[:, c], gath.at[x, z, :, c], local_sem.at[f])
        copy.start()
        locals_.append(copy)

    def piece(f, stage, at, part=None):
        c = halves[f]
        along_x = (f == 0) == (stage == 0)
        if stage == 0:
            span = slice(None) if part is None else pl.ds(part * (rows // 2), rows // 2)
            if along_x:
                return gath.at[at, z, span, c]
            return gath.at[x, at, span, c]
        span = slice(None) if part is None else pl.ds(part * (side // 2), side // 2)
        if along_x:
            return gath.at[at, span, :, c]
        return gath.at[span, at, :, c]

    sends = []
    for stage in range(2):
        first, geometry = {}, {}
        for f in range(2):
            along_x = (f == 0) == (stage == 0)
            axis = 0 if along_x else 1
            pos = x if along_x else z
            base = (f * 2 + stage) * 4
            geometry[f] = (axis, pos, base)
            if stage == 0:
                locals_[f].wait()
            own = piece(f, stage, pos)
            first[f] = []
            for j, delta in enumerate((1, -1)):
                copy = pltpu.make_async_remote_copy(
                    src_ref=own, dst_ref=own,
                    send_sem=send_sem.at[base + j], recv_sem=recv_sem.at[base + j],
                    device_id={"wa": peer(axis, delta)}, device_id_type=MESH)
                copy.start()
                first[f].append(copy)
                sends.append(copy)
        second = []
        for f in range(2):
            axis, pos, base = geometry[f]
            for j, delta in enumerate((1, -1)):
                first[f][j].wait_recv()
                origin = lax.rem(pos - delta + side, side)
                part = piece(f, stage, origin, j)
                copy = pltpu.make_async_remote_copy(
                    src_ref=part, dst_ref=part,
                    send_sem=send_sem.at[base + 2 + j], recv_sem=recv_sem.at[base + 2 + j],
                    device_id={"wa": peer(axis, delta)}, device_id_type=MESH)
                copy.start()
                second.append(copy)
                sends.append(copy)
        for copy in second:
            copy.wait_recv()
    for copy in sends:
        copy.wait_send()
    final = pltpu.make_async_copy(gath, out_ref, local_sem.at[2])
    final.start()
    final.wait()


def grid_all_gather(h, n, collective_id):
    side = 4
    rows, width = h.shape
    cols = width // 2
    out = pl.pallas_call(
        functools.partial(_grid_ag_kernel, side, cols),
        out_shape=jax.ShapeDtypeStruct((side, side, rows, width), h.dtype),
        in_specs=[pl.BlockSpec(memory_space=pltpu.VMEM)],
        out_specs=pl.BlockSpec(memory_space=pltpu.VMEM),
        scratch_shapes=[
            pltpu.VMEM((side, side, rows, width), h.dtype),
            pltpu.SemaphoreType.DMA((4 * side,)),
            pltpu.SemaphoreType.DMA((4 * side,)),
            pltpu.SemaphoreType.DMA((3,)),
        ],
        compiler_params=pltpu.CompilerParams(collective_id=collective_id, has_side_effects=True),
    )(h)
    return out.reshape(n * rows, width)


def _down_rs_kernel(n, rows, h_ref, w_hbm, out_ref, wbuf, sendbuf, slots, send_sem, recv_sem, w_sem):
    me = lax.axis_index("ha")
    load = pltpu.make_async_copy(w_hbm, wbuf, w_sem.at[0])
    load.start()
    _greet("ha", n, me)
    load.wait()
    copies = []
    order = sorted(range(1, n), key=lambda k: -min(k, n - k))
    for k in order:
        peer = lax.rem(me + k, n)
        block = h_ref[pl.ds(pl.multiple_of(peer * rows, rows), rows), :]
        sendbuf[k] = jnp.dot(block, wbuf[...], preferred_element_type=jnp.float32).astype(sendbuf.dtype)
        copy = pltpu.make_async_remote_copy(
            src_ref=sendbuf.at[k], dst_ref=slots.at[k],
            send_sem=send_sem.at[k], recv_sem=recv_sem.at[k],
            device_id={"ha": peer}, device_id_type=MESH)
        copy.start()
        copies.append(copy)
    block = h_ref[pl.ds(pl.multiple_of(me * rows, rows), rows), :]
    total = jnp.dot(block, wbuf[...], preferred_element_type=jnp.float32)
    for k, copy in zip(order, copies):
        copy.wait()
        total = total + slots[k].astype(jnp.float32)
    out_ref[...] = total


def down_reduce_scatter(hidden, down_weight, n, collective_id):
    rows = hidden.shape[0] // n
    depth, width = down_weight.shape
    return pl.pallas_call(
        functools.partial(_down_rs_kernel, n, rows),
        out_shape=jax.ShapeDtypeStruct((rows, width), jnp.float32),
        in_specs=[pl.BlockSpec(memory_space=pltpu.VMEM), pl.BlockSpec(memory_space=pl.ANY)],
        out_specs=pl.BlockSpec(memory_space=pltpu.VMEM),
        scratch_shapes=[
            pltpu.VMEM((depth, width), down_weight.dtype),
            pltpu.VMEM((n, rows, width), jnp.bfloat16),
            pltpu.VMEM((n, rows, width), jnp.bfloat16),
            pltpu.SemaphoreType.DMA((n,)),
            pltpu.SemaphoreType.DMA((n,)),
            pltpu.SemaphoreType.DMA((1,)),
        ],
        compiler_params=pltpu.CompilerParams(
            collective_id=collective_id, has_side_effects=True, vmem_limit_bytes=48 * 1024 * 1024),
    )(hidden, down_weight)


def body(tokens, norm_gain, gate_weight, up_weight, down_weight):
    n_wa = lax.axis_size("wa")
    n_ha = lax.axis_size("ha")
    own_values = tokens.astype(jnp.float32)
    model_width = own_values.shape[1] * n_wa
    own_rows = own_values.shape[0]
    partial_squares = jnp.sum(own_values * own_values, axis=1)
    packed = jnp.pad(partial_squares.reshape(8, own_rows // 8), ((0, 0), (0, 128 - own_rows // 8)))
    squares = exchange(packed, "sum", "wa", n_wa, 0)[:, : own_rows // 8].reshape(own_rows, 1)
    mean_square = squares / model_width
    normed = (own_values * lax.rsqrt(mean_square + 1e-05) * norm_gain[None, :]).astype(jnp.bfloat16)
    gathered = exchange(normed, "gather", "ha", n_ha, 1)
    hidden_width = gate_weight.shape[1]
    hidden = ring_reduce_scatter(gathered, gate_weight, up_weight, n_wa, 2)
    all_hidden = grid_all_gather(hidden, n_wa, 3)
    mixed_out = down_reduce_scatter(all_hidden, down_weight, n_ha, 4)
    return mixed_out.astype(jnp.bfloat16)


def solution(mesh):
    placed = (P("ha", "wa"), P("wa"), P("wa", "ha"), P("wa", "ha"), P("ha", "wa"))
    return jax.shard_map(body, mesh=mesh, in_specs=placed, out_specs=P("ha", "wa"), check_vma=False)
```

```python
import functools

import jax
import jax.numpy as jnp
from jax import lax
from jax.experimental import pallas as pl
from jax.experimental.pallas import tpu as pltpu
from jax.sharding import PartitionSpec as P

MESH = pl.DeviceIdType.MESH


def _greet(axis, n, me):
    barrier = pltpu.get_barrier_semaphore()
    for k in range(1, n):
        pl.semaphore_signal(barrier, inc=1, device_id={axis: lax.rem(me + k, n)}, device_id_type=MESH)
    pl.semaphore_wait(barrier, n - 1)


def _exchange_kernel(mode, axis, n, rows, x_ref, out_ref, slots, send_sem, recv_sem):
    me = lax.axis_index(axis)
    _greet(axis, n, me)
    copies = []
    for k in range(1, n):
        peer = lax.rem(me + k, n)
        if mode == "gather":
            source = x_ref
        elif mode == "scatter":
            source = x_ref.at[pl.ds(pl.multiple_of(peer * rows, rows), rows)]
        else:
            source = x_ref
        copy = pltpu.make_async_remote_copy(
            src_ref=source,
            dst_ref=slots.at[k],
            send_sem=send_sem.at[k],
            recv_sem=recv_sem.at[k],
            device_id={axis: peer},
            device_id_type=MESH,
        )
        copy.start()
        copies.append(copy)
    if mode == "gather":
        out_ref[pl.ds(pl.multiple_of(me * rows, rows), rows), :] = x_ref[...]
        for k, copy in enumerate(copies, 1):
            copy.wait()
            sender = lax.rem(me + n - k, n)
            out_ref[pl.ds(pl.multiple_of(sender * rows, rows), rows), :] = slots[k]
    elif mode == "scatter":
        total = x_ref[pl.ds(pl.multiple_of(me * rows, rows), rows), :].astype(jnp.float32)
        for k, copy in enumerate(copies, 1):
            copy.wait()
            total = total + slots[k].astype(jnp.float32)
        out_ref[...] = total
    else:
        for copy in copies:
            copy.wait()
        slots[0] = x_ref[...]
        total = jnp.zeros(out_ref.shape, jnp.float32)
        for sender in range(n):
            total = total + slots[lax.rem(me + n - sender, n)].astype(jnp.float32)
        out_ref[...] = total


def exchange(x, mode, axis, n, collective_id):
    if n == 1:
        return x.astype(jnp.float32) if mode != "gather" else x
    if mode == "gather":
        rows = x.shape[0]
        out_shape = jax.ShapeDtypeStruct((n * rows, x.shape[1]), x.dtype)
    elif mode == "scatter":
        rows = x.shape[0] // n
        out_shape = jax.ShapeDtypeStruct((rows, x.shape[1]), jnp.float32)
    else:
        rows = x.shape[0]
        out_shape = jax.ShapeDtypeStruct(x.shape, jnp.float32)
    return pl.pallas_call(
        functools.partial(_exchange_kernel, mode, axis, n, rows),
        out_shape=out_shape,
        in_specs=[pl.BlockSpec(memory_space=pltpu.VMEM)],
        out_specs=pl.BlockSpec(memory_space=pltpu.VMEM),
        scratch_shapes=[
            pltpu.VMEM((n, rows, x.shape[1]), x.dtype),
            pltpu.SemaphoreType.DMA((n,)),
            pltpu.SemaphoreType.DMA((n,)),
        ],
        compiler_params=pltpu.CompilerParams(collective_id=collective_id, has_side_effects=True),
    )(x)


def _ring_rs_kernel(side, cols, parts, t_ref, g_hbm, u_hbm, out_ref, summed, wbuf, first_buf, recv_b, tmp, recv1,
                    acc1, s1, recv2, acc2, send_sem, recv_sem, w_sem):
    w = lax.axis_index("wa")
    x, z = w // side, lax.rem(w, side)
    loads = []
    for f in range(4):
        source = g_hbm if f < 2 else u_hbm
        load = pltpu.make_async_copy(source.at[:, pl.ds((f % 2) * cols, cols)], wbuf.at[f], w_sem.at[f])
        load.start()
        loads.append(load)

    def peer(axis, delta):
        if axis == 0:
            return lax.rem(x + delta + side, side) * side + z
        return x * side + lax.rem(z + delta + side, side)

    barrier = pltpu.get_barrier_semaphore()
    for axis in (0, 1):
        for delta in (1, -1):
            pl.semaphore_signal(barrier, inc=1, device_id={"wa": peer(axis, delta)}, device_id_type=MESH)
    pl.semaphore_wait(barrier, 4)

    flows = []
    for f in range(4):
        first = 0 if f < 2 else 1
        delta = 1 if f % 2 == 0 else -1
        flows.append((first, delta, pl.ds(f * cols, cols)))

    def own1(f, chunk):
        if flows[f][0] == 0:
            rows = t_ref[chunk]
        else:
            rows = t_ref[:, chunk]
        block = rows.reshape(side * rows.shape[1], rows.shape[2])
        product = jnp.dot(block, wbuf[f], preferred_element_type=jnp.float32)
        return product.reshape(side, rows.shape[1], cols)

    def sem(stage, step, f, h):
        return ((stage * 3 + step) * 4 + f) * parts + h

    sub = t_ref.shape[2] // parts
    halves = [pl.ds(h * sub, sub) for h in range(parts)]
    sends = []
    pos1 = [x if flows[f][0] == 0 else z for f in range(4)]
    pos2 = [z if flows[f][0] == 0 else x for f in range(4)]
    last = [[None] * parts for _ in range(4)]

    def send(stage, step, f, h, source, target, axis):
        copy = pltpu.make_async_remote_copy(
            src_ref=source, dst_ref=target,
            send_sem=send_sem.at[sem(stage, step, f, h)], recv_sem=recv_sem.at[sem(stage, step, f, h)],
            device_id={"wa": peer(axis, flows[f][1])}, device_id_type=MESH)
        copy.start()
        sends.append(copy)
        last[f][h] = copy

    for step in range(side - 1):
        for f in range(4):
            first, delta, _ = flows[f]
            chunk = lax.rem(pos1[f] - delta * (step + 1) + 2 * side, side)
            if step == 0:
                loads[f].wait()
                first_buf[f] = own1(f, chunk).astype(first_buf.dtype)
                for h, r in enumerate(halves):
                    send(0, step, f, h, first_buf.at[f, :, r], recv_b.at[f, :, r], first)
            else:
                tmp[f] = own1(f, chunk)
                for h, r in enumerate(halves):
                    last[f][h].wait_recv()
                    if step == 1:
                        arrived = recv_b[f, :, r].astype(jnp.float32)
                    else:
                        arrived = recv1[f, step - 1, :, r]
                    acc1[f, step - 1, :, r] = arrived + tmp[f, :, r]
                    send(0, step, f, h, acc1.at[f, step - 1, :, r], recv1.at[f, step, :, r], first)
    for f in range(4):
        first, delta, _ = flows[f]
        tmp[f] = own1(f, pos1[f])
        chunk = lax.rem(pos2[f] - delta + 2 * side, side)
        for h, r in enumerate(halves):
            last[f][h].wait_recv()
            s1[f, :, r] = recv1[f, side - 2, :, r] + tmp[f, :, r]
            send(1, 0, f, h, s1.at[f, chunk, r], recv2.at[f, 0, r], 1 - first)
    for step in range(1, side - 1):
        for f in range(4):
            first, delta, _ = flows[f]
            chunk = lax.rem(pos2[f] - delta * (step + 1) + 2 * side, side)
            for h, r in enumerate(halves):
                last[f][h].wait_recv()
                acc2[f, step - 1, r] = recv2[f, step - 1, r] + s1[f, chunk, r]
                send(1, step, f, h, acc2.at[f, step - 1, r], recv2.at[f, step, r], 1 - first)
    for f in range(4):
        for h, r in enumerate(halves):
            last[f][h].wait_recv()
            summed[r, flows[f][2]] = recv2[f, side - 2, r] + s1[f, pos2[f], r]
    gate = summed[:, pl.ds(0, 2 * cols)]
    up = summed[:, pl.ds(2 * cols, 2 * cols)]
    out_ref[...] = (gate / (1.0 + jnp.exp(-gate)) * up).astype(out_ref.dtype)
    for copy in sends:
        copy.wait_send()


def ring_reduce_scatter(tokens, gate_weight, up_weight, n, collective_id):
    side = 4
    rows = tokens.shape[0] // n
    depth = tokens.shape[1]
    width = 2 * gate_weight.shape[1]
    cols = width // 4
    t4 = tokens.reshape(side, side, rows, depth)
    f32 = jnp.float32
    return pl.pallas_call(
        functools.partial(_ring_rs_kernel, side, cols, 2),
        out_shape=jax.ShapeDtypeStruct((rows, width // 2), jnp.bfloat16),
        in_specs=[pl.BlockSpec(memory_space=pltpu.VMEM), pl.BlockSpec(memory_space=pl.ANY),
                  pl.BlockSpec(memory_space=pl.ANY)],
        out_specs=pl.BlockSpec(memory_space=pltpu.VMEM),
        scratch_shapes=[
            pltpu.VMEM((rows, width), f32),
            pltpu.VMEM((4, depth, cols), gate_weight.dtype),
            pltpu.VMEM((4, side, rows, cols), jnp.bfloat16),
            pltpu.VMEM((4, side, rows, cols), jnp.bfloat16),
            pltpu.VMEM((4, side, rows, cols), f32),
            pltpu.VMEM((4, side - 1, side, rows, cols), f32),
            pltpu.VMEM((4, side - 2, side, rows, cols), f32),
            pltpu.VMEM((4, side, rows, cols), f32),
            pltpu.VMEM((4, side - 1, rows, cols), f32),
            pltpu.VMEM((4, side - 2, rows, cols), f32),
            pltpu.SemaphoreType.DMA((48,)),
            pltpu.SemaphoreType.DMA((48,)),
            pltpu.SemaphoreType.DMA((4,)),
        ],
        compiler_params=pltpu.CompilerParams(
            collective_id=collective_id, has_side_effects=True, vmem_limit_bytes=63 * 1024 * 1024),
    )(t4, gate_weight, up_weight)


def _grid_ag_kernel(side, cols, h_ref, out_ref, gath, send_sem, recv_sem, local_sem):
    w = lax.axis_index("wa")
    x, z = w // side, lax.rem(w, side)

    def peer(axis, delta):
        if axis == 0:
            return lax.rem(x + delta + side, side) * side + z
        return x * side + lax.rem(z + delta + side, side)

    barrier = pltpu.get_barrier_semaphore()
    for axis in (0, 1):
        for delta in (1, -1):
            pl.semaphore_signal(barrier, inc=1, device_id={"wa": peer(axis, delta)}, device_id_type=MESH)
    pl.semaphore_wait(barrier, 4)

    halves = [pl.ds(0, cols), pl.ds(cols, cols)]
    rows = h_ref.shape[0]
    locals_ = []
    for f in range(2):
        c = halves[f]
        copy = pltpu.make_async_copy(h_ref.at[:, c], gath.at[x, z, :, c], local_sem.at[f])
        copy.start()
        locals_.append(copy)

    def piece(f, stage, at, part=None):
        c = halves[f]
        along_x = (f == 0) == (stage == 0)
        if stage == 0:
            span = slice(None) if part is None else pl.ds(part * (rows // 2), rows // 2)
            if along_x:
                return gath.at[at, z, span, c]
            return gath.at[x, at, span, c]
        span = slice(None) if part is None else pl.ds(part * (side // 2), side // 2)
        if along_x:
            return gath.at[at, span, :, c]
        return gath.at[span, at, :, c]

    sends = []
    for stage in range(2):
        first, geometry = {}, {}
        for f in range(2):
            along_x = (f == 0) == (stage == 0)
            axis = 0 if along_x else 1
            pos = x if along_x else z
            base = (f * 2 + stage) * 4
            geometry[f] = (axis, pos, base)
            if stage == 0:
                locals_[f].wait()
            own = piece(f, stage, pos)
            first[f] = []
            for j, delta in enumerate((1, -1)):
                copy = pltpu.make_async_remote_copy(
                    src_ref=own, dst_ref=own,
                    send_sem=send_sem.at[base + j], recv_sem=recv_sem.at[base + j],
                    device_id={"wa": peer(axis, delta)}, device_id_type=MESH)
                copy.start()
                first[f].append(copy)
                sends.append(copy)
        second = []
        for f in range(2):
            axis, pos, base = geometry[f]
            for j, delta in enumerate((1, -1)):
                first[f][j].wait_recv()
                origin = lax.rem(pos - delta + side, side)
                part = piece(f, stage, origin, j)
                copy = pltpu.make_async_remote_copy(
                    src_ref=part, dst_ref=part,
                    send_sem=send_sem.at[base + 2 + j], recv_sem=recv_sem.at[base + 2 + j],
                    device_id={"wa": peer(axis, delta)}, device_id_type=MESH)
                copy.start()
                second.append(copy)
                sends.append(copy)
        for copy in second:
            copy.wait_recv()
    for copy in sends:
        copy.wait_send()
    final = pltpu.make_async_copy(gath, out_ref, local_sem.at[2])
    final.start()
    final.wait()


def grid_all_gather(h, n, collective_id):
    side = 4
    rows, width = h.shape
    cols = width // 2
    out = pl.pallas_call(
        functools.partial(_grid_ag_kernel, side, cols),
        out_shape=jax.ShapeDtypeStruct((side, side, rows, width), h.dtype),
        in_specs=[pl.BlockSpec(memory_space=pltpu.VMEM)],
        out_specs=pl.BlockSpec(memory_space=pltpu.VMEM),
        scratch_shapes=[
            pltpu.VMEM((side, side, rows, width), h.dtype),
            pltpu.SemaphoreType.DMA((4 * side,)),
            pltpu.SemaphoreType.DMA((4 * side,)),
            pltpu.SemaphoreType.DMA((3,)),
        ],
        compiler_params=pltpu.CompilerParams(collective_id=collective_id, has_side_effects=True),
    )(h)
    return out.reshape(n * rows, width)


def _down_rs_kernel(n, rows, h_ref, w_hbm, out_ref, wbuf, sendbuf, slots, send_sem, recv_sem, w_sem):
    me = lax.axis_index("ha")
    load = pltpu.make_async_copy(w_hbm, wbuf, w_sem.at[0])
    load.start()
    _greet("ha", n, me)
    load.wait()
    copies = []
    order = sorted(range(1, n), key=lambda k: -min(k, n - k))
    for k in order:
        peer = lax.rem(me + k, n)
        block = h_ref[pl.ds(pl.multiple_of(peer * rows, rows), rows), :]
        sendbuf[k] = jnp.dot(block, wbuf[...], preferred_element_type=jnp.float32).astype(sendbuf.dtype)
        copy = pltpu.make_async_remote_copy(
            src_ref=sendbuf.at[k], dst_ref=slots.at[k],
            send_sem=send_sem.at[k], recv_sem=recv_sem.at[k],
            device_id={"ha": peer}, device_id_type=MESH)
        copy.start()
        copies.append(copy)
    block = h_ref[pl.ds(pl.multiple_of(me * rows, rows), rows), :]
    total = jnp.dot(block, wbuf[...], preferred_element_type=jnp.float32)
    for k, copy in zip(order, copies):
        copy.wait()
        total = total + slots[k].astype(jnp.float32)
    out_ref[...] = total


def down_reduce_scatter(hidden, down_weight, n, collective_id):
    rows = hidden.shape[0] // n
    depth, width = down_weight.shape
    return pl.pallas_call(
        functools.partial(_down_rs_kernel, n, rows),
        out_shape=jax.ShapeDtypeStruct((rows, width), jnp.float32),
        in_specs=[pl.BlockSpec(memory_space=pltpu.VMEM), pl.BlockSpec(memory_space=pl.ANY)],
        out_specs=pl.BlockSpec(memory_space=pltpu.VMEM),
        scratch_shapes=[
            pltpu.VMEM((depth, width), down_weight.dtype),
            pltpu.VMEM((n, rows, width), jnp.bfloat16),
            pltpu.VMEM((n, rows, width), jnp.bfloat16),
            pltpu.SemaphoreType.DMA((n,)),
            pltpu.SemaphoreType.DMA((n,)),
            pltpu.SemaphoreType.DMA((1,)),
        ],
        compiler_params=pltpu.CompilerParams(
            collective_id=collective_id, has_side_effects=True, vmem_limit_bytes=48 * 1024 * 1024),
    )(hidden, down_weight)


def _grid_sum_kernel(side, x_ref, out_ref, total1, slots1, slots2, send_sem, recv_sem):
    w = lax.axis_index("wa")
    x, z = w // side, lax.rem(w, side)

    def peer(axis, k):
        if axis == 0:
            return lax.rem(x + k, side) * side + z
        return x * side + lax.rem(z + k, side)

    barrier = pltpu.get_barrier_semaphore()
    for axis in (0, 1):
        for k in range(1, side):
            pl.semaphore_signal(barrier, inc=1, device_id={"wa": peer(axis, k)}, device_id_type=MESH)
    pl.semaphore_wait(barrier, 2 * (side - 1))
    for axis, source, slots, pos in ((0, x_ref, slots1, x), (1, total1, slots2, z)):
        copies = []
        for k in range(1, side):
            copy = pltpu.make_async_remote_copy(
                src_ref=source, dst_ref=slots.at[k],
                send_sem=send_sem.at[axis * side + k], recv_sem=recv_sem.at[axis * side + k],
                device_id={"wa": peer(axis, k)}, device_id_type=MESH)
            copy.start()
            copies.append(copy)
        for copy in copies:
            copy.wait()
        slots[0] = source[...]
        total = jnp.zeros(x_ref.shape, jnp.float32)
        for sender in range(side):
            total = total + slots[lax.rem(pos + side - sender, side)]
        if axis == 0:
            total1[...] = total
        else:
            out_ref[...] = total


def grid_sum(x, collective_id):
    side = 4
    return pl.pallas_call(
        functools.partial(_grid_sum_kernel, side),
        out_shape=jax.ShapeDtypeStruct(x.shape, jnp.float32),
        in_specs=[pl.BlockSpec(memory_space=pltpu.VMEM)],
        out_specs=pl.BlockSpec(memory_space=pltpu.VMEM),
        scratch_shapes=[
            pltpu.VMEM(x.shape, jnp.float32),
            pltpu.VMEM((side,) + x.shape, jnp.float32),
            pltpu.VMEM((side,) + x.shape, jnp.float32),
            pltpu.SemaphoreType.DMA((2 * side,)),
            pltpu.SemaphoreType.DMA((2 * side,)),
        ],
        compiler_params=pltpu.CompilerParams(collective_id=collective_id, has_side_effects=True),
    )(x)


def body(tokens, norm_gain, gate_weight, up_weight, down_weight):
    n_wa = lax.axis_size("wa")
    n_ha = lax.axis_size("ha")
    own_values = tokens.astype(jnp.float32)
    model_width = own_values.shape[1] * n_wa
    own_rows = own_values.shape[0]
    partial_squares = jnp.sum(own_values * own_values, axis=1)
    packed = jnp.pad(partial_squares.reshape(8, own_rows // 8), ((0, 0), (0, 128 - own_rows // 8)))
    squares = grid_sum(packed, 0)[:, : own_rows // 8].reshape(own_rows, 1)
    mean_square = squares / model_width
    normed = (own_values * lax.rsqrt(mean_square + 1e-05) * norm_gain[None, :]).astype(jnp.bfloat16)
    gathered = exchange(normed, "gather", "ha", n_ha, 1)
    hidden_width = gate_weight.shape[1]
    hidden = ring_reduce_scatter(gathered, gate_weight, up_weight, n_wa, 2)
    all_hidden = grid_all_gather(hidden, n_wa, 3)
    mixed_out = down_reduce_scatter(all_hidden, down_weight, n_ha, 4)
    return mixed_out.astype(jnp.bfloat16)


def solution(mesh):
    placed = (P("ha", "wa"), P("wa"), P("wa", "ha"), P("wa", "ha"), P("ha", "wa"))
    return jax.shard_map(body, mesh=mesh, in_specs=placed, out_specs=P("ha", "wa"), check_vma=False)
```

```python
import functools

import jax
import jax.numpy as jnp
from jax import lax
from jax.experimental import pallas as pl
from jax.experimental.pallas import tpu as pltpu
from jax.sharding import PartitionSpec as P

MESH = pl.DeviceIdType.MESH


def _greet(axis, n, me):
    barrier = pltpu.get_barrier_semaphore()
    for k in range(1, n):
        pl.semaphore_signal(barrier, inc=1, device_id={axis: lax.rem(me + k, n)}, device_id_type=MESH)
    pl.semaphore_wait(barrier, n - 1)


def _exchange_kernel(mode, axis, n, rows, x_ref, out_ref, slots, send_sem, recv_sem):
    me = lax.axis_index(axis)
    _greet(axis, n, me)
    copies = []
    for k in range(1, n):
        peer = lax.rem(me + k, n)
        if mode == "gather":
            source = x_ref
        elif mode == "scatter":
            source = x_ref.at[pl.ds(pl.multiple_of(peer * rows, rows), rows)]
        else:
            source = x_ref
        copy = pltpu.make_async_remote_copy(
            src_ref=source,
            dst_ref=slots.at[k],
            send_sem=send_sem.at[k],
            recv_sem=recv_sem.at[k],
            device_id={axis: peer},
            device_id_type=MESH,
        )
        copy.start()
        copies.append(copy)
    if mode == "gather":
        out_ref[pl.ds(pl.multiple_of(me * rows, rows), rows), :] = x_ref[...]
        for k, copy in enumerate(copies, 1):
            copy.wait()
            sender = lax.rem(me + n - k, n)
            out_ref[pl.ds(pl.multiple_of(sender * rows, rows), rows), :] = slots[k]
    elif mode == "scatter":
        total = x_ref[pl.ds(pl.multiple_of(me * rows, rows), rows), :].astype(jnp.float32)
        for k, copy in enumerate(copies, 1):
            copy.wait()
            total = total + slots[k].astype(jnp.float32)
        out_ref[...] = total
    else:
        for copy in copies:
            copy.wait()
        slots[0] = x_ref[...]
        total = jnp.zeros(out_ref.shape, jnp.float32)
        for sender in range(n):
            total = total + slots[lax.rem(me + n - sender, n)].astype(jnp.float32)
        out_ref[...] = total


def exchange(x, mode, axis, n, collective_id):
    if n == 1:
        return x.astype(jnp.float32) if mode != "gather" else x
    if mode == "gather":
        rows = x.shape[0]
        out_shape = jax.ShapeDtypeStruct((n * rows, x.shape[1]), x.dtype)
    elif mode == "scatter":
        rows = x.shape[0] // n
        out_shape = jax.ShapeDtypeStruct((rows, x.shape[1]), jnp.float32)
    else:
        rows = x.shape[0]
        out_shape = jax.ShapeDtypeStruct(x.shape, jnp.float32)
    return pl.pallas_call(
        functools.partial(_exchange_kernel, mode, axis, n, rows),
        out_shape=out_shape,
        in_specs=[pl.BlockSpec(memory_space=pltpu.VMEM)],
        out_specs=pl.BlockSpec(memory_space=pltpu.VMEM),
        scratch_shapes=[
            pltpu.VMEM((n, rows, x.shape[1]), x.dtype),
            pltpu.SemaphoreType.DMA((n,)),
            pltpu.SemaphoreType.DMA((n,)),
        ],
        compiler_params=pltpu.CompilerParams(collective_id=collective_id, has_side_effects=True),
    )(x)


def _ring_rs_kernel(side, cols, parts, t_ref, g_hbm, u_hbm, out_ref, summed, wbuf, first_buf, recv_b, tmp, recv1,
                    acc1, s1, recv2, acc2, send_sem, recv_sem, w_sem):
    w = lax.axis_index("wa")
    x, z = w // side, lax.rem(w, side)
    loads = []
    for f in range(4):
        source = g_hbm if f < 2 else u_hbm
        load = pltpu.make_async_copy(source.at[:, pl.ds((f % 2) * cols, cols)], wbuf.at[f], w_sem.at[f])
        load.start()
        loads.append(load)

    def peer(axis, delta):
        if axis == 0:
            return lax.rem(x + delta + side, side) * side + z
        return x * side + lax.rem(z + delta + side, side)

    barrier = pltpu.get_barrier_semaphore()
    for axis in (0, 1):
        for delta in (1, -1):
            pl.semaphore_signal(barrier, inc=1, device_id={"wa": peer(axis, delta)}, device_id_type=MESH)
    pl.semaphore_wait(barrier, 4)

    flows = []
    for f in range(4):
        first = 0 if f < 2 else 1
        delta = 1 if f % 2 == 0 else -1
        flows.append((first, delta, pl.ds(f * cols, cols)))

    def own1(f, chunk):
        if flows[f][0] == 0:
            rows = t_ref[chunk]
        else:
            rows = t_ref[:, chunk]
        block = rows.reshape(side * rows.shape[1], rows.shape[2])
        product = jnp.dot(block, wbuf[f], preferred_element_type=jnp.float32)
        return product.reshape(side, rows.shape[1], cols)

    def sem(stage, step, f, h):
        return ((stage * 3 + step) * 4 + f) * parts + h

    sub = t_ref.shape[2] // parts
    halves = [pl.ds(h * sub, sub) for h in range(parts)]
    sends = []
    pos1 = [x if flows[f][0] == 0 else z for f in range(4)]
    pos2 = [z if flows[f][0] == 0 else x for f in range(4)]
    last = [[None] * parts for _ in range(4)]

    def send(stage, step, f, h, source, target, axis):
        copy = pltpu.make_async_remote_copy(
            src_ref=source, dst_ref=target,
            send_sem=send_sem.at[sem(stage, step, f, h)], recv_sem=recv_sem.at[sem(stage, step, f, h)],
            device_id={"wa": peer(axis, flows[f][1])}, device_id_type=MESH)
        copy.start()
        sends.append(copy)
        last[f][h] = copy

    for step in range(side - 1):
        for f in range(4):
            first, delta, _ = flows[f]
            chunk = lax.rem(pos1[f] - delta * (step + 1) + 2 * side, side)
            if step == 0:
                loads[f].wait()
                first_buf[f] = own1(f, chunk).astype(first_buf.dtype)
                for h, r in enumerate(halves):
                    send(0, step, f, h, first_buf.at[f, :, r], recv_b.at[f, :, r], first)
            else:
                tmp[f] = own1(f, chunk)
                for h, r in enumerate(halves):
                    last[f][h].wait_recv()
                    if step == 1:
                        arrived = recv_b[f, :, r].astype(jnp.float32)
                    else:
                        arrived = recv1[f, step - 1, :, r]
                    acc1[f, step - 1, :, r] = arrived + tmp[f, :, r]
                    send(0, step, f, h, acc1.at[f, step - 1, :, r], recv1.at[f, step, :, r], first)
    for f in range(4):
        first, delta, _ = flows[f]
        tmp[f] = own1(f, pos1[f])
        chunk = lax.rem(pos2[f] - delta + 2 * side, side)
        for h, r in enumerate(halves):
            last[f][h].wait_recv()
            s1[f, :, r] = recv1[f, side - 2, :, r] + tmp[f, :, r]
            send(1, 0, f, h, s1.at[f, chunk, r], recv2.at[f, 0, r], 1 - first)
    for step in range(1, side - 1):
        for f in range(4):
            first, delta, _ = flows[f]
            chunk = lax.rem(pos2[f] - delta * (step + 1) + 2 * side, side)
            for h, r in enumerate(halves):
                last[f][h].wait_recv()
                acc2[f, step - 1, r] = recv2[f, step - 1, r] + s1[f, chunk, r]
                send(1, step, f, h, acc2.at[f, step - 1, r], recv2.at[f, step, r], 1 - first)
    for f in range(4):
        for h, r in enumerate(halves):
            last[f][h].wait_recv()
            summed[r, flows[f][2]] = recv2[f, side - 2, r] + s1[f, pos2[f], r]
    gate = summed[:, pl.ds(0, 2 * cols)]
    up = summed[:, pl.ds(2 * cols, 2 * cols)]
    out_ref[...] = (gate / (1.0 + jnp.exp(-gate)) * up).astype(out_ref.dtype)
    for copy in sends:
        copy.wait_send()


def ring_reduce_scatter(tokens, gate_weight, up_weight, n, collective_id):
    side = 4
    rows = tokens.shape[0] // n
    depth = tokens.shape[1]
    width = 2 * gate_weight.shape[1]
    cols = width // 4
    t4 = tokens.reshape(side, side, rows, depth)
    f32 = jnp.float32
    return pl.pallas_call(
        functools.partial(_ring_rs_kernel, side, cols, 2),
        out_shape=jax.ShapeDtypeStruct((rows, width // 2), jnp.bfloat16),
        in_specs=[pl.BlockSpec(memory_space=pltpu.VMEM), pl.BlockSpec(memory_space=pl.ANY),
                  pl.BlockSpec(memory_space=pl.ANY)],
        out_specs=pl.BlockSpec(memory_space=pltpu.VMEM),
        scratch_shapes=[
            pltpu.VMEM((rows, width), f32),
            pltpu.VMEM((4, depth, cols), gate_weight.dtype),
            pltpu.VMEM((4, side, rows, cols), jnp.bfloat16),
            pltpu.VMEM((4, side, rows, cols), jnp.bfloat16),
            pltpu.VMEM((4, side, rows, cols), f32),
            pltpu.VMEM((4, side - 1, side, rows, cols), f32),
            pltpu.VMEM((4, side - 2, side, rows, cols), f32),
            pltpu.VMEM((4, side, rows, cols), f32),
            pltpu.VMEM((4, side - 1, rows, cols), f32),
            pltpu.VMEM((4, side - 2, rows, cols), f32),
            pltpu.SemaphoreType.DMA((48,)),
            pltpu.SemaphoreType.DMA((48,)),
            pltpu.SemaphoreType.DMA((4,)),
        ],
        compiler_params=pltpu.CompilerParams(
            collective_id=collective_id, has_side_effects=True, vmem_limit_bytes=63 * 1024 * 1024),
    )(t4, gate_weight, up_weight)


def _grid_ag_kernel(side, cols, h_ref, gath, send_sem, recv_sem, local_sem):
    w = lax.axis_index("wa")
    x, z = w // side, lax.rem(w, side)

    def peer(axis, delta):
        if axis == 0:
            return lax.rem(x + delta + side, side) * side + z
        return x * side + lax.rem(z + delta + side, side)

    barrier = pltpu.get_barrier_semaphore()
    for axis in (0, 1):
        for delta in (1, -1):
            pl.semaphore_signal(barrier, inc=1, device_id={"wa": peer(axis, delta)}, device_id_type=MESH)
    pl.semaphore_wait(barrier, 4)

    halves = [pl.ds(0, cols), pl.ds(cols, cols)]
    rows = h_ref.shape[0]
    locals_ = []
    for f in range(2):
        c = halves[f]
        copy = pltpu.make_async_copy(h_ref.at[:, c], gath.at[x, z, :, c], local_sem.at[f])
        copy.start()
        locals_.append(copy)

    def piece(f, stage, at, part=None):
        c = halves[f]
        along_x = (f == 0) == (stage == 0)
        if stage == 0:
            span = slice(None) if part is None else pl.ds(part * (rows // 2), rows // 2)
            if along_x:
                return gath.at[at, z, span, c]
            return gath.at[x, at, span, c]
        span = slice(None) if part is None else pl.ds(part * (side // 2), side // 2)
        if along_x:
            return gath.at[at, span, :, c]
        return gath.at[span, at, :, c]

    sends = []
    for stage in range(2):
        first, geometry = {}, {}
        for f in range(2):
            along_x = (f == 0) == (stage == 0)
            axis = 0 if along_x else 1
            pos = x if along_x else z
            base = (f * 2 + stage) * 4
            geometry[f] = (axis, pos, base)
            if stage == 0:
                locals_[f].wait()
            own = piece(f, stage, pos)
            first[f] = []
            for j, delta in enumerate((1, -1)):
                copy = pltpu.make_async_remote_copy(
                    src_ref=own, dst_ref=own,
                    send_sem=send_sem.at[base + j], recv_sem=recv_sem.at[base + j],
                    device_id={"wa": peer(axis, delta)}, device_id_type=MESH)
                copy.start()
                first[f].append(copy)
                sends.append(copy)
        second = []
        for f in range(2):
            axis, pos, base = geometry[f]
            for j, delta in enumerate((1, -1)):
                first[f][j].wait_recv()
                origin = lax.rem(pos - delta + side, side)
                part = piece(f, stage, origin, j)
                copy = pltpu.make_async_remote_copy(
                    src_ref=part, dst_ref=part,
                    send_sem=send_sem.at[base + 2 + j], recv_sem=recv_sem.at[base + 2 + j],
                    device_id={"wa": peer(axis, delta)}, device_id_type=MESH)
                copy.start()
                second.append(copy)
                sends.append(copy)
        for copy in second:
            copy.wait_recv()
    for copy in sends:
        copy.wait_send()


def grid_all_gather(h, n, collective_id):
    side = 4
    rows, width = h.shape
    cols = width // 2
    out = pl.pallas_call(
        functools.partial(_grid_ag_kernel, side, cols),
        out_shape=jax.ShapeDtypeStruct((side, side, rows, width), h.dtype),
        in_specs=[pl.BlockSpec(memory_space=pltpu.VMEM)],
        out_specs=pl.BlockSpec(memory_space=pltpu.VMEM),
        scratch_shapes=[
            pltpu.SemaphoreType.DMA((4 * side,)),
            pltpu.SemaphoreType.DMA((4 * side,)),
            pltpu.SemaphoreType.DMA((3,)),
        ],
        compiler_params=pltpu.CompilerParams(collective_id=collective_id, has_side_effects=True),
    )(h)
    return out.reshape(n * rows, width)


def _down_rs_kernel(n, rows, h_ref, w_hbm, out_ref, wbuf, sendbuf, slots, send_sem, recv_sem, w_sem):
    me = lax.axis_index("ha")
    load = pltpu.make_async_copy(w_hbm, wbuf, w_sem.at[0])
    load.start()
    _greet("ha", n, me)
    load.wait()
    copies = []
    order = sorted(range(1, n), key=lambda k: -min(k, n - k))
    for k in order:
        peer = lax.rem(me + k, n)
        block = h_ref[pl.ds(pl.multiple_of(peer * rows, rows), rows), :]
        sendbuf[k] = jnp.dot(block, wbuf[...], preferred_element_type=jnp.float32).astype(sendbuf.dtype)
        copy = pltpu.make_async_remote_copy(
            src_ref=sendbuf.at[k], dst_ref=slots.at[k],
            send_sem=send_sem.at[k], recv_sem=recv_sem.at[k],
            device_id={"ha": peer}, device_id_type=MESH)
        copy.start()
        copies.append(copy)
    block = h_ref[pl.ds(pl.multiple_of(me * rows, rows), rows), :]
    total = jnp.dot(block, wbuf[...], preferred_element_type=jnp.float32)
    for k, copy in zip(order, copies):
        copy.wait()
        total = total + slots[k].astype(jnp.float32)
    out_ref[...] = total


def down_reduce_scatter(hidden, down_weight, n, collective_id):
    rows = hidden.shape[0] // n
    depth, width = down_weight.shape
    return pl.pallas_call(
        functools.partial(_down_rs_kernel, n, rows),
        out_shape=jax.ShapeDtypeStruct((rows, width), jnp.float32),
        in_specs=[pl.BlockSpec(memory_space=pltpu.VMEM), pl.BlockSpec(memory_space=pl.ANY)],
        out_specs=pl.BlockSpec(memory_space=pltpu.VMEM),
        scratch_shapes=[
            pltpu.VMEM((depth, width), down_weight.dtype),
            pltpu.VMEM((n, rows, width), jnp.bfloat16),
            pltpu.VMEM((n, rows, width), jnp.bfloat16),
            pltpu.SemaphoreType.DMA((n,)),
            pltpu.SemaphoreType.DMA((n,)),
            pltpu.SemaphoreType.DMA((1,)),
        ],
        compiler_params=pltpu.CompilerParams(
            collective_id=collective_id, has_side_effects=True, vmem_limit_bytes=48 * 1024 * 1024),
    )(hidden, down_weight)


def body(tokens, norm_gain, gate_weight, up_weight, down_weight):
    n_wa = lax.axis_size("wa")
    n_ha = lax.axis_size("ha")
    own_values = tokens.astype(jnp.float32)
    model_width = own_values.shape[1] * n_wa
    own_rows = own_values.shape[0]
    partial_squares = jnp.sum(own_values * own_values, axis=1)
    packed = jnp.pad(partial_squares.reshape(8, own_rows // 8), ((0, 0), (0, 128 - own_rows // 8)))
    squares = exchange(packed, "sum", "wa", n_wa, 0)[:, : own_rows // 8].reshape(own_rows, 1)
    mean_square = squares / model_width
    normed = (own_values * lax.rsqrt(mean_square + 1e-05) * norm_gain[None, :]).astype(jnp.bfloat16)
    gathered = exchange(normed, "gather", "ha", n_ha, 1)
    hidden_width = gate_weight.shape[1]
    hidden = ring_reduce_scatter(gathered, gate_weight, up_weight, n_wa, 2)
    all_hidden = grid_all_gather(hidden, n_wa, 3)
    mixed_out = down_reduce_scatter(all_hidden, down_weight, n_ha, 4)
    return mixed_out.astype(jnp.bfloat16)


def solution(mesh):
    placed = (P("ha", "wa"), P("wa"), P("wa", "ha"), P("wa", "ha"), P("ha", "wa"))
    return jax.shard_map(body, mesh=mesh, in_specs=placed, out_specs=P("ha", "wa"), check_vma=False)
```

```python
import functools

import jax
import jax.numpy as jnp
from jax import lax
from jax.experimental import pallas as pl
from jax.experimental.pallas import tpu as pltpu
from jax.sharding import PartitionSpec as P

MESH = pl.DeviceIdType.MESH


def _greet(axis, n, me):
    barrier = pltpu.get_barrier_semaphore()
    for k in range(1, n):
        pl.semaphore_signal(barrier, inc=1, device_id={axis: lax.rem(me + k, n)}, device_id_type=MESH)
    pl.semaphore_wait(barrier, n - 1)


def _exchange_kernel(mode, axis, n, rows, x_ref, out_ref, slots, send_sem, recv_sem):
    me = lax.axis_index(axis)
    _greet(axis, n, me)
    copies = []
    for k in range(1, n):
        peer = lax.rem(me + k, n)
        if mode == "gather":
            source = x_ref
        elif mode == "scatter":
            source = x_ref.at[pl.ds(pl.multiple_of(peer * rows, rows), rows)]
        else:
            source = x_ref
        if mode == "gather":
            target = out_ref.at[pl.ds(pl.multiple_of(me * rows, rows), rows)]
        else:
            target = slots.at[k]
        copy = pltpu.make_async_remote_copy(
            src_ref=source,
            dst_ref=target,
            send_sem=send_sem.at[k],
            recv_sem=recv_sem.at[k],
            device_id={axis: peer},
            device_id_type=MESH,
        )
        copy.start()
        copies.append(copy)
    if mode == "gather":
        out_ref[pl.ds(pl.multiple_of(me * rows, rows), rows), :] = x_ref[...]
        for copy in copies:
            copy.wait()
    elif mode == "scatter":
        total = x_ref[pl.ds(pl.multiple_of(me * rows, rows), rows), :].astype(jnp.float32)
        for k, copy in enumerate(copies, 1):
            copy.wait()
            total = total + slots[k].astype(jnp.float32)
        out_ref[...] = total
    else:
        for copy in copies:
            copy.wait()
        slots[0] = x_ref[...]
        total = jnp.zeros(out_ref.shape, jnp.float32)
        for sender in range(n):
            total = total + slots[lax.rem(me + n - sender, n)].astype(jnp.float32)
        out_ref[...] = total


def exchange(x, mode, axis, n, collective_id):
    if n == 1:
        return x.astype(jnp.float32) if mode != "gather" else x
    if mode == "gather":
        rows = x.shape[0]
        out_shape = jax.ShapeDtypeStruct((n * rows, x.shape[1]), x.dtype)
    elif mode == "scatter":
        rows = x.shape[0] // n
        out_shape = jax.ShapeDtypeStruct((rows, x.shape[1]), jnp.float32)
    else:
        rows = x.shape[0]
        out_shape = jax.ShapeDtypeStruct(x.shape, jnp.float32)
    return pl.pallas_call(
        functools.partial(_exchange_kernel, mode, axis, n, rows),
        out_shape=out_shape,
        in_specs=[pl.BlockSpec(memory_space=pltpu.VMEM)],
        out_specs=pl.BlockSpec(memory_space=pltpu.VMEM),
        scratch_shapes=[
            pltpu.VMEM((n, rows, x.shape[1]), x.dtype),
            pltpu.SemaphoreType.DMA((n,)),
            pltpu.SemaphoreType.DMA((n,)),
        ],
        compiler_params=pltpu.CompilerParams(collective_id=collective_id, has_side_effects=True),
    )(x)


def _ring_rs_kernel(side, cols, parts, t_ref, g_hbm, u_hbm, out_ref, summed, wbuf, first_buf, recv_b, tmp, recv1,
                    acc1, s1, recv2, acc2, send_sem, recv_sem, w_sem):
    w = lax.axis_index("wa")
    x, z = w // side, lax.rem(w, side)
    loads = []
    for f in range(4):
        source = g_hbm if f < 2 else u_hbm
        load = pltpu.make_async_copy(source.at[:, pl.ds((f % 2) * cols, cols)], wbuf.at[f], w_sem.at[f])
        load.start()
        loads.append(load)

    def peer(axis, delta):
        if axis == 0:
            return lax.rem(x + delta + side, side) * side + z
        return x * side + lax.rem(z + delta + side, side)

    barrier = pltpu.get_barrier_semaphore()
    for axis in (0, 1):
        for delta in (1, -1):
            pl.semaphore_signal(barrier, inc=1, device_id={"wa": peer(axis, delta)}, device_id_type=MESH)
    pl.semaphore_wait(barrier, 4)

    flows = []
    for f in range(4):
        first = 0 if f < 2 else 1
        delta = 1 if f % 2 == 0 else -1
        flows.append((first, delta, pl.ds(f * cols, cols)))

    def own1(f, chunk):
        if flows[f][0] == 0:
            rows = t_ref[chunk]
        else:
            rows = t_ref[:, chunk]
        block = rows.reshape(side * rows.shape[1], rows.shape[2])
        product = jnp.dot(block, wbuf[f], preferred_element_type=jnp.float32)
        return product.reshape(side, rows.shape[1], cols)

    def sem(stage, step, f, h):
        return ((stage * 3 + step) * 4 + f) * parts + h

    sub = t_ref.shape[2] // parts
    halves = [pl.ds(h * sub, sub) for h in range(parts)]
    sends = []
    pos1 = [x if flows[f][0] == 0 else z for f in range(4)]
    pos2 = [z if flows[f][0] == 0 else x for f in range(4)]
    last = [[None] * parts for _ in range(4)]

    def send(stage, step, f, h, source, target, axis):
        copy = pltpu.make_async_remote_copy(
            src_ref=source, dst_ref=target,
            send_sem=send_sem.at[sem(stage, step, f, h)], recv_sem=recv_sem.at[sem(stage, step, f, h)],
            device_id={"wa": peer(axis, flows[f][1])}, device_id_type=MESH)
        copy.start()
        sends.append(copy)
        last[f][h] = copy

    for step in range(side - 1):
        for f in range(4):
            first, delta, _ = flows[f]
            chunk = lax.rem(pos1[f] - delta * (step + 1) + 2 * side, side)
            if step == 0:
                loads[f].wait()
                first_buf[f] = own1(f, chunk).astype(first_buf.dtype)
                for h, r in enumerate(halves):
                    send(0, step, f, h, first_buf.at[f, :, r], recv_b.at[f, :, r], first)
            else:
                tmp[f] = own1(f, chunk)
                for h, r in enumerate(halves):
                    last[f][h].wait_recv()
                    if step == 1:
                        arrived = recv_b[f, :, r].astype(jnp.float32)
                    else:
                        arrived = recv1[f, step - 1, :, r]
                    acc1[f, step - 1, :, r] = arrived + tmp[f, :, r]
                    send(0, step, f, h, acc1.at[f, step - 1, :, r], recv1.at[f, step, :, r], first)
    for f in range(4):
        first, delta, _ = flows[f]
        tmp[f] = own1(f, pos1[f])
        chunk = lax.rem(pos2[f] - delta + 2 * side, side)
        for h, r in enumerate(halves):
            last[f][h].wait_recv()
            s1[f, :, r] = recv1[f, side - 2, :, r] + tmp[f, :, r]
            send(1, 0, f, h, s1.at[f, chunk, r], recv2.at[f, 0, r], 1 - first)
    for step in range(1, side - 1):
        for f in range(4):
            first, delta, _ = flows[f]
            chunk = lax.rem(pos2[f] - delta * (step + 1) + 2 * side, side)
            for h, r in enumerate(halves):
                last[f][h].wait_recv()
                acc2[f, step - 1, r] = recv2[f, step - 1, r] + s1[f, chunk, r]
                send(1, step, f, h, acc2.at[f, step - 1, r], recv2.at[f, step, r], 1 - first)
    for f in range(4):
        for h, r in enumerate(halves):
            last[f][h].wait_recv()
            summed[r, flows[f][2]] = recv2[f, side - 2, r] + s1[f, pos2[f], r]
    gate = summed[:, pl.ds(0, 2 * cols)]
    up = summed[:, pl.ds(2 * cols, 2 * cols)]
    out_ref[...] = (gate / (1.0 + jnp.exp(-gate)) * up).astype(out_ref.dtype)
    for copy in sends:
        copy.wait_send()


def ring_reduce_scatter(tokens, gate_weight, up_weight, n, collective_id):
    side = 4
    rows = tokens.shape[0] // n
    depth = tokens.shape[1]
    width = 2 * gate_weight.shape[1]
    cols = width // 4
    t4 = tokens.reshape(side, side, rows, depth)
    f32 = jnp.float32
    return pl.pallas_call(
        functools.partial(_ring_rs_kernel, side, cols, 2),
        out_shape=jax.ShapeDtypeStruct((rows, width // 2), jnp.bfloat16),
        in_specs=[pl.BlockSpec(memory_space=pltpu.VMEM), pl.BlockSpec(memory_space=pl.ANY),
                  pl.BlockSpec(memory_space=pl.ANY)],
        out_specs=pl.BlockSpec(memory_space=pltpu.VMEM),
        scratch_shapes=[
            pltpu.VMEM((rows, width), f32),
            pltpu.VMEM((4, depth, cols), gate_weight.dtype),
            pltpu.VMEM((4, side, rows, cols), jnp.bfloat16),
            pltpu.VMEM((4, side, rows, cols), jnp.bfloat16),
            pltpu.VMEM((4, side, rows, cols), f32),
            pltpu.VMEM((4, side - 1, side, rows, cols), f32),
            pltpu.VMEM((4, side - 2, side, rows, cols), f32),
            pltpu.VMEM((4, side, rows, cols), f32),
            pltpu.VMEM((4, side - 1, rows, cols), f32),
            pltpu.VMEM((4, side - 2, rows, cols), f32),
            pltpu.SemaphoreType.DMA((48,)),
            pltpu.SemaphoreType.DMA((48,)),
            pltpu.SemaphoreType.DMA((4,)),
        ],
        compiler_params=pltpu.CompilerParams(
            collective_id=collective_id, has_side_effects=True, vmem_limit_bytes=63 * 1024 * 1024),
    )(t4, gate_weight, up_weight)


def _grid_ag_kernel(side, cols, h_ref, gath, send_sem, recv_sem, local_sem):
    w = lax.axis_index("wa")
    x, z = w // side, lax.rem(w, side)

    def peer(axis, delta):
        if axis == 0:
            return lax.rem(x + delta + side, side) * side + z
        return x * side + lax.rem(z + delta + side, side)

    barrier = pltpu.get_barrier_semaphore()
    for axis in (0, 1):
        for delta in (1, -1):
            pl.semaphore_signal(barrier, inc=1, device_id={"wa": peer(axis, delta)}, device_id_type=MESH)
    pl.semaphore_wait(barrier, 4)

    halves = [pl.ds(0, cols), pl.ds(cols, cols)]
    rows = h_ref.shape[0]
    locals_ = []
    for f in range(2):
        c = halves[f]
        copy = pltpu.make_async_copy(h_ref.at[:, c], gath.at[x, z, :, c], local_sem.at[f])
        copy.start()
        locals_.append(copy)

    def piece(f, stage, at, part=None):
        c = halves[f]
        along_x = (f == 0) == (stage == 0)
        if stage == 0:
            span = slice(None) if part is None else pl.ds(part * (rows // 2), rows // 2)
            if along_x:
                return gath.at[at, z, span, c]
            return gath.at[x, at, span, c]
        span = slice(None) if part is None else pl.ds(part * (side // 2), side // 2)
        if along_x:
            return gath.at[at, span, :, c]
        return gath.at[span, at, :, c]

    sends = []
    for stage in range(2):
        first, geometry = {}, {}
        for f in range(2):
            along_x = (f == 0) == (stage == 0)
            axis = 0 if along_x else 1
            pos = x if along_x else z
            base = (f * 2 + stage) * 4
            geometry[f] = (axis, pos, base)
            if stage == 0:
                locals_[f].wait()
            own = piece(f, stage, pos)
            first[f] = []
            for j, delta in enumerate((1, -1)):
                copy = pltpu.make_async_remote_copy(
                    src_ref=own, dst_ref=own,
                    send_sem=send_sem.at[base + j], recv_sem=recv_sem.at[base + j],
                    device_id={"wa": peer(axis, delta)}, device_id_type=MESH)
                copy.start()
                first[f].append(copy)
                sends.append(copy)
        second = []
        for f in range(2):
            axis, pos, base = geometry[f]
            for j, delta in enumerate((1, -1)):
                first[f][j].wait_recv()
                origin = lax.rem(pos - delta + side, side)
                part = piece(f, stage, origin, j)
                copy = pltpu.make_async_remote_copy(
                    src_ref=part, dst_ref=part,
                    send_sem=send_sem.at[base + 2 + j], recv_sem=recv_sem.at[base + 2 + j],
                    device_id={"wa": peer(axis, delta)}, device_id_type=MESH)
                copy.start()
                second.append(copy)
                sends.append(copy)
        for copy in second:
            copy.wait_recv()
    for copy in sends:
        copy.wait_send()


def grid_all_gather(h, n, collective_id):
    side = 4
    rows, width = h.shape
    cols = width // 2
    out = pl.pallas_call(
        functools.partial(_grid_ag_kernel, side, cols),
        out_shape=jax.ShapeDtypeStruct((side, side, rows, width), h.dtype),
        in_specs=[pl.BlockSpec(memory_space=pltpu.VMEM)],
        out_specs=pl.BlockSpec(memory_space=pltpu.VMEM),
        scratch_shapes=[
            pltpu.SemaphoreType.DMA((4 * side,)),
            pltpu.SemaphoreType.DMA((4 * side,)),
            pltpu.SemaphoreType.DMA((3,)),
        ],
        compiler_params=pltpu.CompilerParams(collective_id=collective_id, has_side_effects=True),
    )(h)
    return out.reshape(n * rows, width)


def _down_rs_kernel(n, rows, h_ref, w_hbm, out_ref, wbuf, sendbuf, slots, send_sem, recv_sem, w_sem):
    me = lax.axis_index("ha")
    load = pltpu.make_async_copy(w_hbm, wbuf, w_sem.at[0])
    load.start()
    _greet("ha", n, me)
    load.wait()
    copies = []
    order = sorted(range(1, n), key=lambda k: -min(k, n - k))
    for k in order:
        peer = lax.rem(me + k, n)
        block = h_ref[pl.ds(pl.multiple_of(peer * rows, rows), rows), :]
        sendbuf[k] = jnp.dot(block, wbuf[...], preferred_element_type=jnp.float32).astype(sendbuf.dtype)
        copy = pltpu.make_async_remote_copy(
            src_ref=sendbuf.at[k], dst_ref=slots.at[k],
            send_sem=send_sem.at[k], recv_sem=recv_sem.at[k],
            device_id={"ha": peer}, device_id_type=MESH)
        copy.start()
        copies.append(copy)
    block = h_ref[pl.ds(pl.multiple_of(me * rows, rows), rows), :]
    total = jnp.dot(block, wbuf[...], preferred_element_type=jnp.float32)
    for k, copy in zip(order, copies):
        copy.wait()
        total = total + slots[k].astype(jnp.float32)
    out_ref[...] = total


def down_reduce_scatter(hidden, down_weight, n, collective_id):
    rows = hidden.shape[0] // n
    depth, width = down_weight.shape
    return pl.pallas_call(
        functools.partial(_down_rs_kernel, n, rows),
        out_shape=jax.ShapeDtypeStruct((rows, width), jnp.float32),
        in_specs=[pl.BlockSpec(memory_space=pltpu.VMEM), pl.BlockSpec(memory_space=pl.ANY)],
        out_specs=pl.BlockSpec(memory_space=pltpu.VMEM),
        scratch_shapes=[
            pltpu.VMEM((depth, width), down_weight.dtype),
            pltpu.VMEM((n, rows, width), jnp.bfloat16),
            pltpu.VMEM((n, rows, width), jnp.bfloat16),
            pltpu.SemaphoreType.DMA((n,)),
            pltpu.SemaphoreType.DMA((n,)),
            pltpu.SemaphoreType.DMA((1,)),
        ],
        compiler_params=pltpu.CompilerParams(
            collective_id=collective_id, has_side_effects=True, vmem_limit_bytes=48 * 1024 * 1024),
    )(hidden, down_weight)


def body(tokens, norm_gain, gate_weight, up_weight, down_weight):
    n_wa = lax.axis_size("wa")
    n_ha = lax.axis_size("ha")
    own_values = tokens.astype(jnp.float32)
    model_width = own_values.shape[1] * n_wa
    own_rows = own_values.shape[0]
    partial_squares = jnp.sum(own_values * own_values, axis=1)
    packed = jnp.pad(partial_squares.reshape(8, own_rows // 8), ((0, 0), (0, 128 - own_rows // 8)))
    squares = exchange(packed, "sum", "wa", n_wa, 0)[:, : own_rows // 8].reshape(own_rows, 1)
    mean_square = squares / model_width
    normed = (own_values * lax.rsqrt(mean_square + 1e-05) * norm_gain[None, :]).astype(jnp.bfloat16)
    gathered = exchange(normed, "gather", "ha", n_ha, 1)
    hidden_width = gate_weight.shape[1]
    hidden = ring_reduce_scatter(gathered, gate_weight, up_weight, n_wa, 2)
    all_hidden = grid_all_gather(hidden, n_wa, 3)
    mixed_out = down_reduce_scatter(all_hidden, down_weight, n_ha, 4)
    return mixed_out.astype(jnp.bfloat16)


def solution(mesh):
    placed = (P("ha", "wa"), P("wa"), P("wa", "ha"), P("wa", "ha"), P("ha", "wa"))
    return jax.shard_map(body, mesh=mesh, in_specs=placed, out_specs=P("ha", "wa"), check_vma=False)
```
